128 devices in a mesh: gx: 16 (over y_hi, x, core), gy: 8 (over y_lo, z).
Axes of the slice: x: 4, y: 4 (y_hi: 2, y_lo: 2; y = y_hi * 2 + y_lo), z: 4, core: 2. Of those that a mesh axis runs over, the one named last changes fastest.
Arguments:
- held_head: float32 [16384, 8, 128], P(('gx', 'gy')), may hold values from -6 to -0.5
- held_head_old: float32 [16384, 8, 128], P(('gx', 'gy')), may hold values from -6 to -0.5
- material_ids: int32 [128, 128, 1024], P(None, 'gx', 'gy'), may hold values from 0 to 15
- block_map: int32 [128, 128], replicated, may hold values from 0 to 127, as said below
- conductivity: float32 [3, 16], replicated, may hold values from 0.1 to 10
- vg_alpha: float32 [16], replicated, may hold values from 0.5 to 4
- vg_n: float32 [16], replicated, may hold values from 1.5 to 3
- capacity: float32 [16], replicated, may hold values from 0.1 to 0.45
Outputs:
- update: float32 [128, 128, 1024], P(None, 'gx', 'gy')
The draws below stay inside these ranges and needn't reach their ends.
Inputs may be any that keep to these rules, and one draw needn't show every extreme that they name: Every row and every column of block_map holds each brick number once.
All inputs are finite; a program needn't handle non-finite values.
Results may differ from the reference program's by a relative error of at most 0.0001.
Values sent between devices are 32-bit elements; how exact they have to be, the bound alone decides.
No kernel may reach another device: no remote copies, remote signals or barrier semaphores. Data moves between devices by JAX's collectives and lax.ppermute only.
A program may use at most 128 MiB of HBM per device.

```python
import math
import jax
import jax.numpy as jnp
from jax import lax

CX = 8
CY = 128
NZ = 128
MATERIALS = 16
ITERS = 4
BRICKS = 128
NX = 128
NY = 1024
SLAB = 1
N_GX = 16
N_GY = 8


def draw_block_map(key, part):
    first_key = jax.random.fold_in(key, 11)
    second_key = jax.random.fold_in(key, 12)
    third_key = jax.random.fold_in(key, 13)
    row_shift = jax.random.permutation(first_key, BRICKS)
    column_shift = jax.random.permutation(second_key, BRICKS)
    relabel = jax.random.permutation(third_key, BRICKS)
    square = (row_shift[:, None] + column_shift[None, :]) % BRICKS
    return relabel[square].astype(jnp.int32)


def place_ends(drawn, rng, smallest, top_value):
    spot = [jax.random.randint(jax.random.fold_in(rng, axis), (), 0, length) for axis, length in enumerate(drawn.shape)]
    longest = drawn.shape.index(max(drawn.shape))
    neighbour = spot[:longest] + [(spot[longest] + 1) % drawn.shape[longest]] + spot[longest + 1:]
    return drawn.at[tuple(spot)].set(smallest).at[tuple(neighbour)].set(top_value)


def shard_levels(stream_key, dims, split, low, top_value):
    def one(dim, parts):
        steps = jax.random.uniform(jax.random.fold_in(jax.random.fold_in(stream_key, 6), dim), (parts,), jnp.float32, low / len(split), top_value / len(split))
        return jnp.repeat(jnp.exp(steps), dims[dim] // parts).reshape((-1,) + (1,) * (len(dims) - dim - 1))

    factor_of = one(*split[0])
    for cut in split[1:]:
        factor_of = factor_of * one(*cut)
    return factor_of


def setup_inputs(seed: int = 0) -> dict:
    keys = jax.random.split(jax.random.key(seed), 9)
    return {
        "held_head": jnp.clip(-6.0 + 5.5 * jax.random.uniform(keys[0], (BRICKS * NZ, CX, CY), jnp.float32) ** shard_levels(keys[0], (BRICKS * NZ, CX, CY), ((0, 128),), -0.2, 0.2), -6.0, -0.5),
        "held_head_old": jnp.clip(-6.0 + 5.5 * jax.random.uniform(keys[1], (BRICKS * NZ, CX, CY), jnp.float32) ** shard_levels(keys[1], (BRICKS * NZ, CX, CY), ((0, 128),), -0.2, 0.2), -6.0, -0.5),
        "material_ids": place_ends(jax.random.randint(keys[2], (NZ, NX, NY), 0, MATERIALS), jax.random.fold_in(keys[2], 1), 0, MATERIALS - 1).astype(jnp.int32),
        "block_map": draw_block_map(jax.random.fold_in(keys[8], 71), 0),
        "conductivity": jnp.clip(jnp.exp(jax.random.uniform(keys[4], (3, MATERIALS), jnp.float32, math.log(0.1), math.log(10.0))), 0.1, 10.0),
        "vg_alpha": jnp.clip(jnp.exp(jax.random.uniform(keys[5], (MATERIALS,), jnp.float32, math.log(0.5), math.log(4.0))), 0.5, 4.0),
        "vg_n": jnp.clip(jax.random.uniform(keys[6], (MATERIALS,), jnp.float32, 1.5, 3.0), 1.5, 3.0),
        "capacity": jnp.clip(jax.random.uniform(keys[7], (MATERIALS,), jnp.float32, 0.1, 0.45), 0.1, 0.45),
    }


STORE = 4.0

def retention(level, alpha_cell, expo_cell):
    scaled = alpha_cell * -level
    power = jnp.exp(expo_cell * jnp.log(scaled))
    exponent = 1.0 - 1.0 / expo_cell
    inverse = 1.0 / (1.0 + power)
    saturation = jnp.exp(exponent * jnp.log(inverse))
    inner_term = -jnp.expm1(exponent * jnp.log1p(-inverse))
    relperm = jnp.sqrt(saturation) * inner_term * inner_term
    return (saturation, relperm)

def properties(material_ids, conductivity, vg_alpha, vg_n, capacity):
    blank = jnp.zeros(material_ids.shape, conductivity.dtype)
    fields = [blank, blank, blank, blank, blank, blank]
    for m in range(MATERIALS):
        match_cell = material_ids == m
        values = (conductivity[0, m], conductivity[1, m], conductivity[2, m], vg_alpha[m], vg_n[m], capacity[m])
        fields = [jnp.where(match_cell, value, field) for value, field in zip(values, fields)]
    return fields

def pair_slices(padded, axis):
    lower_index = [slice(1, -1), slice(1, -1), slice(1, -1)]
    higher_index = [slice(1, -1), slice(1, -1), slice(1, -1)]
    lower_index[axis] = slice(0, -1)
    higher_index[axis] = slice(1, None)
    return (padded[tuple(lower_index)], padded[tuple(higher_index)])

def face_terms(pad_head, pad_rel, pad_cond, axis, rise):
    head_low, head_high = pair_slices(pad_head, axis)
    rel_low, rel_high = pair_slices(pad_rel, axis)
    cond_low, cond_high = pair_slices(pad_cond, axis)
    trans = 2.0 * cond_low * cond_high / (cond_low + cond_high)
    potential = head_high - head_low + rise
    along = trans * (0.5 * (rel_low + rel_high))
    slope = trans * potential * 0.5
    return (along, slope, along * potential)

def net_inflow(flux, axis):
    extent = flux.shape[axis]
    return lax.slice_in_dim(flux, 1, extent, axis=axis) - lax.slice_in_dim(flux, 0, extent - 1, axis=axis)

def least_squares(hess, beta):
    matrix_rows = [hess[i] for i in range(ITERS + 1)]
    target = [beta] + [jnp.zeros_like(beta) for i in range(ITERS)]
    for j in range(ITERS):
        first = matrix_rows[j][j]
        second = matrix_rows[j + 1][j]
        radius = jnp.sqrt(first * first + second * second)
        cosine = first / radius
        sine_value = second / radius
        row_top, row_next = (matrix_rows[j], matrix_rows[j + 1])
        matrix_rows[j] = cosine * row_top + sine_value * row_next
        matrix_rows[j + 1] = cosine * row_next - sine_value * row_top
        goal_top, goal_next = (target[j], target[j + 1])
        target[j] = cosine * goal_top + sine_value * goal_next
        target[j + 1] = cosine * goal_next - sine_value * goal_top
    coeffs = [None] * ITERS
    for j in reversed(range(ITERS)):
        running = target[j]
        for k in range(j + 1, ITERS):
            running = running - matrix_rows[j][k] * coeffs[k]
        coeffs[j] = running / matrix_rows[j][j]
    return coeffs

def reference(held_head, held_head_old, material_ids, block_map, conductivity, vg_alpha, vg_n, capacity):
    global_map = block_map.astype(jnp.int32)
    numbers = jnp.arange(BRICKS, dtype=jnp.int32)
    holder = lax.optimization_barrier(jnp.sum(jnp.where(global_map[None, :, :] == numbers[:, None, None], numbers[None, :, None], 0), axis=1))

    def relay_one(held):
        pieces = held.reshape((BRICKS, BRICKS, SLAB, CX, CY))
        bricks = pieces[holder, numbers[None, :]]
        bricks = bricks.reshape((N_GX, N_GY, NZ, CX, CY))
        return jnp.transpose(bricks, (2, 0, 3, 1, 4)).reshape((NZ, NX, NY))
    head = relay_one(held_head)
    head_old = relay_one(held_head_old)
    cond_x, cond_y, cond_z, alpha_cell, expo_cell, cap_cell = properties(material_ids, conductivity, vg_alpha, vg_n, capacity)
    ones_field = jnp.ones_like(head)
    (saturation, relperm), (d_sat, d_rel) = jax.jvp(lambda level: retention(level, alpha_cell, expo_cell), (head,), (ones_field,))
    old_sat = retention(head_old, alpha_cell, expo_cell)[0]
    pad_head = jnp.pad(head, 1)
    pad_rel = jnp.pad(relperm, 1)
    pad_drel = jnp.pad(d_rel, 1)
    layout = [(1, jnp.pad(cond_x, 1), 0.0), (2, jnp.pad(cond_y, 1), 0.0), (0, jnp.pad(cond_z, 1), 1.0)]
    coefficients = []
    total_in = None
    for axis, pad_cond, rise in layout:
        along, slope, flux = face_terms(pad_head, pad_rel, pad_cond, axis, rise)
        coefficients.append((axis, along, slope))
        inflow = net_inflow(flux, axis)
        total_in = inflow if total_in is None else total_in + inflow
    newton_residual = STORE * cap_cell * (saturation - old_sat) - total_in
    diagonal = STORE * cap_cell * d_sat

    def apply_jacobian(field):
        pad_field = jnp.pad(field, 1)
        pad_weighted = pad_drel * pad_field
        total_change = None
        for axis, along, slope in coefficients:
            field_low, field_high = pair_slices(pad_field, axis)
            weight_low, weight_high = pair_slices(pad_weighted, axis)
            change = along * (field_high - field_low) + slope * (weight_low + weight_high)
            inflow = net_inflow(change, axis)
            total_change = inflow if total_change is None else total_change + inflow
        return diagonal * field - total_change
    start = -newton_residual
    beta = jnp.sqrt(jnp.sum(start * start))
    basis = [start / beta]
    hess = jnp.zeros((ITERS + 1, ITERS), newton_residual.dtype)
    for j in range(ITERS):
        image = apply_jacobian(basis[j])
        products = [jnp.sum(image * vector) for vector in basis]
        for k in range(j + 1):
            image = image - products[k] * basis[k]
        norm_value = jnp.sqrt(jnp.sum(image * image))
        for k in range(j + 1):
            hess = hess.at[k, j].set(products[k])
        hess = hess.at[j + 1, j].set(norm_value)
        if j + 1 < ITERS:
            basis.append(image / norm_value)
    coeffs = least_squares(hess, beta)
    update = coeffs[0] * basis[0]
    for k in range(1, ITERS):
        update = update + coeffs[k] * basis[k]
    return update
```

```python
import jax
import jax.numpy as jnp
from jax import lax
from jax.experimental import pallas as pl
from jax.experimental.pallas import tpu as pltpu
from jax.sharding import PartitionSpec as P

MATERIALS = 16
STORE = 4.0
AXES = ("gx", "gy")

PIECE = 40
DEPTH = 5
EX = 8 + 2 * DEPTH
EY = 144
PY = 160
CHUNK = 24
CHUNKS = EY // CHUNK
PAIRS = [(i, j) for j in range(1, 5) for i in range(0, j + 1)]


def f32(*shape):
    return jax.ShapeDtypeStruct(shape, jnp.float32)


def params(mib):
    return pltpu.CompilerParams(vmem_limit_bytes=mib << 20)


VMEM = pl.BlockSpec(memory_space=pltpu.VMEM)
SMEM = pl.BlockSpec(memory_space=pltpu.SMEM)


def iota(shape, axis):
    return lax.broadcasted_iota(jnp.int32, shape, axis)


def loop(count, body):
    lax.fori_loop(0, count, lambda i, c: (body(i), c)[1], 0)


def pack_kernel(slot_of, head, old, out, edge):
    sub = iota((8, 128), 0)

    def brick(b):
        own = slot_of[b]
        below = slot_of[jnp.maximum(b - 8, 0)]
        above = slot_of[jnp.minimum(b + 8, 127)]
        head_below, head_above = head[below], head[above]
        old_below, old_above = old[below], old[above]

        def put(tile, value):
            out[pl.ds(pl.multiple_of(b * PIECE + 8 * tile, 8), 8), :] = value

        put(0, head[own])
        put(1, old[own])
        put(2, jnp.where(sub >= 3, head_below, head_above))
        put(3, jnp.where(sub < 3, old_above, jnp.where(sub < 5, head_above, old_below)))
        put(4, jnp.where(sub == 3, old_above, old_below))

    def four(i):
        for k in range(4):
            brick(4 * i + k)

    loop(32, four)
    lane = iota((128, 128), 1)
    edge[0:16, :] = jnp.full((16, 128), -1.0, jnp.float32)
    edge[144:160, :] = jnp.full((16, 128), -1.0, jnp.float32)
    for field, (y_row, corner_row) in enumerate(((32, 34), (33, 37))):
        columns = jnp.zeros((128, 128), jnp.float32)
        for x in range(8):
            rows = out[pl.ds(8 * field + x, 128, stride=PIECE), :]
            low = pltpu.roll(rows, (8 * x + 8) % 128, 1)
            high = pltpu.roll(rows, 64 + 8 * x, 1)
            columns = jnp.where((lane >= 8 * x) & (lane < 8 * x + 8), low, columns)
            columns = jnp.where((lane >= 64 + 8 * x) & (lane < 72 + 8 * x), high, columns)
        edge[16:144, :] = columns
        out[pl.ds(y_row, 128, stride=PIECE), :] = jnp.where(lane < 64, edge[15:143, :], edge[17:145, :])
        out[pl.ds(corner_row, 128, stride=PIECE), :] = jnp.where(
            lane < 64,
            jnp.where(lane < 32, edge[23:151, :], edge[7:135, :]),
            jnp.where(lane < 96, edge[25:153, :], edge[9:137, :]),
        )


def turn_ids_kernel(ids, out):
    for x in range(8):
        out[x] = ids[pl.ds(x, 128, stride=8), :].astype(jnp.float32).T


def properties_kernel(
    place, conductivity, vg_alpha, vg_n, capacity, below, own, above, y_low, y_high,
    alpha, expo, exponent, cap, trans_x, trans_y, trans_z, cond_x, cond_y,
):
    def lookup(ids, rows):
        fields = [jnp.zeros(ids.shape, jnp.float32) for _ in range(6)]
        for m in range(MATERIALS):
            match = ids == float(m)
            values = (
                conductivity[0, m], conductivity[1, m], conductivity[2, m],
                vg_alpha[m], vg_n[m], capacity[m],
            )
            fields = [jnp.where(match, value, field) for value, field in zip(values, fields)]
        return fields

    lane = iota((8, 128), 1)

    def fill(xi, tile, ids):
        rows = pl.ds(8 * tile if isinstance(tile, int) else pl.multiple_of(8 * tile, 8), 8)
        next_rows = pl.ds(8 + 8 * tile if isinstance(tile, int) else pl.multiple_of(8 + 8 * tile, 8), 8)
        kx, ky, kz, a, n, c = lookup(ids, rows)
        alpha[xi, rows, :] = a
        expo[xi, rows, :] = n
        exponent[xi, rows, :] = 1.0 - 1.0 / n
        cap[xi, rows, :] = STORE * c
        cond_x[xi, rows, :] = kx
        cond_y[xi, next_rows, :] = ky
        kz_up = pltpu.roll(kz, 127, 1)
        trans_z[xi, rows, :] = jnp.where(lane < 127, 2.0 * kz * kz_up / (kz + kz_up), 0.0)

    def fill_row(xi, source, x):
        fill(xi, 0, y_low[xi])
        fill(xi, 17, y_high[xi])

        def tiles(t):
            for k in range(2):
                fill(xi, 1 + 2 * t + k, source[x, pl.ds(pl.multiple_of(16 * t + 8 * k, 8), 8), :])

        loop(8, tiles)

    loop(5, lambda x: fill_row(x, below, x))
    loop(8, lambda x: fill_row(x + 5, own, x))
    loop(5, lambda x: fill_row(x + 13, above, x))

    x_first = place[0] * 8 - DEPTH
    y_first = place[1] * 128 - 8
    row = iota((CHUNK, 128), 0)

    def faces(xi):
        x = x_first + xi
        inside = jnp.where((x >= 0) & (x + 1 < place[2] * 8), 1.0, 0.0)
        for c in range(CHUNKS):
            rows = slice(CHUNK * c, CHUNK * (c + 1))
            a, b = cond_x[xi, rows, :], cond_x[jnp.minimum(xi + 1, EX - 1), rows, :]
            trans_x[xi, rows, :] = inside * (2.0 * a * b / (a + b))
            a = cond_y[xi, 8 + CHUNK * c : 8 + CHUNK * (c + 1), :]
            b = cond_y[xi, 9 + CHUNK * c : 9 + CHUNK * (c + 1), :]
            y = y_first + CHUNK * c + row
            trans_y[xi, 8 + CHUNK * c : 8 + CHUNK * (c + 1), :] = jnp.where(
                (y >= 0) & (y + 1 < place[3] * 128), 2.0 * a * b / (a + b), 0.0
            )

    loop(EX, faces)


def wetness(level, alpha, expo, exponent):
    power = jnp.exp(expo * jnp.log(alpha * -level))
    return power, -jnp.log(1.0 + power)


def retention(level, alpha, expo, exponent):
    log_scaled = expo * jnp.log(alpha * -level)
    power = jnp.exp(log_scaled)
    total = 1.0 + power
    inverse = 1.0 / total
    log_inverse = -jnp.log(total)
    root = jnp.exp(0.5 * exponent * log_inverse)
    saturation = root * root
    rest = power * inverse
    z = 1.0 / (1.0 + 2.0 * power)
    zz = z * z
    series = 1.0 / 15.0
    for k in (13.0, 11.0, 9.0, 7.0, 5.0, 3.0, 1.0):
        series = series * zz + 1.0 / k
    log_rest = jnp.where(power >= 1.0, -2.0 * z * series, log_scaled + log_inverse)
    e = exponent * log_rest
    rest_power = jnp.exp(e)
    taylor = 1.0 + e * (1.0 / 8.0)
    for k in (7.0, 6.0, 5.0, 4.0, 3.0, 2.0):
        taylor = 1.0 + (e * (1.0 / k)) * taylor
    inner = jnp.where(e > -0.35, -e * taylor, 1.0 - rest_power)
    relperm = root * inner * inner
    rate = (expo - 1.0) / -level
    d_sat = saturation * rest * rate
    d_rel = root * inner * rate * (0.5 * inner * rest + 2.0 * inverse * rest_power)
    return saturation, relperm, d_sat, d_rel


def split(a, factor):
    c = a * factor
    high = c - (c - a)
    return high, a - high


def two_sum(a, b):
    s = a + b
    t = s - a
    return s, (a - (s - t)) + (b - t)


def df_add(a, b):
    s, e = two_sum(a[0], b[0])
    e = e + (a[1] + b[1])
    t = s + e
    return t, e - (t - s)


def df_mul(a, b):
    ah, al = split(a[0], 4097.0)
    bh, bl = split(b[0], 4097.0)
    p = a[0] * b[0]
    e = ((ah * bh - p) + ah * bl + al * bh) + al * bl
    e = e + (a[0] * b[1] + a[1] * b[0])
    t = p + e
    return t, e - (t - p)


def df_neg(a):
    return -a[0], -a[1]


def df_div(a, b):
    q = a[0] / b[0]
    zero = jnp.zeros_like(q)
    r = df_add(a, df_neg(df_mul((q, zero), b)))
    q2 = r[0] / b[0]
    r = df_add(r, df_neg(df_mul((q2, zero), b)))
    q3 = r[0] / b[0]
    s, e = two_sum(q, q2)
    return two_sum(s, e + q3)


def main_kernel(
    source, recv, alpha, expo, exponent, cap, trans_x, trans_y, trans_z, kept, sums,
    ordered, head, old, rel, d_rel, own_c, cxp, cxm, cyp, cym, czp, czm, k0, k1, k2, k3, k4,
):
    sub = iota((8, 128), 0)
    lane = iota((8, 128), 1)

    def layer(z):
        def tile(k, t):
            return recv[pl.ds(pl.multiple_of(source[k, z] * PIECE + 8 * t, 8), 8), :]

        def put(t, value):
            ordered[pl.ds(pl.multiple_of(z * PIECE + 8 * t, 8), 8), :] = value

        put(0, tile(0, 0))
        put(1, tile(0, 1))
        put(2, jnp.where(sub >= 3, tile(1, 2), tile(2, 2)))
        put(3, jnp.where(sub < 5, tile(2, 3), tile(1, 3)))
        sides = jnp.where(lane < 64, tile(3, 4), tile(4, 4))
        corners = jnp.where(
            lane < 64,
            jnp.where(lane < 32, tile(5, 4), tile(6, 4)),
            jnp.where(lane < 96, tile(7, 4), tile(8, 4)),
        )
        put(
            4,
            jnp.where(
                sub < 2, sides, jnp.where(sub == 3, tile(2, 4), jnp.where(sub == 4, tile(1, 4), corners))
            ),
        )

    def two_layers(i):
        layer(2 * i)
        layer(2 * i + 1)

    loop(64, two_layers)

    def plane(r):
        return ordered[pl.ds(r, 128, stride=PIECE), :].T

    for xi, r in enumerate([19, 20, 21, 22, 23] + list(range(8)) + [16, 17, 18, 27, 28]):
        head[xi, 16:144, :] = plane(r)
    for xi, r in enumerate([36, 29, 30, 31] + list(range(8, 16)) + [24, 25, 26, 35]):
        old[xi + 1, 16:144, :] = plane(r)
    for field, (y_row, corner_row) in ((head, (32, 34)), (old, (33, 37))):
        sides = plane(y_row)
        for x in range(8):
            field[5 + x, 8:16, :] = sides[8 * x : 8 * x + 8]
            field[5 + x, 144:152, :] = sides[64 + 8 * x : 72 + 8 * x]
        corners = plane(corner_row)
        for k in range(4):
            field[13 + k, 8:16, :] = corners[8 * k : 8 * k + 8]
            field[1 + k, 8:16, :] = corners[32 + 8 * k : 40 + 8 * k]
            field[13 + k, 144:152, :] = corners[64 + 8 * k : 72 + 8 * k]
            field[1 + k, 144:152, :] = corners[96 + 8 * k : 104 + 8 * k]
    for xi in (0, 17):
        head[xi, 8:16, :] = jnp.full((8, 128), -1.0, jnp.float32)
        head[xi, 144:152, :] = jnp.full((8, 128), -1.0, jnp.float32)

    def curves(xi):
        for c in range(CHUNKS):
            at = slice(CHUNK * c, CHUNK * (c + 1))
            to = slice(8 + CHUNK * c, 8 + CHUNK * (c + 1))
            sat_v, rel_v, dsat_v, drel_v = retention(
                head[xi, to, :], alpha[xi, at, :], expo[xi, at, :], exponent[xi, at, :]
            )
            k0[xi, to, :] = sat_v
            rel[xi, to, :] = rel_v
            d_rel[xi, to, :] = drel_v
            own_c[xi, to, :] = cap[xi, at, :] * dsat_v

    loop(EX, curves)

    def face(t, h_a, h_b, r_a, r_b, d_a, d_b, rise):
        potential = h_b - h_a
        if rise:
            potential = potential + rise
        along = t * (0.5 * (r_a + r_b))
        slope = (0.5 * t) * potential
        return along, slope, along * potential, slope * (d_a + d_b)

    def coefficients(i):
        xi = i + 1
        for c in range(CHUNKS):
            at = slice(CHUNK * c, CHUNK * (c + 1))
            to = slice(8 + CHUNK * c, 8 + CHUNK * (c + 1))
            up = slice(9 + CHUNK * c, 9 + CHUNK * (c + 1))
            down = slice(7 + CHUNK * c, 7 + CHUNK * (c + 1))
            _, log_old = wetness(old[xi, to, :], alpha[xi, at, :], expo[xi, at, :], exponent[xi, at, :])
            old_sat = jnp.exp(exponent[xi, at, :] * log_old)
            start = cap[xi, at, :] * (old_sat - k0[xi, to, :])
            h, r, d = head[xi, to, :], rel[xi, to, :], d_rel[xi, to, :]
            centre = own_c[xi, to, :]
            around = (
                (
                    trans_x[xi, at, :], trans_x[xi - 1, at, :], 0.0, cxp, cxm,
                    [f[xi + 1, to, :] for f in (head, rel, d_rel)],
                    [f[xi - 1, to, :] for f in (head, rel, d_rel)],
                ),
                (
                    trans_y[xi, to, :], trans_y[xi, down, :], 0.0, cyp, cym,
                    [f[xi, up, :] for f in (head, rel, d_rel)],
                    [f[xi, down, :] for f in (head, rel, d_rel)],
                ),
                (
                    trans_z[xi, at, :], pltpu.roll(trans_z[xi, at, :], 1, 1), 1.0, czp, czm,
                    [pltpu.roll(f, 127, 1) for f in (h, r, d)],
                    [pltpu.roll(f, 1, 1) for f in (h, r, d)],
                ),
            )
            for t_p, t_m, rise, c_p, c_m, (h_p, r_p, d_p), (h_m, r_m, d_m) in around:
                along, slope, flux, both = face(t_p, h, h_p, r, r_p, d, d_p, rise)
                along_m, slope_m, flux_m, both_m = face(t_m, h_m, h, r_m, r, d_m, d, rise)
                c_p[xi, to, :] = along + slope * d_p
                c_m[xi, to, :] = along_m - slope_m * d_m
                start = start + (flux - flux_m)
                centre = centre - (both - both_m)
            own_c[xi, to, :] = centre
            k0[xi, to, :] = start

    loop(16, coefficients)

    vectors = (k0, k1, k2, k3, k4)
    for step in range(4):
        v_ref, w_ref = vectors[step], vectors[step + 1]

        def apply(i):
            xi = i + 2 + step
            for c in range(CHUNKS):
                to = slice(8 + CHUNK * c, 8 + CHUNK * (c + 1))
                up = slice(9 + CHUNK * c, 9 + CHUNK * (c + 1))
                down = slice(7 + CHUNK * c, 7 + CHUNK * (c + 1))
                v = v_ref[xi, to, :]
                w = own_c[xi, to, :] * v
                w = w + cxp[xi, to, :] * (v - v_ref[xi + 1, to, :])
                w = w + cxm[xi, to, :] * (v - v_ref[xi - 1, to, :])
                w = w + cyp[xi, to, :] * (v - v_ref[xi, up, :])
                w = w + cym[xi, to, :] * (v - v_ref[xi, down, :])
                w = w + czp[xi, to, :] * (v - pltpu.roll(v, 127, 1))
                w = w + czm[xi, to, :] * (v - pltpu.roll(v, 1, 1))
                w_ref[xi, to, :] = w

        loop(14 - 2 * step, apply)

    def largest(i, tops):
        xi = 5 + i
        for c in range(16):
            at = slice(16 + 8 * c, 24 + 8 * c)
            tops = [jnp.maximum(top, jnp.abs(v[xi, at, :])) for top, v in zip(tops, vectors)]
        return tops

    tops = lax.fori_loop(0, 8, largest, [jnp.zeros((8, 128), jnp.float32) for _ in range(5)])
    scales, inverses = [], []
    for top in tops:
        top = jnp.broadcast_to(jnp.max(top, keepdims=True), (8, 128))
        scale = jnp.full((8, 128), 2.0**96, jnp.float32)
        inverse = jnp.full((8, 128), 2.0**-96, jnp.float32)
        for j in range(-5, 7):
            over = top >= 2.0 ** (16 * j - 8)
            scale = jnp.where(over, 2.0 ** (-16 * j), scale)
            inverse = jnp.where(over, 2.0 ** (16 * j), inverse)
        scales.append(scale)
        inverses.append(inverse)

    def products(i, totals):
        leading, rest = totals
        xi = 5 + i // 8
        first = 16 + 16 * (i % 8)
        for k in range(2):
            at = pl.ds(pl.multiple_of(first + 8 * k, 8), 8)
            values = [v[xi, at, :] * scale for v, scale in zip(vectors, scales)]
            halves = [split(value, 65537.0) for value in values]
            leading, rest = list(leading), list(rest)
            for e, (p, q) in enumerate(PAIRS):
                leading[e] = leading[e] + halves[p][0] * halves[q][0]
                rest[e] = rest[e] + (halves[p][0] * halves[q][1] + halves[p][1] * values[q])
        return leading, rest

    zeros = [jnp.zeros((8, 128), jnp.float32) for _ in PAIRS]
    leading, rest = lax.fori_loop(0, 64, products, (zeros, list(zeros)))
    groups = []
    for g in range(2):
        high = jnp.zeros((8, 128), jnp.float32)
        low = jnp.zeros((8, 128), jnp.float32)
        for e in range(8 * g, min(8 * g + 8, len(PAIRS))):
            pair = two_sum(leading[e], rest[e])
            for shift in (4, 2, 1):
                pair = df_add(pair, (pltpu.roll(pair[0], shift, 0), pltpu.roll(pair[1], shift, 0)))
            high = jnp.where(sub == e - 8 * g, pair[0], high)
            low = jnp.where(sub == e - 8 * g, pair[1], low)
        pair = (high, low)
        for shift in (64, 32, 16, 8, 4, 2, 1):
            pair = df_add(pair, (pltpu.roll(pair[0], shift, 1), pltpu.roll(pair[1], shift, 1)))
        groups.append(pair)
    line = jnp.zeros((8, 128), jnp.float32)
    for e in range(len(PAIRS)):
        pair = groups[e // 8]
        for half in range(2):
            line = jnp.where(lane == 16 * half + e, pair[half][e % 8 : e % 8 + 1, :], line)
    for k in range(5):
        line = jnp.where(lane == 32 + k, inverses[k], line)
        line = jnp.where(lane == 40 + k, scales[k], line)
    for t in range(16):
        sums[8 * t : 8 * t + 8, :] = line

    def keep(x):
        for k in range(4):
            kept[k, x] = vectors[k][x + 5, 16:144, :]

    loop(8, keep)


def turn_back_kernel(kept, out):
    for k in range(4):
        for x in range(8):
            out[k, pl.ds(x, 128, stride=8), :] = kept[k, x].T


def finish_kernel(recv, vectors, out):
    data = recv[...]
    lane = iota((128, 128), 1)
    smallest = jnp.min(data, axis=0, keepdims=True)
    factor = data * jnp.broadcast_to(pltpu.roll(jnp.broadcast_to(smallest, (8, 128)), 120, 1)[0:1], (128, 128))
    left = jnp.zeros((128, 128), jnp.float32)
    right = jnp.zeros((128, 128), jnp.float32)
    for k in range(5):
        column = jnp.broadcast_to(factor[:, 32 + k : 33 + k], (128, 128))
        for e, (p, q) in enumerate(PAIRS):
            if p == k:
                left = jnp.where(lane % 16 == e, column, left)
            if q == k:
                right = jnp.where(lane % 16 == e, column, right)
    scaled = data * left * right
    low = pltpu.roll(scaled, 112, 1)
    pair = (scaled[0:8], low[0:8])
    for t in range(1, 16):
        pair = df_add(pair, (scaled[8 * t : 8 * t + 8], low[8 * t : 8 * t + 8]))
    for shift in (4, 2, 1):
        pair = df_add(pair, (pltpu.roll(pair[0], shift, 0), pltpu.roll(pair[1], shift, 0)))
    entry = {}
    for e, (p, q) in enumerate(PAIRS):
        entry[p, q] = tuple(jnp.broadcast_to(half[:, e : e + 1], (8, 128)) for half in pair)

    def scale_of(k):
        return jnp.broadcast_to(smallest[:, k : k + 1], (8, 128))

    rows = {(i, j): entry[i + 1, j + 1] for i in range(4) for j in range(i, 4)}
    right_side = [entry[0, j + 1] for j in range(4)]
    for k in range(4):
        for i in range(k + 1, 4):
            ratio = df_neg(df_div(rows[k, i], rows[k, k]))
            for j in range(i, 4):
                rows[i, j] = df_add(rows[i, j], df_mul(ratio, rows[k, j]))
            right_side[i] = df_add(right_side[i], df_mul(ratio, right_side[k]))
    coeffs = [None] * 4
    for k in reversed(range(4)):
        running = right_side[k]
        for j in range(k + 1, 4):
            running = df_add(running, df_neg(df_mul(rows[k, j], coeffs[j])))
        coeffs[k] = df_div(running, rows[k, k])
    inverse_first = jnp.max(jnp.where(lane == 32, data, 0.0), axis=0, keepdims=True)
    inverse_first = jnp.broadcast_to(jnp.max(inverse_first, axis=1, keepdims=True), (8, 128))
    weights = [(coeffs[k][0] * scale_of(41 + k)) * inverse_first for k in range(4)]

    def rows_of(t):
        for k in range(4):
            at = pl.ds(pl.multiple_of(32 * t + 8 * k, 8), 8)
            total = weights[0] * vectors[0, at, :]
            for j in range(1, 4):
                total = total + weights[j] * vectors[j, at, :]
            out[at, :] = total

    loop(32, rows_of)


def call(kernel, out_shape, in_specs, out_specs, scratch, mib, cost):
    return pl.pallas_call(
        kernel,
        out_shape=out_shape,
        in_specs=in_specs,
        out_specs=out_specs,
        scratch_shapes=scratch,
        compiler_params=params(mib),
        cost_estimate=pl.CostEstimate(flops=cost[0], bytes_accessed=cost[1], transcendentals=0),
    )


def body(held_head, held_head_old, material_ids, block_map, conductivity, vg_alpha, vg_n, capacity):
    count_x, count_y = lax.axis_size("gx"), lax.axis_size("gy")
    devices = count_x * count_y
    at_x, at_y = lax.axis_index("gx"), lax.axis_index("gy")
    own_index = at_x * count_y + at_y
    numbers = jnp.arange(devices, dtype=jnp.int32)
    own_row = block_map[own_index]
    slot_of = jnp.sum(jnp.where(own_row[None, :] == numbers[:, None], numbers[None, :], 0), axis=1)
    scratch = lambda *shape: pltpu.VMEM(shape, jnp.float32)

    packed = call(
        pack_kernel, f32(devices * PIECE, 128), [SMEM, VMEM, VMEM], VMEM, [scratch(PY, 128)], 16, (10**6, 4 * 10**6)
    )(slot_of, held_head, held_head_old)
    arrived = lax.all_to_all(packed, AXES, split_axis=0, concat_axis=0, tiled=True)

    offsets = (0, -count_y, count_y, -1, 1, count_y - 1, -count_y - 1, count_y + 1, -count_y + 1)
    bricks = own_index + jnp.array(offsets, jnp.int32)
    source = jnp.sum(
        jnp.where(block_map[None] == bricks[:, None, None], numbers[None, :, None], 0), axis=1
    )

    ids = call(
        turn_ids_kernel, f32(8, 128, 128), [VMEM], VMEM, [], 8, (10**6, 10**6)
    )(material_ids.reshape(1024, 128))
    up_x = [(i, i + 1) for i in range(count_x - 1)]
    down_x = [(i + 1, i) for i in range(count_x - 1)]
    up_y = [(i, i + 1) for i in range(count_y - 1)]
    down_y = [(i + 1, i) for i in range(count_y - 1)]
    below = lax.ppermute(ids[8 - DEPTH :], "gx", up_x)
    above = lax.ppermute(ids[:DEPTH], "gx", down_x)
    last = jnp.concatenate([part[:, 120:] for part in (below, ids, above)], axis=0)
    first = jnp.concatenate([part[:, :8] for part in (below, ids, above)], axis=0)
    y_low = lax.ppermute(last, "gy", up_y)
    y_high = lax.ppermute(first, "gy", down_y)
    place = jnp.stack([at_x, at_y, jnp.int32(count_x), jnp.int32(count_y)])
    fields = call(
        properties_kernel,
        [f32(EX, EY, 128)] * 5 + [f32(EX, PY, 128), f32(EX, EY, 128)],
        [SMEM] * 5 + [VMEM] * 5,
        [VMEM] * 7,
        [scratch(EX, EY, 128), scratch(EX, PY, 128)],
        24,
        (40 * 10**6, 12 * 10**6),
    )(place, conductivity, vg_alpha, vg_n, capacity, below, ids, above, y_low, y_high)

    kept, sums = call(
        main_kernel,
        [f32(4, 8, 128, 128), f32(devices, 128)],
        [SMEM] + [VMEM] * 8,
        [VMEM] * 2,
        [scratch(devices * PIECE, 128)] + [scratch(EX, PY, 128)] * 16,
        56,
        (200 * 10**6, 16 * 10**6),
    )(source, arrived, *fields)
    gathered = lax.all_to_all(sums.reshape(devices, 1, 128), AXES, split_axis=0, concat_axis=0, tiled=True)
    turned = call(turn_back_kernel, f32(4, 1024, 128), [VMEM], VMEM, [], 8, (10**6, 4 * 10**6))(kept)
    update = call(finish_kernel, f32(1024, 128), [VMEM] * 2, VMEM, [], 16, (10**6, 3 * 10**6))(
        gathered.reshape(devices, 128), turned
    )
    return update.reshape(128, 8, 128)


def solution(mesh):
    return jax.shard_map(
        body,
        mesh=mesh,
        in_specs=(
            P(("gx", "gy"), None, None),
            P(("gx", "gy"), None, None),
            P(None, "gx", "gy"),
            P(),
            P(),
            P(),
            P(),
            P(),
        ),
        out_specs=P(None, "gx", "gy"),
        check_vma=False,
    )
```

```python
import jax
import jax.numpy as jnp
from jax import lax
from jax.experimental import pallas as pl
from jax.experimental.pallas import tpu as pltpu
from jax.sharding import PartitionSpec as P

MATERIALS = 16
STORE = 4.0
AXES = ("gx", "gy")

PIECE = 40
DEPTH = 5
EX = 8 + 2 * DEPTH
EY = 144
PY = 160
CHUNK = 24
CHUNKS = EY // CHUNK
PAIRS = [(i, j) for j in range(1, 5) for i in range(0, j + 1)]


def f32(*shape):
    return jax.ShapeDtypeStruct(shape, jnp.float32)


def params(mib):
    return pltpu.CompilerParams(vmem_limit_bytes=mib << 20)


VMEM = pl.BlockSpec(memory_space=pltpu.VMEM)
SMEM = pl.BlockSpec(memory_space=pltpu.SMEM)
HBM = pl.BlockSpec(memory_space=pltpu.HBM)


def iota(shape, axis):
    return lax.broadcasted_iota(jnp.int32, shape, axis)


def loop(count, body):
    lax.fori_loop(0, count, lambda i, c: (body(i), c)[1], 0)


def pack_kernel(slot_of, head, old, packed, out, edge, sem):
    sub = iota((8, 128), 0)

    def brick(b):
        own = slot_of[b]
        below = slot_of[jnp.maximum(b - 8, 0)]
        above = slot_of[jnp.minimum(b + 8, 127)]
        head_below, head_above = head[below], head[above]
        old_below, old_above = old[below], old[above]

        def put(tile, value):
            out[pl.ds(pl.multiple_of(b * PIECE + 8 * tile, 8), 8), :] = value

        put(0, head[own])
        put(1, old[own])
        put(2, jnp.where(sub >= 3, head_below, head_above))
        put(3, jnp.where(sub < 3, old_above, jnp.where(sub < 5, head_above, old_below)))
        put(4, jnp.where(sub == 3, old_above, old_below))

    def four(i):
        for k in range(4):
            brick(4 * i + k)

    loop(32, four)
    lane = iota((128, 128), 1)
    edge[0:16, :] = jnp.full((16, 128), -1.0, jnp.float32)
    edge[144:160, :] = jnp.full((16, 128), -1.0, jnp.float32)
    for field, (y_row, corner_row) in enumerate(((32, 34), (33, 37))):
        columns = jnp.zeros((128, 128), jnp.float32)
        for x in range(8):
            rows = out[pl.ds(8 * field + x, 128, stride=PIECE), :]
            low = pltpu.roll(rows, (8 * x + 8) % 128, 1)
            high = pltpu.roll(rows, 64 + 8 * x, 1)
            columns = jnp.where((lane >= 8 * x) & (lane < 8 * x + 8), low, columns)
            columns = jnp.where((lane >= 64 + 8 * x) & (lane < 72 + 8 * x), high, columns)
        edge[16:144, :] = columns
        out[pl.ds(y_row, 128, stride=PIECE), :] = jnp.where(lane < 64, edge[15:143, :], edge[17:145, :])
        out[pl.ds(corner_row, 128, stride=PIECE), :] = jnp.where(
            lane < 64,
            jnp.where(lane < 32, edge[23:151, :], edge[7:135, :]),
            jnp.where(lane < 96, edge[25:153, :], edge[9:137, :]),
        )
    copy = pltpu.make_async_copy(out, packed, sem)
    copy.start()
    copy.wait()


def turn_ids_kernel(ids, out, first, last):
    for x in range(8):
        plane = ids[pl.ds(x, 128, stride=8), :].astype(jnp.float32).T
        out[x] = plane
        first[x] = plane[:8]
        last[x] = plane[120:]


def widen_ids_kernel(y_low, own, y_high, wide, first, last):
    for x in range(8):
        wide[x, 0:8, :] = y_low[x]
        wide[x, 8:136, :] = own[x]
        wide[x, 136:144, :] = y_high[x]
    for x in range(DEPTH):
        for to, k in ((first, x), (last, x + 8 - DEPTH)):
            to[x, 0:8, :] = y_low[k]
            to[x, 8:136, :] = own[k]
            to[x, 136:144, :] = y_high[k]


def properties_kernel(
    place, conductivity, vg_alpha, vg_n, capacity, below, own, above,
    out_a, out_n, out_m, out_c, out_x, out_y, out_z,
    alpha, expo, exponent, cap, trans_x, trans_y, trans_z, cond_x, cond_y, sems,
):
    def copies(first, last):
        made = (alpha, expo, exponent, cap, trans_x, trans_y, trans_z)
        outs = (out_a, out_n, out_m, out_c, out_x, out_y, out_z)
        return [pltpu.make_async_copy(made[k], outs[k], sems.at[k]) for k in range(first, last)]

    def lookup(ids, rows):
        fields = [jnp.zeros(ids.shape, jnp.float32) for _ in range(6)]
        for m in range(MATERIALS):
            match = ids == float(m)
            values = (
                conductivity[0, m], conductivity[1, m], conductivity[2, m],
                vg_alpha[m], vg_n[m], capacity[m],
            )
            fields = [jnp.where(match, value, field) for value, field in zip(values, fields)]
        return fields

    lane = iota((8, 128), 1)

    def fill(xi, tile, ids):
        rows = pl.ds(8 * tile if isinstance(tile, int) else pl.multiple_of(8 * tile, 8), 8)
        next_rows = pl.ds(8 + 8 * tile if isinstance(tile, int) else pl.multiple_of(8 + 8 * tile, 8), 8)
        kx, ky, kz, a, n, c = lookup(ids, rows)
        alpha[xi, rows, :] = a
        expo[xi, rows, :] = n
        exponent[xi, rows, :] = 1.0 - 1.0 / n
        cap[xi, rows, :] = STORE * c
        cond_x[xi, rows, :] = kx
        cond_y[xi, next_rows, :] = ky
        kz_up = pltpu.roll(kz, 127, 1)
        trans_z[xi, rows, :] = jnp.where(lane < 127, 2.0 * kz * kz_up / (kz + kz_up), 0.0)

    def fill_row(xi, source, x):
        def tiles(t):
            for k in range(2):
                fill(xi, 2 * t + k, source[x, pl.ds(pl.multiple_of(16 * t + 8 * k, 8), 8), :])

        loop(9, tiles)

    loop(5, lambda x: fill_row(x, below, x))
    loop(8, lambda x: fill_row(x + 5, own, x))
    loop(5, lambda x: fill_row(x + 13, above, x))

    for copy in copies(0, 4):
        copy.start()
    x_first = place[0] * 8 - DEPTH
    y_first = place[1] * 128 - 8
    row = iota((CHUNK, 128), 0)

    def faces(xi):
        x = x_first + xi
        inside = jnp.where((x >= 0) & (x + 1 < place[2] * 8), 1.0, 0.0)
        for c in range(CHUNKS):
            rows = slice(CHUNK * c, CHUNK * (c + 1))
            a, b = cond_x[xi, rows, :], cond_x[jnp.minimum(xi + 1, EX - 1), rows, :]
            trans_x[xi, rows, :] = inside * (2.0 * a * b / (a + b))
            a = cond_y[xi, 8 + CHUNK * c : 8 + CHUNK * (c + 1), :]
            b = cond_y[xi, 9 + CHUNK * c : 9 + CHUNK * (c + 1), :]
            y = y_first + CHUNK * c + row
            trans_y[xi, 8 + CHUNK * c : 8 + CHUNK * (c + 1), :] = jnp.where(
                (y >= 0) & (y + 1 < place[3] * 128), 2.0 * a * b / (a + b), 0.0
            )

    loop(EX, faces)
    for copy in copies(4, 7):
        copy.start()
    for copy in copies(0, 7):
        copy.wait()


def wetness(level, alpha, expo, exponent):
    power = jnp.exp(expo * jnp.log(alpha * -level))
    return power, -jnp.log(1.0 + power)


def retention(level, alpha, expo, exponent):
    log_scaled = expo * jnp.log(alpha * -level)
    power = jnp.exp(log_scaled)
    total = 1.0 + power
    inverse = 1.0 / total
    log_inverse = -jnp.log(total)
    root = jnp.exp(0.5 * exponent * log_inverse)
    saturation = root * root
    rest = power * inverse
    z = 1.0 / (1.0 + 2.0 * power)
    zz = z * z
    series = 1.0 / 15.0
    for k in (13.0, 11.0, 9.0, 7.0, 5.0, 3.0, 1.0):
        series = series * zz + 1.0 / k
    log_rest = jnp.where(power >= 1.0, -2.0 * z * series, log_scaled + log_inverse)
    e = exponent * log_rest
    rest_power = jnp.exp(e)
    taylor = 1.0 + e * (1.0 / 8.0)
    for k in (7.0, 6.0, 5.0, 4.0, 3.0, 2.0):
        taylor = 1.0 + (e * (1.0 / k)) * taylor
    inner = jnp.where(e > -0.35, -e * taylor, 1.0 - rest_power)
    relperm = root * inner * inner
    rate = (expo - 1.0) / -level
    d_sat = saturation * rest * rate
    d_rel = root * inner * rate * (0.5 * inner * rest + 2.0 * inverse * rest_power)
    return saturation, relperm, d_sat, d_rel


def split(a, factor):
    c = a * factor
    high = c - (c - a)
    return high, a - high


def two_sum(a, b):
    s = a + b
    t = s - a
    return s, (a - (s - t)) + (b - t)


def df_add(a, b):
    s, e = two_sum(a[0], b[0])
    e = e + (a[1] + b[1])
    t = s + e
    return t, e - (t - s)


def df_mul(a, b):
    ah, al = split(a[0], 4097.0)
    bh, bl = split(b[0], 4097.0)
    p = a[0] * b[0]
    e = ((ah * bh - p) + ah * bl + al * bh) + al * bl
    e = e + (a[0] * b[1] + a[1] * b[0])
    t = p + e
    return t, e - (t - p)


def df_neg(a):
    return -a[0], -a[1]


def df_div(a, b):
    q = a[0] / b[0]
    zero = jnp.zeros_like(q)
    r = df_add(a, df_neg(df_mul((q, zero), b)))
    q2 = r[0] / b[0]
    r = df_add(r, df_neg(df_mul((q2, zero), b)))
    q3 = r[0] / b[0]
    s, e = two_sum(q, q2)
    return two_sum(s, e + q3)


def main_kernel(
    source, recv, in_a, in_n, in_m, in_c, in_x, in_y, in_z, kept, sums,
    alpha, expo, exponent, cap, trans_x, trans_y, trans_z, sems, ordered, head, old, rel, d_rel, own_c, cxp, cxm, cyp, cym, czp, czm, k0, k1, k2, k3, k4,
):
    sub = iota((8, 128), 0)
    lane = iota((8, 128), 1)
    refs = (
        (in_a, alpha), (in_n, expo), (in_m, exponent), (in_c, cap),
        (in_x, trans_x), (in_y, trans_y), (in_z, trans_z),
    )
    copies = [pltpu.make_async_copy(a, b, sems.at[k]) for k, (a, b) in enumerate(refs)]
    for copy in copies:
        copy.start()

    def layer(z):
        def tile(k, t):
            return recv[pl.ds(pl.multiple_of(source[k, z] * PIECE + 8 * t, 8), 8), :]

        def put(t, value):
            ordered[pl.ds(pl.multiple_of(z * PIECE + 8 * t, 8), 8), :] = value

        put(0, tile(0, 0))
        put(1, tile(0, 1))
        put(2, jnp.where(sub >= 3, tile(1, 2), tile(2, 2)))
        put(3, jnp.where(sub < 5, tile(2, 3), tile(1, 3)))
        sides = jnp.where(lane < 64, tile(3, 4), tile(4, 4))
        corners = jnp.where(
            lane < 64,
            jnp.where(lane < 32, tile(5, 4), tile(6, 4)),
            jnp.where(lane < 96, tile(7, 4), tile(8, 4)),
        )
        put(
            4,
            jnp.where(
                sub < 2, sides, jnp.where(sub == 3, tile(2, 4), jnp.where(sub == 4, tile(1, 4), corners))
            ),
        )

    def two_layers(i):
        layer(2 * i)
        layer(2 * i + 1)

    loop(64, two_layers)

    def plane(r):
        return ordered[pl.ds(r, 128, stride=PIECE), :].T

    for xi, r in enumerate([19, 20, 21, 22, 23] + list(range(8)) + [16, 17, 18, 27, 28]):
        head[xi, 16:144, :] = plane(r)
    for xi, r in enumerate([36, 29, 30, 31] + list(range(8, 16)) + [24, 25, 26, 35]):
        old[xi + 1, 16:144, :] = plane(r)
    for field, (y_row, corner_row) in ((head, (32, 34)), (old, (33, 37))):
        sides = plane(y_row)
        for x in range(8):
            field[5 + x, 8:16, :] = sides[8 * x : 8 * x + 8]
            field[5 + x, 144:152, :] = sides[64 + 8 * x : 72 + 8 * x]
        corners = plane(corner_row)
        for k in range(4):
            field[13 + k, 8:16, :] = corners[8 * k : 8 * k + 8]
            field[1 + k, 8:16, :] = corners[32 + 8 * k : 40 + 8 * k]
            field[13 + k, 144:152, :] = corners[64 + 8 * k : 72 + 8 * k]
            field[1 + k, 144:152, :] = corners[96 + 8 * k : 104 + 8 * k]
    for xi in (0, 17):
        head[xi, 8:16, :] = jnp.full((8, 128), -1.0, jnp.float32)
        head[xi, 144:152, :] = jnp.full((8, 128), -1.0, jnp.float32)

    def curves(xi):
        for c in range(CHUNKS):
            at = slice(CHUNK * c, CHUNK * (c + 1))
            to = slice(8 + CHUNK * c, 8 + CHUNK * (c + 1))
            sat_v, rel_v, dsat_v, drel_v = retention(
                head[xi, to, :], alpha[xi, at, :], expo[xi, at, :], exponent[xi, at, :]
            )
            k0[xi, to, :] = sat_v
            rel[xi, to, :] = rel_v
            d_rel[xi, to, :] = drel_v
            own_c[xi, to, :] = cap[xi, at, :] * dsat_v

    for copy in copies:
        copy.wait()
    loop(EX, curves)

    def face(t, h_a, h_b, r_a, r_b, d_a, d_b, rise):
        potential = h_b - h_a
        if rise:
            potential = potential + rise
        along = t * (0.5 * (r_a + r_b))
        slope = (0.5 * t) * potential
        return along, slope, along * potential, slope * (d_a + d_b)

    def coefficients(i):
        xi = i + 1
        for c in range(CHUNKS):
            at = slice(CHUNK * c, CHUNK * (c + 1))
            to = slice(8 + CHUNK * c, 8 + CHUNK * (c + 1))
            up = slice(9 + CHUNK * c, 9 + CHUNK * (c + 1))
            down = slice(7 + CHUNK * c, 7 + CHUNK * (c + 1))
            _, log_old = wetness(old[xi, to, :], alpha[xi, at, :], expo[xi, at, :], exponent[xi, at, :])
            old_sat = jnp.exp(exponent[xi, at, :] * log_old)
            start = cap[xi, at, :] * (old_sat - k0[xi, to, :])
            h, r, d = head[xi, to, :], rel[xi, to, :], d_rel[xi, to, :]
            centre = own_c[xi, to, :]
            around = (
                (
                    trans_x[xi, at, :], trans_x[xi - 1, at, :], 0.0, cxp, cxm,
                    [f[xi + 1, to, :] for f in (head, rel, d_rel)],
                    [f[xi - 1, to, :] for f in (head, rel, d_rel)],
                ),
                (
                    trans_y[xi, to, :], trans_y[xi, down, :], 0.0, cyp, cym,
                    [f[xi, up, :] for f in (head, rel, d_rel)],
                    [f[xi, down, :] for f in (head, rel, d_rel)],
                ),
                (
                    trans_z[xi, at, :], pltpu.roll(trans_z[xi, at, :], 1, 1), 1.0, czp, czm,
                    [pltpu.roll(f, 127, 1) for f in (h, r, d)],
                    [pltpu.roll(f, 1, 1) for f in (h, r, d)],
                ),
            )
            for t_p, t_m, rise, c_p, c_m, (h_p, r_p, d_p), (h_m, r_m, d_m) in around:
                along, slope, flux, both = face(t_p, h, h_p, r, r_p, d, d_p, rise)
                along_m, slope_m, flux_m, both_m = face(t_m, h_m, h, r_m, r, d_m, d, rise)
                c_p[xi, to, :] = along + slope * d_p
                c_m[xi, to, :] = along_m - slope_m * d_m
                start = start + (flux - flux_m)
                centre = centre - (both - both_m)
            own_c[xi, to, :] = centre
            k0[xi, to, :] = start

    loop(16, coefficients)

    vectors = (k0, k1, k2, k3, k4)
    for step in range(4):
        v_ref, w_ref = vectors[step], vectors[step + 1]

        def apply(i):
            xi = i + 2 + step
            for c in range(CHUNKS):
                to = slice(8 + CHUNK * c, 8 + CHUNK * (c + 1))
                up = slice(9 + CHUNK * c, 9 + CHUNK * (c + 1))
                down = slice(7 + CHUNK * c, 7 + CHUNK * (c + 1))
                v = v_ref[xi, to, :]
                w = own_c[xi, to, :] * v
                w = w + cxp[xi, to, :] * (v - v_ref[xi + 1, to, :])
                w = w + cxm[xi, to, :] * (v - v_ref[xi - 1, to, :])
                w = w + cyp[xi, to, :] * (v - v_ref[xi, up, :])
                w = w + cym[xi, to, :] * (v - v_ref[xi, down, :])
                w = w + czp[xi, to, :] * (v - pltpu.roll(v, 127, 1))
                w = w + czm[xi, to, :] * (v - pltpu.roll(v, 1, 1))
                w_ref[xi, to, :] = w

        loop(14 - 2 * step, apply)

    keeps = [
        pltpu.make_async_copy(vectors[k].at[5:13, 16:144, :], kept.at[k], sems.at[7 + k]) for k in range(4)
    ]
    for copy in keeps:
        copy.start()

    def largest(i, tops):
        xi = 5 + i
        for c in range(16):
            at = slice(16 + 8 * c, 24 + 8 * c)
            tops = [jnp.maximum(top, jnp.abs(v[xi, at, :])) for top, v in zip(tops, vectors)]
        return tops

    tops = lax.fori_loop(0, 8, largest, [jnp.zeros((8, 128), jnp.float32) for _ in range(5)])
    scales, inverses = [], []
    for top in tops:
        top = jnp.broadcast_to(jnp.max(top, keepdims=True), (8, 128))
        scale = jnp.full((8, 128), 2.0**96, jnp.float32)
        inverse = jnp.full((8, 128), 2.0**-96, jnp.float32)
        for j in range(-5, 7):
            over = top >= 2.0 ** (16 * j - 8)
            scale = jnp.where(over, 2.0 ** (-16 * j), scale)
            inverse = jnp.where(over, 2.0 ** (16 * j), inverse)
        scales.append(scale)
        inverses.append(inverse)

    def products(i, totals):
        leading, rest = totals
        xi = 5 + i // 8
        first = 16 + 16 * (i % 8)
        for k in range(2):
            at = pl.ds(pl.multiple_of(first + 8 * k, 8), 8)
            values = [v[xi, at, :] * scale for v, scale in zip(vectors, scales)]
            halves = [split(value, 65537.0) for value in values]
            leading, rest = list(leading), list(rest)
            for e, (p, q) in enumerate(PAIRS):
                leading[e] = leading[e] + halves[p][0] * halves[q][0]
                rest[e] = rest[e] + (halves[p][0] * halves[q][1] + halves[p][1] * values[q])
        return leading, rest

    zeros = [jnp.zeros((8, 128), jnp.float32) for _ in PAIRS]
    leading, rest = lax.fori_loop(0, 64, products, (zeros, list(zeros)))
    groups = []
    for g in range(2):
        high = jnp.zeros((8, 128), jnp.float32)
        low = jnp.zeros((8, 128), jnp.float32)
        for e in range(8 * g, min(8 * g + 8, len(PAIRS))):
            pair = two_sum(leading[e], rest[e])
            for shift in (4, 2, 1):
                pair = df_add(pair, (pltpu.roll(pair[0], shift, 0), pltpu.roll(pair[1], shift, 0)))
            high = jnp.where(sub == e - 8 * g, pair[0], high)
            low = jnp.where(sub == e - 8 * g, pair[1], low)
        pair = (high, low)
        for shift in (64, 32, 16, 8, 4, 2, 1):
            pair = df_add(pair, (pltpu.roll(pair[0], shift, 1), pltpu.roll(pair[1], shift, 1)))
        groups.append(pair)
    line = jnp.zeros((8, 128), jnp.float32)
    for e in range(len(PAIRS)):
        pair = groups[e // 8]
        for half in range(2):
            line = jnp.where(lane == 16 * half + e, pair[half][e % 8 : e % 8 + 1, :], line)
    for k in range(5):
        line = jnp.where(lane == 32 + k, inverses[k], line)
        line = jnp.where(lane == 40 + k, scales[k], line)
    for t in range(16):
        sums[8 * t : 8 * t + 8, :] = line

    for copy in keeps:
        copy.wait()


def turn_back_kernel(kept, out):
    for k in range(4):
        for x in range(8):
            out[k, pl.ds(x, 128, stride=8), :] = kept[k, x].T


def finish_kernel(recv, vectors, out):
    data = recv[...]
    lane = iota((128, 128), 1)
    smallest = jnp.min(data, axis=0, keepdims=True)
    factor = data * jnp.broadcast_to(pltpu.roll(jnp.broadcast_to(smallest, (8, 128)), 120, 1)[0:1], (128, 128))
    left = jnp.zeros((128, 128), jnp.float32)
    right = jnp.zeros((128, 128), jnp.float32)
    for k in range(5):
        column = jnp.broadcast_to(factor[:, 32 + k : 33 + k], (128, 128))
        for e, (p, q) in enumerate(PAIRS):
            if p == k:
                left = jnp.where(lane % 16 == e, column, left)
            if q == k:
                right = jnp.where(lane % 16 == e, column, right)
    scaled = data * left * right
    low = pltpu.roll(scaled, 112, 1)
    pair = (scaled[0:8], low[0:8])
    for t in range(1, 16):
        pair = df_add(pair, (scaled[8 * t : 8 * t + 8], low[8 * t : 8 * t + 8]))
    for shift in (4, 2, 1):
        pair = df_add(pair, (pltpu.roll(pair[0], shift, 0), pltpu.roll(pair[1], shift, 0)))
    entry = {}
    for e, (p, q) in enumerate(PAIRS):
        entry[p, q] = tuple(jnp.broadcast_to(half[:, e : e + 1], (8, 128)) for half in pair)

    def scale_of(k):
        return jnp.broadcast_to(smallest[:, k : k + 1], (8, 128))

    rows = {(i, j): entry[i + 1, j + 1] for i in range(4) for j in range(i, 4)}
    right_side = [entry[0, j + 1] for j in range(4)]
    for k in range(4):
        for i in range(k + 1, 4):
            ratio = df_neg(df_div(rows[k, i], rows[k, k]))
            for j in range(i, 4):
                rows[i, j] = df_add(rows[i, j], df_mul(ratio, rows[k, j]))
            right_side[i] = df_add(right_side[i], df_mul(ratio, right_side[k]))
    coeffs = [None] * 4
    for k in reversed(range(4)):
        running = right_side[k]
        for j in range(k + 1, 4):
            running = df_add(running, df_neg(df_mul(rows[k, j], coeffs[j])))
        coeffs[k] = df_div(running, rows[k, k])
    inverse_first = jnp.max(jnp.where(lane == 32, data, 0.0), axis=0, keepdims=True)
    inverse_first = jnp.broadcast_to(jnp.max(inverse_first, axis=1, keepdims=True), (8, 128))
    weights = [(coeffs[k][0] * scale_of(41 + k)) * inverse_first for k in range(4)]

    def rows_of(t):
        for k in range(4):
            at = pl.ds(pl.multiple_of(32 * t + 8 * k, 8), 8)
            total = weights[0] * vectors[0, at, :]
            for j in range(1, 4):
                total = total + weights[j] * vectors[j, at, :]
            out[at, :] = total

    loop(32, rows_of)


def call(kernel, out_shape, in_specs, out_specs, scratch, mib, cost):
    return pl.pallas_call(
        kernel,
        out_shape=out_shape,
        in_specs=in_specs,
        out_specs=out_specs,
        scratch_shapes=scratch,
        compiler_params=params(mib),
        cost_estimate=pl.CostEstimate(flops=cost[0], bytes_accessed=cost[1], transcendentals=0),
    )


def body(held_head, held_head_old, material_ids, block_map, conductivity, vg_alpha, vg_n, capacity):
    count_x, count_y = lax.axis_size("gx"), lax.axis_size("gy")
    devices = count_x * count_y
    at_x, at_y = lax.axis_index("gx"), lax.axis_index("gy")
    own_index = at_x * count_y + at_y
    numbers = jnp.arange(devices, dtype=jnp.int32)
    own_row = block_map[own_index]
    slot_of = jnp.sum(jnp.where(own_row[None, :] == numbers[:, None], numbers[None, :], 0), axis=1)
    scratch = lambda *shape: pltpu.VMEM(shape, jnp.float32)

    up_x = [(i, i + 1) for i in range(count_x - 1)]
    down_x = [(i + 1, i) for i in range(count_x - 1)]
    up_y = [(i, i + 1) for i in range(count_y - 1)]
    down_y = [(i + 1, i) for i in range(count_y - 1)]
    ids, first, last = call(
        turn_ids_kernel, [f32(8, 128, 128)] + [f32(8, 8, 128)] * 2, [VMEM], [VMEM] * 3, [], 8, (10**6, 10**6)
    )(material_ids.reshape(1024, 128))
    y_low = lax.ppermute(last, "gy", up_y)
    y_high = lax.ppermute(first, "gy", down_y)
    ids, first, last = call(
        widen_ids_kernel, [f32(8, EY, 128)] + [f32(DEPTH, EY, 128)] * 2, [VMEM] * 3, [VMEM] * 3, [], 8, (10**6, 10**6)
    )(y_low, ids, y_high)
    slot_of, first, last = lax.optimization_barrier((slot_of, first, last))
    below = lax.ppermute(last, "gx", up_x)
    above = lax.ppermute(first, "gx", down_x)

    packed = call(
        pack_kernel,
        f32(devices * PIECE, 128),
        [SMEM, VMEM, VMEM],
        HBM,
        [scratch(devices * PIECE, 128), scratch(PY, 128), pltpu.SemaphoreType.DMA],
        63,
        (10**6, 4 * 10**6),
    )(slot_of, held_head, held_head_old)
    packed, below, above = lax.optimization_barrier((packed, below, above))
    arrived = lax.all_to_all(packed, AXES, split_axis=0, concat_axis=0, tiled=True)

    offsets = (0, -count_y, count_y, -1, 1, count_y - 1, -count_y - 1, count_y + 1, -count_y + 1)
    bricks = own_index + jnp.array(offsets, jnp.int32)
    source = jnp.sum(
        jnp.where(block_map[None] == bricks[:, None, None], numbers[None, :, None], 0), axis=1
    )
    place = jnp.stack([at_x, at_y, jnp.int32(count_x), jnp.int32(count_y)])
    fields = call(
        properties_kernel,
        [f32(EX, EY, 128)] * 5 + [f32(EX, PY, 128), f32(EX, EY, 128)],
        [SMEM] * 5 + [VMEM] * 3,
        [HBM] * 7,
        [scratch(EX, EY, 128)] * 5 + [scratch(EX, PY, 128)] + [scratch(EX, EY, 128)] * 2
        + [scratch(EX, PY, 128), pltpu.SemaphoreType.DMA((7,))],
        63,
        (40 * 10**6, 12 * 10**6),
    )(place, conductivity, vg_alpha, vg_n, capacity, below, ids, above)

    kept, sums = call(
        main_kernel,
        [f32(4, 8, 128, 128), f32(devices, 128)],
        [SMEM, VMEM] + [HBM] * 7,
        [HBM, VMEM],
        [scratch(EX, EY, 128)] * 5 + [scratch(EX, PY, 128), scratch(EX, EY, 128)]
        + [pltpu.SemaphoreType.DMA((11,)), scratch(devices * PIECE, 128)] + [scratch(EX, PY, 128)] * 16,
        63,
        (200 * 10**6, 16 * 10**6),
    )(source, arrived, *fields)
    gathered = lax.all_to_all(sums.reshape(devices, 1, 128), AXES, split_axis=0, concat_axis=0, tiled=True)
    turned = call(turn_back_kernel, f32(4, 1024, 128), [VMEM], VMEM, [], 8, (10**6, 4 * 10**6))(kept)
    update = call(finish_kernel, f32(1024, 128), [VMEM] * 2, VMEM, [], 8, (10**6, 3 * 10**6))(
        gathered.reshape(devices, 128), turned
    )
    return update.reshape(128, 8, 128)


def solution(mesh):
    return jax.shard_map(
        body,
        mesh=mesh,
        in_specs=(
            P(("gx", "gy"), None, None),
            P(("gx", "gy"), None, None),
            P(None, "gx", "gy"),
            P(),
            P(),
            P(),
            P(),
            P(),
        ),
        out_specs=P(None, "gx", "gy"),
        check_vma=False,
    )
```

```python
import jax
import jax.numpy as jnp
from jax import lax
from jax.experimental import pallas as pl
from jax.experimental.pallas import tpu as pltpu
from jax.sharding import PartitionSpec as P

MATERIALS = 16
STORE = 4.0
AXES = ("gx", "gy")

PIECE = 40
DEPTH = 5
EX = 8 + 2 * DEPTH
EY = 144
PY = 160
CHUNK = 24
CHUNKS = EY // CHUNK
PAIRS = [(i, j) for j in range(1, 5) for i in range(0, j + 1)]


def f32(*shape):
    return jax.ShapeDtypeStruct(shape, jnp.float32)


def params(mib):
    return pltpu.CompilerParams(vmem_limit_bytes=mib << 20)


VMEM = pl.BlockSpec(memory_space=pltpu.VMEM)
SMEM = pl.BlockSpec(memory_space=pltpu.SMEM)
HBM = pl.BlockSpec(memory_space=pltpu.HBM)


def iota(shape, axis):
    return lax.broadcasted_iota(jnp.int32, shape, axis)


def loop(count, body):
    lax.fori_loop(0, count, lambda i, c: (body(i), c)[1], 0)


def pack_kernel(slot_of, head, old, packed, out, edge, sem):
    sub = iota((8, 128), 0)

    def brick(b):
        own = slot_of[b]
        below = slot_of[jnp.maximum(b - 8, 0)]
        above = slot_of[jnp.minimum(b + 8, 127)]
        head_below, head_above = head[below], head[above]
        old_below, old_above = old[below], old[above]

        def put(tile, value):
            out[pl.ds(pl.multiple_of(b * PIECE + 8 * tile, 8), 8), :] = value

        put(0, head[own])
        put(1, old[own])
        put(2, jnp.where(sub >= 3, head_below, head_above))
        put(3, jnp.where(sub < 3, old_above, jnp.where(sub < 5, head_above, old_below)))
        put(4, jnp.where(sub == 3, old_above, old_below))

    def four(i):
        for k in range(4):
            brick(4 * i + k)

    loop(32, four)
    lane = iota((128, 128), 1)
    edge[0:16, :] = jnp.full((16, 128), -1.0, jnp.float32)
    edge[144:160, :] = jnp.full((16, 128), -1.0, jnp.float32)
    for field, (y_row, corner_row) in enumerate(((32, 34), (33, 37))):
        columns = jnp.zeros((128, 128), jnp.float32)
        for x in range(8):
            rows = out[pl.ds(8 * field + x, 128, stride=PIECE), :]
            low = pltpu.roll(rows, (8 * x + 8) % 128, 1)
            high = pltpu.roll(rows, 64 + 8 * x, 1)
            columns = jnp.where((lane >= 8 * x) & (lane < 8 * x + 8), low, columns)
            columns = jnp.where((lane >= 64 + 8 * x) & (lane < 72 + 8 * x), high, columns)
        edge[16:144, :] = columns
        out[pl.ds(y_row, 128, stride=PIECE), :] = jnp.where(lane < 64, edge[15:143, :], edge[17:145, :])
        out[pl.ds(corner_row, 128, stride=PIECE), :] = jnp.where(
            lane < 64,
            jnp.where(lane < 32, edge[23:151, :], edge[7:135, :]),
            jnp.where(lane < 96, edge[25:153, :], edge[9:137, :]),
        )
    copy = pltpu.make_async_copy(out, packed, sem)
    copy.start()
    copy.wait()


def turn_ids_kernel(ids, out, first, last):
    for x in range(8):
        plane = ids[pl.ds(x, 128, stride=8), :].astype(jnp.float32).T
        out[x] = plane
        if x < DEPTH:
            first[x] = plane
        if x >= 8 - DEPTH:
            last[x - 8 + DEPTH] = plane


def edge_ids_kernel(below, own, above, first, last):
    for k, part in ((0, below), (5, own), (13, above)):
        for x in range(part.shape[0]):
            first[k + x] = part[x, 0:8, :]
            last[k + x] = part[x, 120:128, :]


def tables_of(conductivity, vg_alpha, vg_n, capacity):
    lane = iota((8, 128), 1)
    reads = [
        lambda m: conductivity[0, m], lambda m: conductivity[1, m], lambda m: conductivity[2, m],
        lambda m: vg_alpha[m], lambda m: vg_n[m], lambda m: capacity[m],
    ]
    tables = []
    for read in reads:
        table = jnp.zeros((8, 128), jnp.float32)
        for m in range(MATERIALS):
            table = jnp.where(lane == m, read(m), table)
        tables.append(table)
    return tables


def lookup(tables, ids):
    index = ids.astype(jnp.int32)
    return [jnp.take_along_axis(table, index, axis=1) for table in tables]


def harmonic(a, b):
    return 2.0 * a * b / (a + b)


def upward_faces(kz):
    return jnp.where(iota(kz.shape, 1) < 127, harmonic(kz, pltpu.roll(kz, 127, 1)), 0.0)


def x_inside(place, xi):
    x = place[0] * 8 - DEPTH + xi
    return jnp.where((x >= 0) & (x + 1 < place[2] * 8), 1.0, 0.0)


def y_inside(place, shape, first):
    y = place[1] * 128 - 8 + first + iota(shape, 0)
    return (y >= 0) & (y + 1 < place[3] * 128)


def properties_kernel(
    place, conductivity, vg_alpha, vg_n, capacity, below, own, above,
    out_a, out_n, out_m, out_c, out_x, out_y, out_z, out_e,
    alpha, expo, exponent, cap, trans_x, trans_y, trans_z, edges, cond_x, cond_y, sems,
):
    def copies(first, last):
        made = (alpha, expo, exponent, cap, trans_x, trans_y, trans_z, edges)
        outs = (out_a, out_n, out_m, out_c, out_x, out_y, out_z, out_e)
        return [pltpu.make_async_copy(made[k], outs[k], sems.at[k]) for k in range(first, last)]

    tables = tables_of(conductivity, vg_alpha, vg_n, capacity)

    def fill_row(xi, source, x):
        for t in range(16):
            at = slice(8 * t, 8 * t + 8)
            kx, ky, kz, a, n, c = lookup(tables, source[x, at, :])
            alpha[xi, at, :] = a
            expo[xi, at, :] = n
            exponent[xi, at, :] = 1.0 - 1.0 / n
            cap[xi, at, :] = STORE * c
            cond_x[xi, at, :] = kx
            cond_y[xi, at, :] = ky
            trans_z[xi, at, :] = upward_faces(kz)
            if t in (0, 15):
                edges[xi, t // 15] = ky

    loop(5, lambda x: fill_row(x, below, x))
    loop(8, lambda x: fill_row(x + 5, own, x))
    loop(5, lambda x: fill_row(x + 13, above, x))
    for copy in copies(0, 4):
        copy.start()

    def faces(xi):
        inside = x_inside(place, xi)
        above_xi = jnp.minimum(xi + 1, EX - 1)
        for c in range(4):
            at = slice(32 * c, 32 * c + 32)
            trans_x[xi, at, :] = inside * harmonic(cond_x[xi, at, :], cond_x[above_xi, at, :])
            up = slice(32 * c + 1, 32 * c + 33)
            trans_y[xi, at, :] = harmonic(cond_y[xi, at, :], cond_y[xi, up, :])

    loop(EX, faces)
    for copy in copies(4, 8):
        copy.start()
    for copy in copies(0, 8):
        copy.wait()


def wetness(level, alpha, expo, exponent):
    power = jnp.exp(expo * jnp.log(alpha * -level))
    return power, -jnp.log(1.0 + power)


def retention(level, alpha, expo, exponent):
    log_scaled = expo * jnp.log(alpha * -level)
    power = jnp.exp(log_scaled)
    total = 1.0 + power
    inverse = 1.0 / total
    log_inverse = -jnp.log(total)
    root = jnp.exp(0.5 * exponent * log_inverse)
    saturation = root * root
    rest = power * inverse
    z = 1.0 / (1.0 + 2.0 * power)
    zz = z * z
    series = 1.0 / 15.0
    for k in (13.0, 11.0, 9.0, 7.0, 5.0, 3.0, 1.0):
        series = series * zz + 1.0 / k
    log_rest = jnp.where(power >= 1.0, -2.0 * z * series, log_scaled + log_inverse)
    e = exponent * log_rest
    rest_power = jnp.exp(e)
    taylor = 1.0 + e * (1.0 / 8.0)
    for k in (7.0, 6.0, 5.0, 4.0, 3.0, 2.0):
        taylor = 1.0 + (e * (1.0 / k)) * taylor
    inner = jnp.where(e > -0.35, -e * taylor, 1.0 - rest_power)
    relperm = root * inner * inner
    rate = (expo - 1.0) / -level
    d_sat = saturation * rest * rate
    d_rel = root * inner * rate * (0.5 * inner * rest + 2.0 * inverse * rest_power)
    return saturation, relperm, d_sat, d_rel


def split(a, factor):
    c = a * factor
    high = c - (c - a)
    return high, a - high


def two_sum(a, b):
    s = a + b
    t = s - a
    return s, (a - (s - t)) + (b - t)


def df_add(a, b):
    s, e = two_sum(a[0], b[0])
    e = e + (a[1] + b[1])
    t = s + e
    return t, e - (t - s)


def df_mul(a, b):
    ah, al = split(a[0], 4097.0)
    bh, bl = split(b[0], 4097.0)
    p = a[0] * b[0]
    e = ((ah * bh - p) + ah * bl + al * bh) + al * bl
    e = e + (a[0] * b[1] + a[1] * b[0])
    t = p + e
    return t, e - (t - p)


def df_neg(a):
    return -a[0], -a[1]


def df_div(a, b):
    q = a[0] / b[0]
    zero = jnp.zeros_like(q)
    r = df_add(a, df_neg(df_mul((q, zero), b)))
    q2 = r[0] / b[0]
    r = df_add(r, df_neg(df_mul((q2, zero), b)))
    q3 = r[0] / b[0]
    s, e = two_sum(q, q2)
    return two_sum(s, e + q3)


def main_kernel(
    source, place, conductivity, vg_alpha, vg_n, capacity,
    recv, y_low, y_high, edges, in_a, in_n, in_m, in_c, in_x, in_y, in_z, kept, sums,
    alpha, expo, exponent, cap, trans_x, trans_y, trans_z, sems, ordered, head, old, rel, d_rel, own_c, cxp, cxm, cyp, cym, czp, czm, k0, k1, k2, k3, k4,
    side_x, side_y,
):
    sub = iota((8, 128), 0)
    lane = iota((8, 128), 1)
    refs = (
        (in_a, alpha), (in_n, expo), (in_m, exponent), (in_c, cap),
        (in_x, trans_x), (in_y, trans_y), (in_z, trans_z),
    )
    copies = [
        pltpu.make_async_copy(a, b.at[:, 16:144] if b is trans_y else b.at[:, 8:136], sems.at[k])
        for k, (a, b) in enumerate(refs)
    ]
    for copy in copies:
        copy.start()

    def layer(z):
        def tile(k, t):
            return recv[pl.ds(pl.multiple_of(source[k, z] * PIECE + 8 * t, 8), 8), :]

        def put(t, value):
            ordered[pl.ds(pl.multiple_of(z * PIECE + 8 * t, 8), 8), :] = value

        put(0, tile(0, 0))
        put(1, tile(0, 1))
        put(2, jnp.where(sub >= 3, tile(1, 2), tile(2, 2)))
        put(3, jnp.where(sub < 5, tile(2, 3), tile(1, 3)))
        sides = jnp.where(lane < 64, tile(3, 4), tile(4, 4))
        corners = jnp.where(
            lane < 64,
            jnp.where(lane < 32, tile(5, 4), tile(6, 4)),
            jnp.where(lane < 96, tile(7, 4), tile(8, 4)),
        )
        put(
            4,
            jnp.where(
                sub < 2, sides, jnp.where(sub == 3, tile(2, 4), jnp.where(sub == 4, tile(1, 4), corners))
            ),
        )

    def two_layers(i):
        layer(2 * i)
        layer(2 * i + 1)

    loop(64, two_layers)

    def plane(r):
        return ordered[pl.ds(r, 128, stride=PIECE), :].T

    for xi, r in enumerate([19, 20, 21, 22, 23] + list(range(8)) + [16, 17, 18, 27, 28]):
        head[xi, 16:144, :] = plane(r)
    for xi, r in enumerate([36, 29, 30, 31] + list(range(8, 16)) + [24, 25, 26, 35]):
        old[xi + 1, 16:144, :] = plane(r)
    for field, (y_row, corner_row) in ((head, (32, 34)), (old, (33, 37))):
        sides = plane(y_row)
        for x in range(8):
            field[5 + x, 8:16, :] = sides[8 * x : 8 * x + 8]
            field[5 + x, 144:152, :] = sides[64 + 8 * x : 72 + 8 * x]
        corners = plane(corner_row)
        for k in range(4):
            field[13 + k, 8:16, :] = corners[8 * k : 8 * k + 8]
            field[1 + k, 8:16, :] = corners[32 + 8 * k : 40 + 8 * k]
            field[13 + k, 144:152, :] = corners[64 + 8 * k : 72 + 8 * k]
            field[1 + k, 144:152, :] = corners[96 + 8 * k : 104 + 8 * k]
    for xi in (0, 17):
        head[xi, 8:16, :] = jnp.full((8, 128), -1.0, jnp.float32)
        head[xi, 144:152, :] = jnp.full((8, 128), -1.0, jnp.float32)

    def curves(xi):
        for c in range(CHUNKS):
            at = slice(CHUNK * c, CHUNK * (c + 1))
            to = slice(8 + CHUNK * c, 8 + CHUNK * (c + 1))
            sat_v, rel_v, dsat_v, drel_v = retention(
                head[xi, to, :], alpha[xi, at, :], expo[xi, at, :], exponent[xi, at, :]
            )
            k0[xi, to, :] = sat_v
            rel[xi, to, :] = rel_v
            d_rel[xi, to, :] = drel_v
            own_c[xi, to, :] = cap[xi, at, :] * dsat_v

    tables = tables_of(conductivity, vg_alpha, vg_n, capacity)

    def side_rows(xi):
        for source_ids, at in ((y_low, slice(0, 8)), (y_high, slice(136, 144))):
            to = slice(at.start + 8, at.stop + 8)
            kx, ky, kz, a, n, c = lookup(tables, source_ids[xi])
            alpha[xi, at, :] = a
            expo[xi, at, :] = n
            exponent[xi, at, :] = 1.0 - 1.0 / n
            cap[xi, at, :] = STORE * c
            trans_z[xi, at, :] = upward_faces(kz)
            side_x[xi, at.start // 17 : at.start // 17 + 8, :] = kx
            side_y[xi, to, :] = ky
        side_y[xi, 16:24, :] = edges[xi, 0]
        side_y[xi, 136:144, :] = edges[xi, 1]

    loop(EX, side_rows)
    for copy in copies:
        copy.wait()

    def side_faces(xi):
        pair = x_inside(place, xi) * harmonic(side_x[xi], side_x[jnp.minimum(xi + 1, EX - 1)])
        trans_x[xi, 0:8, :] = pair[0:8]
        trans_x[xi, 136:144, :] = pair[8:16]
        for first, last in ((8, 16), (136, 152)):
            here = slice(first, last)
            value = harmonic(side_y[xi, here, :], side_y[xi, first + 1 : last + 1, :])
            trans_y[xi, here, :] = jnp.where(y_inside(place, value.shape, first - 8), value, 0.0)

    loop(EX, side_faces)
    loop(EX, curves)

    def face(t, h_a, h_b, r_a, r_b, d_a, d_b, rise):
        potential = h_b - h_a
        if rise:
            potential = potential + rise
        along = t * (0.5 * (r_a + r_b))
        slope = (0.5 * t) * potential
        return along, slope, along * potential, slope * (d_a + d_b)

    def coefficients(i):
        xi = i + 1
        for c in range(CHUNKS):
            at = slice(CHUNK * c, CHUNK * (c + 1))
            to = slice(8 + CHUNK * c, 8 + CHUNK * (c + 1))
            up = slice(9 + CHUNK * c, 9 + CHUNK * (c + 1))
            down = slice(7 + CHUNK * c, 7 + CHUNK * (c + 1))
            _, log_old = wetness(old[xi, to, :], alpha[xi, at, :], expo[xi, at, :], exponent[xi, at, :])
            old_sat = jnp.exp(exponent[xi, at, :] * log_old)
            start = cap[xi, at, :] * (old_sat - k0[xi, to, :])
            h, r, d = head[xi, to, :], rel[xi, to, :], d_rel[xi, to, :]
            centre = own_c[xi, to, :]
            around = (
                (
                    trans_x[xi, at, :], trans_x[xi - 1, at, :], 0.0, cxp, cxm,
                    [f[xi + 1, to, :] for f in (head, rel, d_rel)],
                    [f[xi - 1, to, :] for f in (head, rel, d_rel)],
                ),
                (
                    trans_y[xi, to, :], trans_y[xi, down, :], 0.0, cyp, cym,
                    [f[xi, up, :] for f in (head, rel, d_rel)],
                    [f[xi, down, :] for f in (head, rel, d_rel)],
                ),
                (
                    trans_z[xi, at, :], pltpu.roll(trans_z[xi, at, :], 1, 1), 1.0, czp, czm,
                    [pltpu.roll(f, 127, 1) for f in (h, r, d)],
                    [pltpu.roll(f, 1, 1) for f in (h, r, d)],
                ),
            )
            for t_p, t_m, rise, c_p, c_m, (h_p, r_p, d_p), (h_m, r_m, d_m) in around:
                along, slope, flux, both = face(t_p, h, h_p, r, r_p, d, d_p, rise)
                along_m, slope_m, flux_m, both_m = face(t_m, h_m, h, r_m, r, d_m, d, rise)
                c_p[xi, to, :] = along + slope * d_p
                c_m[xi, to, :] = along_m - slope_m * d_m
                start = start + (flux - flux_m)
                centre = centre - (both - both_m)
            own_c[xi, to, :] = centre
            k0[xi, to, :] = start

    loop(16, coefficients)

    vectors = (k0, k1, k2, k3, k4)
    for step in range(4):
        v_ref, w_ref = vectors[step], vectors[step + 1]

        def apply(i):
            xi = i + 2 + step
            for c in range(CHUNKS):
                to = slice(8 + CHUNK * c, 8 + CHUNK * (c + 1))
                up = slice(9 + CHUNK * c, 9 + CHUNK * (c + 1))
                down = slice(7 + CHUNK * c, 7 + CHUNK * (c + 1))
                v = v_ref[xi, to, :]
                w = own_c[xi, to, :] * v
                w = w + cxp[xi, to, :] * (v - v_ref[xi + 1, to, :])
                w = w + cxm[xi, to, :] * (v - v_ref[xi - 1, to, :])
                w = w + cyp[xi, to, :] * (v - v_ref[xi, up, :])
                w = w + cym[xi, to, :] * (v - v_ref[xi, down, :])
                w = w + czp[xi, to, :] * (v - pltpu.roll(v, 127, 1))
                w = w + czm[xi, to, :] * (v - pltpu.roll(v, 1, 1))
                w_ref[xi, to, :] = w

        loop(14 - 2 * step, apply)

    keeps = [
        pltpu.make_async_copy(vectors[k].at[5:13, 16:144, :], kept.at[k], sems.at[7 + k]) for k in range(4)
    ]
    for copy in keeps:
        copy.start()

    def largest(i, tops):
        xi = 5 + i
        for c in range(16):
            at = slice(16 + 8 * c, 24 + 8 * c)
            tops = [jnp.maximum(top, jnp.abs(v[xi, at, :])) for top, v in zip(tops, vectors)]
        return tops

    tops = lax.fori_loop(0, 8, largest, [jnp.zeros((8, 128), jnp.float32) for _ in range(5)])
    scales, inverses = [], []
    for top in tops:
        top = jnp.broadcast_to(jnp.max(top, keepdims=True), (8, 128))
        scale = jnp.full((8, 128), 2.0**96, jnp.float32)
        inverse = jnp.full((8, 128), 2.0**-96, jnp.float32)
        for j in range(-5, 7):
            over = top >= 2.0 ** (16 * j - 8)
            scale = jnp.where(over, 2.0 ** (-16 * j), scale)
            inverse = jnp.where(over, 2.0 ** (16 * j), inverse)
        scales.append(scale)
        inverses.append(inverse)

    def products(i, totals):
        leading, rest = totals
        xi = 5 + i // 8
        first = 16 + 16 * (i % 8)
        for k in range(2):
            at = pl.ds(pl.multiple_of(first + 8 * k, 8), 8)
            values = [v[xi, at, :] * scale for v, scale in zip(vectors, scales)]
            halves = [split(value, 65537.0) for value in values]
            leading, rest = list(leading), list(rest)
            for e, (p, q) in enumerate(PAIRS):
                leading[e] = leading[e] + halves[p][0] * halves[q][0]
                rest[e] = rest[e] + (halves[p][0] * halves[q][1] + halves[p][1] * values[q])
        return leading, rest

    zeros = [jnp.zeros((8, 128), jnp.float32) for _ in PAIRS]
    leading, rest = lax.fori_loop(0, 64, products, (zeros, list(zeros)))
    groups = []
    for g in range(2):
        high = jnp.zeros((8, 128), jnp.float32)
        low = jnp.zeros((8, 128), jnp.float32)
        for e in range(8 * g, min(8 * g + 8, len(PAIRS))):
            pair = two_sum(leading[e], rest[e])
            for shift in (4, 2, 1):
                pair = df_add(pair, (pltpu.roll(pair[0], shift, 0), pltpu.roll(pair[1], shift, 0)))
            high = jnp.where(sub == e - 8 * g, pair[0], high)
            low = jnp.where(sub == e - 8 * g, pair[1], low)
        pair = (high, low)
        for shift in (64, 32, 16, 8, 4, 2, 1):
            pair = df_add(pair, (pltpu.roll(pair[0], shift, 1), pltpu.roll(pair[1], shift, 1)))
        groups.append(pair)
    line = jnp.zeros((8, 128), jnp.float32)
    for e in range(len(PAIRS)):
        pair = groups[e // 8]
        for half in range(2):
            line = jnp.where(lane == 16 * half + e, pair[half][e % 8 : e % 8 + 1, :], line)
    for k in range(5):
        line = jnp.where(lane == 32 + k, inverses[k], line)
        line = jnp.where(lane == 40 + k, scales[k], line)
    for t in range(16):
        sums[8 * t : 8 * t + 8, :] = line

    for copy in keeps:
        copy.wait()


def turn_back_kernel(kept, out):
    for k in range(4):
        for x in range(8):
            out[k, pl.ds(x, 128, stride=8), :] = kept[k, x].T


def finish_kernel(recv, vectors, out):
    data = recv[...]
    lane = iota((128, 128), 1)
    smallest = jnp.min(data, axis=0, keepdims=True)
    factor = data * jnp.broadcast_to(pltpu.roll(jnp.broadcast_to(smallest, (8, 128)), 120, 1)[0:1], (128, 128))
    left = jnp.zeros((128, 128), jnp.float32)
    right = jnp.zeros((128, 128), jnp.float32)
    for k in range(5):
        column = jnp.broadcast_to(factor[:, 32 + k : 33 + k], (128, 128))
        for e, (p, q) in enumerate(PAIRS):
            if p == k:
                left = jnp.where(lane % 16 == e, column, left)
            if q == k:
                right = jnp.where(lane % 16 == e, column, right)
    scaled = data * left * right
    low = pltpu.roll(scaled, 112, 1)
    pair = (scaled[0:8], low[0:8])
    for t in range(1, 16):
        pair = df_add(pair, (scaled[8 * t : 8 * t + 8], low[8 * t : 8 * t + 8]))
    for shift in (4, 2, 1):
        pair = df_add(pair, (pltpu.roll(pair[0], shift, 0), pltpu.roll(pair[1], shift, 0)))
    entry = {}
    for e, (p, q) in enumerate(PAIRS):
        entry[p, q] = tuple(jnp.broadcast_to(half[:, e : e + 1], (8, 128)) for half in pair)

    def scale_of(k):
        return jnp.broadcast_to(smallest[:, k : k + 1], (8, 128))

    rows = {(i, j): entry[i + 1, j + 1] for i in range(4) for j in range(i, 4)}
    right_side = [entry[0, j + 1] for j in range(4)]
    for k in range(4):
        for i in range(k + 1, 4):
            ratio = df_neg(df_div(rows[k, i], rows[k, k]))
            for j in range(i, 4):
                rows[i, j] = df_add(rows[i, j], df_mul(ratio, rows[k, j]))
            right_side[i] = df_add(right_side[i], df_mul(ratio, right_side[k]))
    coeffs = [None] * 4
    for k in reversed(range(4)):
        running = right_side[k]
        for j in range(k + 1, 4):
            running = df_add(running, df_neg(df_mul(rows[k, j], coeffs[j])))
        coeffs[k] = df_div(running, rows[k, k])
    inverse_first = jnp.max(jnp.where(lane == 32, data, 0.0), axis=0, keepdims=True)
    inverse_first = jnp.broadcast_to(jnp.max(inverse_first, axis=1, keepdims=True), (8, 128))
    weights = [(coeffs[k][0] * scale_of(41 + k)) * inverse_first for k in range(4)]

    def rows_of(t):
        for k in range(4):
            at = pl.ds(pl.multiple_of(32 * t + 8 * k, 8), 8)
            total = weights[0] * vectors[0, at, :]
            for j in range(1, 4):
                total = total + weights[j] * vectors[j, at, :]
            out[at, :] = total

    loop(32, rows_of)


def call(kernel, out_shape, in_specs, out_specs, scratch, mib, cost):
    return pl.pallas_call(
        kernel,
        out_shape=out_shape,
        in_specs=in_specs,
        out_specs=out_specs,
        scratch_shapes=scratch,
        compiler_params=params(mib),
        cost_estimate=pl.CostEstimate(flops=cost[0], bytes_accessed=cost[1], transcendentals=0),
    )


def body(held_head, held_head_old, material_ids, block_map, conductivity, vg_alpha, vg_n, capacity):
    count_x, count_y = lax.axis_size("gx"), lax.axis_size("gy")
    devices = count_x * count_y
    at_x, at_y = lax.axis_index("gx"), lax.axis_index("gy")
    own_index = at_x * count_y + at_y
    numbers = jnp.arange(devices, dtype=jnp.int32)
    own_row = block_map[own_index]
    slot_of = jnp.sum(jnp.where(own_row[None, :] == numbers[:, None], numbers[None, :], 0), axis=1)
    scratch = lambda *shape: pltpu.VMEM(shape, jnp.float32)

    up_x = [(i, i + 1) for i in range(count_x - 1)]
    down_x = [(i + 1, i) for i in range(count_x - 1)]
    up_y = [(i, i + 1) for i in range(count_y - 1)]
    down_y = [(i + 1, i) for i in range(count_y - 1)]
    ids, first, last = call(
        turn_ids_kernel, [f32(8, 128, 128)] + [f32(DEPTH, 128, 128)] * 2, [VMEM], [VMEM] * 3, [], 8, (10**6, 10**6)
    )(material_ids.reshape(1024, 128))
    slot_of, first, last = lax.optimization_barrier((slot_of, first, last))
    below = lax.ppermute(last, "gx", up_x)
    above = lax.ppermute(first, "gx", down_x)

    packed = call(
        pack_kernel,
        f32(devices * PIECE, 128),
        [SMEM, VMEM, VMEM],
        HBM,
        [scratch(devices * PIECE, 128), scratch(PY, 128), pltpu.SemaphoreType.DMA],
        63,
        (10**6, 4 * 10**6),
    )(slot_of, held_head, held_head_old)
    packed, below, above = lax.optimization_barrier((packed, below, above))
    arrived = lax.all_to_all(packed, AXES, split_axis=0, concat_axis=0, tiled=True)

    offsets = (0, -count_y, count_y, -1, 1, count_y - 1, -count_y - 1, count_y + 1, -count_y + 1)
    bricks = own_index + jnp.array(offsets, jnp.int32)
    source = jnp.sum(
        jnp.where(block_map[None] == bricks[:, None, None], numbers[None, :, None], 0), axis=1
    )
    place = jnp.stack([at_x, at_y, jnp.int32(count_x), jnp.int32(count_y)])
    first, last = call(
        edge_ids_kernel, [f32(EX, 8, 128)] * 2, [VMEM] * 3, [VMEM] * 2, [], 8, (10**5, 10**6)
    )(below, ids, above)
    y_low = lax.ppermute(last, "gy", up_y)
    y_high = lax.ppermute(first, "gy", down_y)
    *fields, edges = call(
        properties_kernel,
        [f32(EX, 128, 128)] * 7 + [f32(EX, 2, 8, 128)],
        [SMEM] * 5 + [VMEM] * 3,
        [HBM] * 8,
        [scratch(EX, 128, 128)] * 7 + [scratch(EX, 2, 8, 128), scratch(EX, 128, 128), scratch(EX, 136, 128)]
        + [pltpu.SemaphoreType.DMA((8,))],
        63,
        (40 * 10**6, 12 * 10**6),
    )(place, conductivity, vg_alpha, vg_n, capacity, below, ids, above)

    kept, sums = call(
        main_kernel,
        [f32(4, 8, 128, 128), f32(devices, 128)],
        [SMEM] * 6 + [VMEM] * 4 + [HBM] * 7,
        [HBM, VMEM],
        [scratch(EX, EY, 128)] * 5 + [scratch(EX, PY, 128), scratch(EX, EY, 128)]
        + [pltpu.SemaphoreType.DMA((11,)), scratch(devices * PIECE, 128)] + [scratch(EX, PY, 128)] * 16
        + [scratch(EX, 16, 128), scratch(EX, PY, 128)],
        63,
        (200 * 10**6, 16 * 10**6),
    )(source, place, conductivity, vg_alpha, vg_n, capacity, arrived, y_low, y_high, edges, *fields)
    gathered = lax.all_to_all(sums.reshape(devices, 1, 128), AXES, split_axis=0, concat_axis=0, tiled=True)
    turned = call(turn_back_kernel, f32(4, 1024, 128), [VMEM], VMEM, [], 8, (10**6, 4 * 10**6))(kept)
    update = call(finish_kernel, f32(1024, 128), [VMEM] * 2, VMEM, [], 8, (10**6, 3 * 10**6))(
        gathered.reshape(devices, 128), turned
    )
    return update.reshape(128, 8, 128)


def solution(mesh):
    return jax.shard_map(
        body,
        mesh=mesh,
        in_specs=(
            P(("gx", "gy"), None, None),
            P(("gx", "gy"), None, None),
            P(None, "gx", "gy"),
            P(),
            P(),
            P(),
            P(),
            P(),
        ),
        out_specs=P(None, "gx", "gy"),
        check_vma=False,
    )
```

```python
import jax
import jax.numpy as jnp
from jax import lax
from jax.experimental import pallas as pl
from jax.experimental.pallas import tpu as pltpu
from jax.sharding import PartitionSpec as P

MATERIALS = 16
STORE = 4.0
AXES = ("gx", "gy")

PIECE = 40
DEPTH = 5
EX = 8 + 2 * DEPTH
EY = 144
PY = 160
CHUNK = 24
CHUNKS = EY // CHUNK
PAIRS = [(i, j) for j in range(1, 5) for i in range(0, j + 1)]


def f32(*shape):
    return jax.ShapeDtypeStruct(shape, jnp.float32)


def params(mib):
    return pltpu.CompilerParams(vmem_limit_bytes=mib << 20)


VMEM = pl.BlockSpec(memory_space=pltpu.VMEM)
SMEM = pl.BlockSpec(memory_space=pltpu.SMEM)
HBM = pl.BlockSpec(memory_space=pltpu.HBM)


def iota(shape, axis):
    return lax.broadcasted_iota(jnp.int32, shape, axis)


def loop(count, body, unroll=1):
    def several(i, carry):
        for k in range(unroll):
            body(unroll * i + k)
        return carry

    lax.fori_loop(0, count // unroll, several, 0)


def pack_kernel(slot_of, head, old, packed, out, edge, sem):
    sub = iota((8, 128), 0)

    def brick(b):
        own = slot_of[0, b]
        below = slot_of[0, jnp.maximum(b - 8, 0)]
        above = slot_of[0, jnp.minimum(b + 8, 127)]
        head_below, head_above = head[below], head[above]
        old_below, old_above = old[below], old[above]

        def put(tile, value):
            out[pl.ds(pl.multiple_of(b * PIECE + 8 * tile, 8), 8), :] = value

        put(0, head[own])
        put(1, old[own])
        put(2, jnp.where(sub >= 3, head_below, head_above))
        put(3, jnp.where(sub < 3, old_above, jnp.where(sub < 5, head_above, old_below)))
        put(4, jnp.where(sub == 3, old_above, old_below))

    loop(128, brick, 8)
    lane = iota((128, 128), 1)
    low = lane % 16 < 8
    edge[0:16, :] = jnp.full((16, 128), -1.0, jnp.float32)
    edge[144:160, :] = jnp.full((16, 128), -1.0, jnp.float32)
    for field, (y_row, corner_row) in enumerate(((32, 34), (33, 37))):
        columns = jnp.zeros((128, 128), jnp.float32)
        for x in range(8):
            rows = out[pl.ds(8 * field + x, 128, stride=PIECE), :]
            columns = jnp.where(lane // 16 == x, pltpu.roll(rows, 16 * x + 8, 1), columns)
        edge[16:144, :] = columns
        out[pl.ds(y_row, 128, stride=PIECE), :] = jnp.where(low, edge[15:143, :], edge[17:145, :])
        out[pl.ds(corner_row, 128, stride=PIECE), :] = jnp.where(
            lane < 64,
            jnp.where(low, edge[23:151, :], edge[25:153, :]),
            jnp.where(low, edge[7:135, :], edge[9:137, :]),
        )
    copy = pltpu.make_async_copy(out, packed, sem)
    copy.start()
    copy.wait()


def turn_ids_kernel(block_map, ids, slot_of, out, first, last):
    row = jnp.broadcast_to(block_map[pl.ds(lax.axis_index(AXES), 1), :], (128, 128))
    match = row == iota((128, 128), 0)
    slot = jnp.sum(jnp.where(match, iota((128, 128), 1), 0).astype(jnp.float32), axis=1, keepdims=True)
    slot_of[...] = jnp.broadcast_to(slot, (128, 128)).T[0:8].astype(jnp.int32)
    for x in range(8):
        plane = ids[pl.ds(x, 128, stride=8), :].astype(jnp.float32).T
        out[x] = plane
        if x < DEPTH:
            first[x] = plane
        if x >= 8 - DEPTH:
            last[x - 8 + DEPTH] = plane


def edge_ids_kernel(below, own, above, first, last):
    for k, part in ((0, below), (5, own), (13, above)):
        for x in range(part.shape[0]):
            first[k + x] = part[x, 0:8, :]
            last[k + x] = part[x, 120:128, :]


def tables_of(conductivity, vg_alpha, vg_n, capacity):
    lane = iota((8, 128), 1)
    reads = [
        lambda m: conductivity[0, m], lambda m: conductivity[1, m], lambda m: conductivity[2, m],
        lambda m: vg_alpha[m], lambda m: vg_n[m], lambda m: capacity[m],
    ]
    tables = []
    for read in reads:
        table = jnp.zeros((8, 128), jnp.float32)
        for m in range(MATERIALS):
            table = jnp.where(lane == m, read(m), table)
        tables.append(table)
    return tables


def lookup(tables, ids):
    index = ids.astype(jnp.int32)
    return [jnp.take_along_axis(table, index, axis=1) for table in tables]


def half_mean(a, b):
    return a * b / (a + b)


def upward_faces(kz):
    return jnp.where(iota(kz.shape, 1) < 127, half_mean(kz, pltpu.roll(kz, 127, 1)), 0.0)


def x_inside(xi):
    x = lax.axis_index("gx") * 8 - DEPTH + xi
    return jnp.where((x >= 0) & (x + 1 < lax.axis_size("gx") * 8), 1.0, 0.0)


def y_inside(shape, first):
    y = lax.axis_index("gy") * 128 - 8 + first + iota(shape, 0)
    return (y >= 0) & (y + 1 < lax.axis_size("gy") * 128)


def properties_kernel(
    conductivity, vg_alpha, vg_n, capacity, below, own, above,
    out_a, out_n, out_m, out_c, out_x, out_y, out_z, out_e,
    alpha, expo, exponent, cap, trans_x, trans_y, trans_z, edges, cond_x, cond_y, sems,
):
    def copies(first, last):
        made = (alpha, expo, exponent, cap, trans_x, trans_y, trans_z, edges)
        outs = (out_a, out_n, out_m, out_c, out_x, out_y, out_z, out_e)
        return [pltpu.make_async_copy(made[k], outs[k], sems.at[k]) for k in range(first, last)]

    tables = tables_of(conductivity, vg_alpha, vg_n, capacity)

    def fill_row(xi, source, x):
        for t in range(16):
            at = slice(8 * t, 8 * t + 8)
            kx, ky, kz, a, n, c = lookup(tables, source[x, at, :])
            alpha[xi, at, :] = a
            expo[xi, at, :] = n
            exponent[xi, at, :] = 1.0 - 1.0 / n
            cap[xi, at, :] = STORE * c
            cond_x[xi, at, :] = kx
            cond_y[xi, at, :] = ky
            trans_z[xi, at, :] = upward_faces(kz)
            if t in (0, 15):
                edges[xi, t // 15] = ky

    loop(5, lambda x: fill_row(x, below, x))
    loop(8, lambda x: fill_row(x + 5, own, x))
    loop(5, lambda x: fill_row(x + 13, above, x))
    for copy in copies(0, 4):
        copy.start()

    def faces(xi):
        inside = x_inside(xi)
        above_xi = jnp.minimum(xi + 1, EX - 1)
        for c in range(4):
            at = slice(32 * c, 32 * c + 32)
            trans_x[xi, at, :] = inside * half_mean(cond_x[xi, at, :], cond_x[above_xi, at, :])
            up = slice(32 * c + 1, 32 * c + 33)
            trans_y[xi, at, :] = half_mean(cond_y[xi, at, :], cond_y[xi, up, :])

    loop(EX, faces)
    for copy in copies(4, 8):
        copy.start()
    for copy in copies(0, 8):
        copy.wait()


def wetness(level, alpha, expo, exponent):
    power = jnp.exp(expo * jnp.log(alpha * -level))
    return power, -jnp.log(1.0 + power)


def retention(level, alpha, expo, exponent):
    log_scaled = expo * jnp.log(alpha * -level)
    power = jnp.exp(log_scaled)
    total = 1.0 + power
    inverse = 1.0 / total
    log_inverse = -jnp.log(total)
    root = jnp.exp(0.5 * exponent * log_inverse)
    saturation = root * root
    rest = power * inverse
    z = 1.0 / (1.0 + 2.0 * power)
    zz = z * z
    series = 1.0 / 15.0
    for k in (13.0, 11.0, 9.0, 7.0, 5.0, 3.0, 1.0):
        series = series * zz + 1.0 / k
    log_rest = jnp.where(power >= 1.0, -2.0 * z * series, log_scaled + log_inverse)
    e = exponent * log_rest
    rest_power = jnp.exp(e)
    taylor = 1.0 + e * (1.0 / 8.0)
    for k in (7.0, 6.0, 5.0, 4.0, 3.0, 2.0):
        taylor = 1.0 + (e * (1.0 / k)) * taylor
    inner = jnp.where(e > -0.35, -e * taylor, 1.0 - rest_power)
    relperm = root * inner * inner
    rate = (expo - 1.0) / -level
    d_sat = saturation * rest * rate
    d_rel = root * inner * rate * (0.5 * inner * rest + 2.0 * inverse * rest_power)
    return saturation, relperm, d_sat, d_rel


def split(a, factor):
    c = a * factor
    high = c - (c - a)
    return high, a - high


def two_sum(a, b):
    s = a + b
    t = s - a
    return s, (a - (s - t)) + (b - t)


def df_add(a, b):
    s, e = two_sum(a[0], b[0])
    e = e + (a[1] + b[1])
    t = s + e
    return t, e - (t - s)


def df_mul(a, b):
    ah, al = split(a[0], 4097.0)
    bh, bl = split(b[0], 4097.0)
    p = a[0] * b[0]
    e = ((ah * bh - p) + ah * bl + al * bh) + al * bl
    e = e + (a[0] * b[1] + a[1] * b[0])
    t = p + e
    return t, e - (t - p)


def df_neg(a):
    return -a[0], -a[1]


def df_div(a, b):
    q = a[0] / b[0]
    zero = jnp.zeros_like(q)
    r = df_add(a, df_neg(df_mul((q, zero), b)))
    q2 = r[0] / b[0]
    r = df_add(r, df_neg(df_mul((q2, zero), b)))
    q3 = r[0] / b[0]
    s, e = two_sum(q, q2)
    return two_sum(s, e + q3)


def main_kernel(
    source, conductivity, vg_alpha, vg_n, capacity,
    recv, y_low, y_high, edges, in_a, in_n, in_m, in_c, in_x, in_y, in_z, kept, sums,
    alpha, expo, exponent, cap, trans_x, trans_y, trans_z, sems, ordered, head, old, rel, d_rel, own_c, cxp, cxm, cyp, cym, czp, czm, k0, k1, k2, k3, k4,
    side_x, side_y,
):
    sub = iota((8, 128), 0)
    lane = iota((8, 128), 1)
    refs = (
        (in_a, alpha), (in_n, expo), (in_m, exponent), (in_c, cap),
        (in_x, trans_x), (in_y, trans_y), (in_z, trans_z),
    )
    copies = [
        pltpu.make_async_copy(a, b.at[:, 16:144] if b is trans_y else b.at[:, 8:136], sems.at[k])
        for k, (a, b) in enumerate(refs)
    ]
    for copy in copies:
        copy.start()

    low = lane % 16 < 8

    def layer(z):
        def tile(k, t):
            return recv[pl.ds(pl.multiple_of(source[k, z] * PIECE + 8 * t, 8), 8), :]

        def put(t, value):
            ordered[pl.ds(pl.multiple_of(z * PIECE + 8 * t, 8), 8), :] = value

        put(0, tile(0, 0))
        put(1, tile(0, 1))
        put(2, jnp.where(sub >= 3, tile(1, 2), tile(2, 2)))
        put(3, jnp.where(sub < 5, tile(2, 3), tile(1, 3)))
        sides = jnp.where(low, tile(3, 4), tile(4, 4))
        corners = jnp.where(
            lane < 64, jnp.where(low, tile(5, 4), tile(7, 4)), jnp.where(low, tile(6, 4), tile(8, 4))
        )
        put(
            4,
            jnp.where(
                sub < 2, sides, jnp.where(sub == 3, tile(2, 4), jnp.where(sub == 4, tile(1, 4), corners))
            ),
        )

    loop(128, layer, 4)

    def plane(r):
        return ordered[pl.ds(r, 128, stride=PIECE), :].T

    for xi, r in enumerate([19, 20, 21, 22, 23] + list(range(8)) + [16, 17, 18, 27, 28]):
        head[xi, 16:144, :] = plane(r)
    for xi, r in enumerate([36, 29, 30, 31] + list(range(8, 16)) + [24, 25, 26, 35]):
        old[xi + 1, 16:144, :] = plane(r)
    for field, (y_row, corner_row) in ((head, (32, 34)), (old, (33, 37))):
        sides = plane(y_row)
        for x in range(8):
            field[5 + x, 8:16, :] = sides[16 * x : 16 * x + 8]
            field[5 + x, 144:152, :] = sides[16 * x + 8 : 16 * x + 16]
        corners = plane(corner_row)
        for x in range(8):
            xi = 13 + x if x < 4 else x - 3
            field[xi, 8:16, :] = corners[16 * x : 16 * x + 8]
            field[xi, 144:152, :] = corners[16 * x + 8 : 16 * x + 16]
    for xi in (0, 17):
        head[xi, 8:16, :] = jnp.full((8, 128), -1.0, jnp.float32)
        head[xi, 144:152, :] = jnp.full((8, 128), -1.0, jnp.float32)

    def curves(xi):
        for c in range(CHUNKS):
            at = slice(CHUNK * c, CHUNK * (c + 1))
            to = slice(8 + CHUNK * c, 8 + CHUNK * (c + 1))
            sat_v, rel_v, dsat_v, drel_v = retention(
                head[xi, to, :], alpha[xi, at, :], expo[xi, at, :], exponent[xi, at, :]
            )
            k0[xi, to, :] = sat_v
            rel[xi, to, :] = rel_v
            d_rel[xi, to, :] = drel_v
            own_c[xi, to, :] = cap[xi, at, :] * dsat_v

    tables = tables_of(conductivity, vg_alpha, vg_n, capacity)

    def side_rows(xi):
        for source_ids, at in ((y_low, slice(0, 8)), (y_high, slice(136, 144))):
            to = slice(at.start + 8, at.stop + 8)
            kx, ky, kz, a, n, c = lookup(tables, source_ids[xi])
            alpha[xi, at, :] = a
            expo[xi, at, :] = n
            exponent[xi, at, :] = 1.0 - 1.0 / n
            cap[xi, at, :] = STORE * c
            trans_z[xi, at, :] = upward_faces(kz)
            side_x[xi, at.start // 17 : at.start // 17 + 8, :] = kx
            side_y[xi, to, :] = ky
        side_y[xi, 16:24, :] = edges[xi, 0]
        side_y[xi, 136:144, :] = edges[xi, 1]

    loop(EX, side_rows, 3)
    for copy in copies[:4]:
        copy.wait()
    loop(EX, curves, 2)
    for copy in copies[4:]:
        copy.wait()

    def side_faces(xi):
        pair = x_inside(xi) * half_mean(side_x[xi], side_x[jnp.minimum(xi + 1, EX - 1)])
        trans_x[xi, 0:8, :] = pair[0:8]
        trans_x[xi, 136:144, :] = pair[8:16]
        for first, last in ((8, 16), (136, 152)):
            here = slice(first, last)
            value = half_mean(side_y[xi, here, :], side_y[xi, first + 1 : last + 1, :])
            trans_y[xi, here, :] = jnp.where(y_inside(value.shape, first - 8), value, 0.0)

    loop(EX, side_faces, 3)

    def face(half, h_a, h_b, r_a, r_b, d_a, d_b, rise):
        potential = h_b - h_a
        if rise:
            potential = potential + rise
        along = half * (r_a + r_b)
        slope = half * potential
        return along + slope * d_b, along - slope * d_a, along * potential, slope * (d_a + d_b)

    def x_faces(xi, to, at, h, r, d):
        c_p, c_m, flux, both = face(
            trans_x[xi, at, :], h, head[xi + 1, to, :], r, rel[xi + 1, to, :], d, d_rel[xi + 1, to, :], 0.0
        )
        cxp[xi, to, :] = c_p
        cxm[xi + 1, to, :] = c_m
        k1[xi, to, :] = flux
        k2[xi, to, :] = both
        return flux, both

    for c in range(CHUNKS):
        at = slice(CHUNK * c, CHUNK * (c + 1))
        to = slice(8 + CHUNK * c, 8 + CHUNK * (c + 1))
        x_faces(0, to, at, head[0, to, :], rel[0, to, :], d_rel[0, to, :])

    def coefficients(i):
        xi = i + 1
        for c in range(CHUNKS):
            at = slice(CHUNK * c, CHUNK * (c + 1))
            to = slice(8 + CHUNK * c, 8 + CHUNK * (c + 1))
            up = slice(9 + CHUNK * c, 9 + CHUNK * (c + 1))
            down = slice(7 + CHUNK * c, 7 + CHUNK * (c + 1))
            _, log_old = wetness(old[xi, to, :], alpha[xi, at, :], expo[xi, at, :], exponent[xi, at, :])
            old_sat = jnp.exp(exponent[xi, at, :] * log_old)
            start = cap[xi, at, :] * (old_sat - k0[xi, to, :])
            h, r, d = head[xi, to, :], rel[xi, to, :], d_rel[xi, to, :]
            flux, both = x_faces(xi, to, at, h, r, d)
            start = start + (flux - k1[xi - 1, to, :])
            centre = own_c[xi, to, :] - (both - k2[xi - 1, to, :])
            c_p, c_m, flux, both = face(
                trans_y[xi, to, :], h, head[xi, up, :], r, rel[xi, up, :], d, d_rel[xi, up, :], 0.0
            )
            cyp[xi, to, :] = c_p
            cym[xi, up, :] = c_m
            k3[xi, to, :] = flux
            k4[xi, to, :] = both
            start = start + (flux - k3[xi, down, :])
            centre = centre - (both - k4[xi, down, :])
            c_p, c_m, flux, both = face(
                trans_z[xi, at, :], h, pltpu.roll(h, 127, 1), r, pltpu.roll(r, 127, 1), d, pltpu.roll(d, 127, 1), 1.0
            )
            czp[xi, to, :] = c_p
            czm[xi, to, :] = pltpu.roll(c_m, 1, 1)
            own_c[xi, to, :] = centre - (both - pltpu.roll(both, 1, 1))
            k0[xi, to, :] = start + (flux - pltpu.roll(flux, 1, 1))

    loop(16, coefficients, 2)

    vectors = (k0, k1, k2, k3, k4)
    for step in range(4):
        v_ref, w_ref = vectors[step], vectors[step + 1]

        def apply(i):
            xi = i + 2 + step
            for c in range(CHUNKS):
                to = slice(8 + CHUNK * c, 8 + CHUNK * (c + 1))
                up = slice(9 + CHUNK * c, 9 + CHUNK * (c + 1))
                down = slice(7 + CHUNK * c, 7 + CHUNK * (c + 1))
                v = v_ref[xi, to, :]
                w = own_c[xi, to, :] * v
                w = w + cxp[xi, to, :] * (v - v_ref[xi + 1, to, :])
                w = w + cxm[xi, to, :] * (v - v_ref[xi - 1, to, :])
                w = w + cyp[xi, to, :] * (v - v_ref[xi, up, :])
                w = w + cym[xi, to, :] * (v - v_ref[xi, down, :])
                w = w + czp[xi, to, :] * (v - pltpu.roll(v, 127, 1))
                w = w + czm[xi, to, :] * (v - pltpu.roll(v, 1, 1))
                w_ref[xi, to, :] = w

        loop(14 - 2 * step, apply, 7 - step)

    keeps = [
        pltpu.make_async_copy(vectors[k].at[5:13, 16:144, :], kept.at[k], sems.at[7 + k]) for k in range(4)
    ]
    for copy in keeps:
        copy.start()

    def largest(i, tops):
        xi = 5 + i
        for c in range(16):
            at = slice(16 + 8 * c, 24 + 8 * c)
            tops = [jnp.maximum(top, jnp.abs(v[xi, at, :])) for top, v in zip(tops, vectors)]
        return tops

    tops = lax.fori_loop(0, 8, largest, [jnp.zeros((8, 128), jnp.float32) for _ in range(5)])
    scales, inverses = [], []
    for top in tops:
        top = jnp.broadcast_to(jnp.max(top, keepdims=True), (8, 128))
        scale = jnp.full((8, 128), 2.0**96, jnp.float32)
        inverse = jnp.full((8, 128), 2.0**-96, jnp.float32)
        for j in range(-5, 7):
            over = top >= 2.0 ** (16 * j - 8)
            scale = jnp.where(over, 2.0 ** (-16 * j), scale)
            inverse = jnp.where(over, 2.0 ** (16 * j), inverse)
        scales.append(scale)
        inverses.append(inverse)

    def products(i, totals):
        leading, rest = totals
        xi = 5 + i // 8
        first = 16 + 16 * (i % 8)
        for k in range(2):
            at = pl.ds(pl.multiple_of(first + 8 * k, 8), 8)
            values = [v[xi, at, :] * scale for v, scale in zip(vectors, scales)]
            halves = [split(value, 65537.0) for value in values]
            leading, rest = list(leading), list(rest)
            for e, (p, q) in enumerate(PAIRS):
                leading[e] = leading[e] + halves[p][0] * halves[q][0]
                rest[e] = rest[e] + (halves[p][0] * halves[q][1] + halves[p][1] * values[q])
        return leading, rest

    zeros = [jnp.zeros((8, 128), jnp.float32) for _ in PAIRS]
    leading, rest = lax.fori_loop(0, 64, products, (zeros, list(zeros)))
    groups = []
    for g in range(2):
        high = jnp.zeros((8, 128), jnp.float32)
        low = jnp.zeros((8, 128), jnp.float32)
        for e in range(8 * g, min(8 * g + 8, len(PAIRS))):
            pair = two_sum(leading[e], rest[e])
            for shift in (4, 2, 1):
                pair = df_add(pair, (pltpu.roll(pair[0], shift, 0), pltpu.roll(pair[1], shift, 0)))
            high = jnp.where(sub == e - 8 * g, pair[0], high)
            low = jnp.where(sub == e - 8 * g, pair[1], low)
        pair = (high, low)
        for shift in (64, 32, 16, 8, 4, 2, 1):
            pair = df_add(pair, (pltpu.roll(pair[0], shift, 1), pltpu.roll(pair[1], shift, 1)))
        groups.append(pair)
    line = jnp.zeros((8, 128), jnp.float32)
    for e in range(len(PAIRS)):
        pair = groups[e // 8]
        for half in range(2):
            line = jnp.where(lane == 16 * half + e, pair[half][e % 8 : e % 8 + 1, :], line)
    for k in range(5):
        line = jnp.where(lane == 32 + k, inverses[k], line)
        line = jnp.where(lane == 40 + k, scales[k], line)
    for t in range(16):
        sums[8 * t : 8 * t + 8, :] = line

    for copy in keeps:
        copy.wait()


def turn_back_kernel(kept, out):
    for k in range(4):
        for x in range(8):
            out[k, pl.ds(x, 128, stride=8), :] = kept[k, x].T


def finish_kernel(recv, vectors, out):
    data = recv[...]
    lane = iota((128, 128), 1)
    smallest = jnp.min(data, axis=0, keepdims=True)
    factor = data * jnp.broadcast_to(pltpu.roll(jnp.broadcast_to(smallest, (8, 128)), 120, 1)[0:1], (128, 128))
    left = jnp.zeros((128, 128), jnp.float32)
    right = jnp.zeros((128, 128), jnp.float32)
    for k in range(5):
        column = jnp.broadcast_to(factor[:, 32 + k : 33 + k], (128, 128))
        for e, (p, q) in enumerate(PAIRS):
            if p == k:
                left = jnp.where(lane % 16 == e, column, left)
            if q == k:
                right = jnp.where(lane % 16 == e, column, right)
    scaled = data * left * right
    low = pltpu.roll(scaled, 112, 1)
    pair = (scaled[0:8], low[0:8])
    for t in range(1, 16):
        pair = df_add(pair, (scaled[8 * t : 8 * t + 8], low[8 * t : 8 * t + 8]))
    for shift in (4, 2, 1):
        pair = df_add(pair, (pltpu.roll(pair[0], shift, 0), pltpu.roll(pair[1], shift, 0)))
    entry = {}
    for e, (p, q) in enumerate(PAIRS):
        entry[p, q] = tuple(jnp.broadcast_to(half[:, e : e + 1], (8, 128)) for half in pair)

    def scale_of(k):
        return jnp.broadcast_to(smallest[:, k : k + 1], (8, 128))

    rows = {(i, j): entry[i + 1, j + 1] for i in range(4) for j in range(i, 4)}
    right_side = [entry[0, j + 1] for j in range(4)]
    for k in range(4):
        for i in range(k + 1, 4):
            ratio = df_neg(df_div(rows[k, i], rows[k, k]))
            for j in range(i, 4):
                rows[i, j] = df_add(rows[i, j], df_mul(ratio, rows[k, j]))
            right_side[i] = df_add(right_side[i], df_mul(ratio, right_side[k]))
    coeffs = [None] * 4
    for k in reversed(range(4)):
        running = right_side[k]
        for j in range(k + 1, 4):
            running = df_add(running, df_neg(df_mul(rows[k, j], coeffs[j])))
        coeffs[k] = df_div(running, rows[k, k])
    inverse_first = jnp.max(jnp.where(lane == 32, data, 0.0), axis=0, keepdims=True)
    inverse_first = jnp.broadcast_to(jnp.max(inverse_first, axis=1, keepdims=True), (8, 128))
    weights = [(coeffs[k][0] * scale_of(41 + k)) * inverse_first for k in range(4)]

    def rows_of(t):
        for k in range(4):
            at = pl.ds(pl.multiple_of(32 * t + 8 * k, 8), 8)
            total = weights[0] * vectors[0, at, :]
            for j in range(1, 4):
                total = total + weights[j] * vectors[j, at, :]
            out[at, :] = total

    loop(32, rows_of)


def call(kernel, out_shape, in_specs, out_specs, scratch, mib, cost):
    return pl.pallas_call(
        kernel,
        out_shape=out_shape,
        in_specs=in_specs,
        out_specs=out_specs,
        scratch_shapes=scratch,
        compiler_params=params(mib),
        cost_estimate=pl.CostEstimate(flops=cost[0], bytes_accessed=cost[1], transcendentals=0),
    )


def body(held_head, held_head_old, material_ids, block_map, conductivity, vg_alpha, vg_n, capacity):
    count_x, count_y = lax.axis_size("gx"), lax.axis_size("gy")
    devices = count_x * count_y
    own_index = lax.axis_index(AXES)
    numbers = jnp.arange(devices, dtype=jnp.int32)
    scratch = lambda *shape: pltpu.VMEM(shape, jnp.float32)

    up_x = [(i, i + 1) for i in range(count_x - 1)]
    down_x = [(i + 1, i) for i in range(count_x - 1)]
    up_y = [(i, i + 1) for i in range(count_y - 1)]
    down_y = [(i + 1, i) for i in range(count_y - 1)]
    slot_of, ids, first, last = call(
        turn_ids_kernel,
        [jax.ShapeDtypeStruct((8, 128), jnp.int32), f32(8, 128, 128)] + [f32(DEPTH, 128, 128)] * 2,
        [VMEM, VMEM],
        [VMEM] * 4,
        [],
        63,
        (10**6, 10**6),
    )(block_map, material_ids.reshape(1024, 128))
    below = lax.ppermute(last, "gx", up_x)
    above = lax.ppermute(first, "gx", down_x)

    packed = call(
        pack_kernel,
        f32(devices * PIECE, 128),
        [SMEM, VMEM, VMEM],
        HBM,
        [scratch(devices * PIECE, 128), scratch(PY, 128), pltpu.SemaphoreType.DMA],
        63,
        (10**6, 4 * 10**6),
    )(slot_of, held_head, held_head_old)
    packed, below, above = lax.optimization_barrier((packed, below, above))
    arrived = lax.all_to_all(packed, AXES, split_axis=0, concat_axis=0, tiled=True)

    offsets = (0, -count_y, count_y, -1, 1, count_y - 1, -count_y - 1, count_y + 1, -count_y + 1)
    bricks = own_index + jnp.array(offsets, jnp.int32)
    source = jnp.sum(
        jnp.where(block_map[None] == bricks[:, None, None], numbers[None, :, None], 0), axis=1
    )
    first, last = call(
        edge_ids_kernel, [f32(EX, 8, 128)] * 2, [VMEM] * 3, [VMEM] * 2, [], 8, (10**5, 10**6)
    )(below, ids, above)
    y_low = lax.ppermute(last, "gy", up_y)
    y_high = lax.ppermute(first, "gy", down_y)
    *fields, edges = call(
        properties_kernel,
        [f32(EX, 128, 128)] * 7 + [f32(EX, 2, 8, 128)],
        [SMEM] * 4 + [VMEM] * 3,
        [HBM] * 8,
        [scratch(EX, 128, 128)] * 7 + [scratch(EX, 2, 8, 128), scratch(EX, 128, 128), scratch(EX, 136, 128)]
        + [pltpu.SemaphoreType.DMA((8,))],
        63,
        (40 * 10**6, 12 * 10**6),
    )(conductivity, vg_alpha, vg_n, capacity, below, ids, above)

    kept, sums = call(
        main_kernel,
        [f32(4, 8, 128, 128), f32(devices, 128)],
        [SMEM] * 5 + [VMEM] * 4 + [HBM] * 7,
        [HBM, VMEM],
        [scratch(EX, EY, 128)] * 5 + [scratch(EX, PY, 128), scratch(EX, EY, 128)]
        + [pltpu.SemaphoreType.DMA((11,)), scratch(devices * PIECE, 128)] + [scratch(EX, PY, 128)] * 16
        + [scratch(EX, 16, 128), scratch(EX, PY, 128)],
        63,
        (200 * 10**6, 16 * 10**6),
    )(source, conductivity, vg_alpha, vg_n, capacity, arrived, y_low, y_high, edges, *fields)
    gathered = lax.all_to_all(sums.reshape(devices, 1, 128), AXES, split_axis=0, concat_axis=0, tiled=True)
    turned = call(turn_back_kernel, f32(4, 1024, 128), [VMEM], VMEM, [], 8, (10**6, 4 * 10**6))(kept)
    update = call(finish_kernel, f32(1024, 128), [VMEM] * 2, VMEM, [], 8, (10**6, 3 * 10**6))(
        gathered.reshape(devices, 128), turned
    )
    return update.reshape(128, 8, 128)


def solution(mesh):
    return jax.shard_map(
        body,
        mesh=mesh,
        in_specs=(
            P(("gx", "gy"), None, None),
            P(("gx", "gy"), None, None),
            P(None, "gx", "gy"),
            P(),
            P(),
            P(),
            P(),
            P(),
        ),
        out_specs=P(None, "gx", "gy"),
        check_vma=False,
    )
```

```python
import jax
import jax.numpy as jnp
from jax import lax
from jax.experimental import pallas as pl
from jax.experimental.pallas import tpu as pltpu
from jax.sharding import PartitionSpec as P

MATERIALS = 16
STORE = 4.0
AXES = ("gx", "gy")

PIECE = 40
DEPTH = 5
EX = 8 + 2 * DEPTH
EY = 144
PY = 160
CHUNK = 24
CHUNKS = EY // CHUNK
PAIRS = [(i, j) for j in range(1, 5) for i in range(0, j + 1)]


def f32(*shape):
    return jax.ShapeDtypeStruct(shape, jnp.float32)


def params(mib):
    return pltpu.CompilerParams(vmem_limit_bytes=mib << 20)


VMEM = pl.BlockSpec(memory_space=pltpu.VMEM)
SMEM = pl.BlockSpec(memory_space=pltpu.SMEM)
HBM = pl.BlockSpec(memory_space=pltpu.HBM)


def iota(shape, axis):
    return lax.broadcasted_iota(jnp.int32, shape, axis)


def loop(count, body, unroll=1):
    def several(i, carry):
        for k in range(unroll):
            body(unroll * i + k)
        return carry

    lax.fori_loop(0, count // unroll, several, 0)


def pack_kernel(slot_of, head, old, packed, out, edge, sem):
    sub = iota((8, 128), 0)

    def brick(b):
        own = slot_of[0, b]
        below = slot_of[0, jnp.maximum(b - 8, 0)]
        above = slot_of[0, jnp.minimum(b + 8, 127)]
        head_below, head_above = head[below], head[above]
        old_below, old_above = old[below], old[above]

        def put(tile, value):
            out[pl.ds(pl.multiple_of(b * PIECE + 8 * tile, 8), 8), :] = value

        put(0, head[own])
        put(1, old[own])
        put(2, jnp.where(sub >= 3, head_below, head_above))
        put(3, jnp.where(sub < 3, old_above, jnp.where(sub < 5, head_above, old_below)))
        put(4, jnp.where(sub == 3, old_above, old_below))

    loop(128, brick, 8)
    lane = iota((128, 128), 1)
    low = lane % 16 < 8
    edge[0:16, :] = jnp.full((16, 128), -1.0, jnp.float32)
    edge[144:160, :] = jnp.full((16, 128), -1.0, jnp.float32)
    for field, (y_row, corner_row) in enumerate(((32, 34), (33, 37))):
        columns = jnp.zeros((128, 128), jnp.float32)
        for x in range(8):
            rows = out[pl.ds(8 * field + x, 128, stride=PIECE), :]
            columns = jnp.where(lane // 16 == x, pltpu.roll(rows, 16 * x + 8, 1), columns)
        edge[16:144, :] = columns
        out[pl.ds(y_row, 128, stride=PIECE), :] = jnp.where(low, edge[15:143, :], edge[17:145, :])
        out[pl.ds(corner_row, 128, stride=PIECE), :] = jnp.where(
            lane < 64,
            jnp.where(low, edge[23:151, :], edge[25:153, :]),
            jnp.where(low, edge[7:135, :], edge[9:137, :]),
        )
    copy = pltpu.make_async_copy(out, packed, sem)
    copy.start()
    copy.wait()


def is_even():
    return lax.axis_index("gx") % 2 == 0


def turn_ids_kernel(block_map, ids, slot_of, inner, outer, turned):
    row = jnp.broadcast_to(block_map[pl.ds(lax.axis_index(AXES), 1), :], (128, 128))
    match = row == iota((128, 128), 0)
    slot = jnp.sum(jnp.where(match, iota((128, 128), 1), 0).astype(jnp.float32), axis=1, keepdims=True)
    slot_of[...] = jnp.broadcast_to(slot, (128, 128)).T[0:8].astype(jnp.int32)
    for x in range(8):
        turned[x] = ids[pl.ds(x, 128, stride=8), :].astype(jnp.float32).T
    first = jnp.where(is_even(), 8 - DEPTH, 0)
    for k in range(DEPTH):
        inner[k] = turned[first + k]
        outer[k] = turned[8 - DEPTH - first + k]


def id_rows(inner, outer, inner_in, outer_in):
    even = is_even()

    def read(k, low, high, at):
        return jnp.where(even, low[k, at, :], high[k, at, :])

    return (
        (0, DEPTH, lambda k, at: read(k, outer_in, inner_in, at)),
        (DEPTH, DEPTH, lambda k, at: read(k, outer, inner, at)),
        (2 * DEPTH, 8 - DEPTH, lambda k, at: read(k + 2 * DEPTH - 8, inner, outer, at)),
        (8 + DEPTH, DEPTH, lambda k, at: read(k, inner_in, outer_in, at)),
    )


def edge_ids_kernel(inner, outer, inner_in, outer_in, first, last):
    for start, count, read in id_rows(inner, outer, inner_in, outer_in):
        for k in range(count):
            first[start + k] = read(k, slice(0, 8))
            last[start + k] = read(k, slice(120, 128))


def tables_of(conductivity, vg_alpha, vg_n, capacity):
    lane = iota((8, 128), 1)
    reads = [
        lambda m: conductivity[0, m], lambda m: conductivity[1, m], lambda m: conductivity[2, m],
        lambda m: vg_alpha[m], lambda m: vg_n[m], lambda m: capacity[m],
    ]
    tables = []
    for read in reads:
        table = jnp.zeros((8, 128), jnp.float32)
        for m in range(MATERIALS):
            table = jnp.where(lane == m, read(m), table)
        tables.append(table)
    return tables


def lookup(tables, ids):
    index = ids.astype(jnp.int32)
    return [jnp.take_along_axis(table, index, axis=1) for table in tables]


def half_mean(a, b):
    return a * b / (a + b)


def upward_faces(kz):
    return jnp.where(iota(kz.shape, 1) < 127, half_mean(kz, pltpu.roll(kz, 127, 1)), 0.0)


def x_inside(xi):
    x = lax.axis_index("gx") * 8 - DEPTH + xi
    return jnp.where((x >= 0) & (x + 1 < lax.axis_size("gx") * 8), 1.0, 0.0)


def y_inside(shape, first):
    y = lax.axis_index("gy") * 128 - 8 + first + iota(shape, 0)
    return (y >= 0) & (y + 1 < lax.axis_size("gy") * 128)


def properties_kernel(
    conductivity, vg_alpha, vg_n, capacity, inner, outer, inner_in, outer_in,
    out_a, out_n, out_m, out_c, out_x, out_y, out_z, out_e,
    alpha, expo, exponent, cap, trans_x, trans_y, trans_z, edges, cond_x, cond_y, sems,
):
    def copies(first, last):
        made = (alpha, expo, exponent, cap, trans_x, trans_y, trans_z, edges)
        outs = (out_a, out_n, out_m, out_c, out_x, out_y, out_z, out_e)
        return [pltpu.make_async_copy(made[k], outs[k], sems.at[k]) for k in range(first, last)]

    tables = tables_of(conductivity, vg_alpha, vg_n, capacity)

    def fill_row(xi, read, k):
        for t in range(16):
            at = slice(8 * t, 8 * t + 8)
            kx, ky, kz, a, n, c = lookup(tables, read(k, at))
            alpha[xi, at, :] = a
            expo[xi, at, :] = n
            exponent[xi, at, :] = 1.0 - 1.0 / n
            cap[xi, at, :] = STORE * c
            cond_x[xi, at, :] = kx
            cond_y[xi, at, :] = ky
            trans_z[xi, at, :] = upward_faces(kz)
            if t in (0, 15):
                edges[xi, t // 15] = ky

    for start, count, read in id_rows(inner, outer, inner_in, outer_in):
        loop(count, lambda k: fill_row(start + k, read, k))
    for copy in copies(0, 4):
        copy.start()

    def faces(xi):
        inside = x_inside(xi)
        above_xi = jnp.minimum(xi + 1, EX - 1)
        for c in range(4):
            at = slice(32 * c, 32 * c + 32)
            trans_x[xi, at, :] = inside * half_mean(cond_x[xi, at, :], cond_x[above_xi, at, :])
            up = slice(32 * c + 1, 32 * c + 33)
            trans_y[xi, at, :] = half_mean(cond_y[xi, at, :], cond_y[xi, up, :])

    loop(EX, faces)
    for copy in copies(4, 8):
        copy.start()
    for copy in copies(0, 8):
        copy.wait()


def wetness(level, alpha, expo, exponent):
    power = jnp.exp(expo * jnp.log(alpha * -level))
    return power, -jnp.log(1.0 + power)


def retention(level, alpha, expo, exponent):
    log_scaled = expo * jnp.log(alpha * -level)
    power = jnp.exp(log_scaled)
    total = 1.0 + power
    inverse = 1.0 / total
    log_inverse = -jnp.log(total)
    root = jnp.exp(0.5 * exponent * log_inverse)
    saturation = root * root
    rest = power * inverse
    z = 1.0 / (1.0 + 2.0 * power)
    zz = z * z
    series = 1.0 / 15.0
    for k in (13.0, 11.0, 9.0, 7.0, 5.0, 3.0, 1.0):
        series = series * zz + 1.0 / k
    log_rest = jnp.where(power >= 1.0, -2.0 * z * series, log_scaled + log_inverse)
    e = exponent * log_rest
    rest_power = jnp.exp(e)
    taylor = 1.0 + e * (1.0 / 8.0)
    for k in (7.0, 6.0, 5.0, 4.0, 3.0, 2.0):
        taylor = 1.0 + (e * (1.0 / k)) * taylor
    inner = jnp.where(e > -0.35, -e * taylor, 1.0 - rest_power)
    relperm = root * inner * inner
    rate = (expo - 1.0) / -level
    d_sat = saturation * rest * rate
    d_rel = root * inner * rate * (0.5 * inner * rest + 2.0 * inverse * rest_power)
    return saturation, relperm, d_sat, d_rel


def split(a, factor):
    c = a * factor
    high = c - (c - a)
    return high, a - high


def two_sum(a, b):
    s = a + b
    t = s - a
    return s, (a - (s - t)) + (b - t)


def df_add(a, b):
    s, e = two_sum(a[0], b[0])
    e = e + (a[1] + b[1])
    t = s + e
    return t, e - (t - s)


def df_mul(a, b):
    ah, al = split(a[0], 4097.0)
    bh, bl = split(b[0], 4097.0)
    p = a[0] * b[0]
    e = ((ah * bh - p) + ah * bl + al * bh) + al * bl
    e = e + (a[0] * b[1] + a[1] * b[0])
    t = p + e
    return t, e - (t - p)


def df_neg(a):
    return -a[0], -a[1]


def df_div(a, b):
    q = a[0] / b[0]
    zero = jnp.zeros_like(q)
    r = df_add(a, df_neg(df_mul((q, zero), b)))
    return two_sum(q, r[0] / b[0])


def main_kernel(
    source, conductivity, vg_alpha, vg_n, capacity,
    arrived, y_low, y_high, edges, in_a, in_n, in_m, in_c, in_x, in_y, in_z, kept, sums,
    recv, alpha, expo, exponent, cap, trans_x, trans_y, trans_z, sems, ordered, head, old, rel, d_rel, own_c, cxp, cxm, cyp, cym, czp, czm, k0, k1, k2, k3, k4,
    side_x, side_y,
):
    sub = iota((8, 128), 0)
    lane = iota((8, 128), 1)
    refs = (
        (in_a, alpha), (in_n, expo), (in_m, exponent), (in_c, cap),
        (in_x, trans_x), (in_y, trans_y), (in_z, trans_z),
    )
    copies = [
        pltpu.make_async_copy(a, b.at[:, 16:144] if b is trans_y else b.at[:, 8:136], sems.at[k])
        for k, (a, b) in enumerate(refs)
    ]
    arrival = pltpu.make_async_copy(arrived, recv, sems.at[11])
    arrival.start()
    for copy in copies:
        copy.start()

    low = lane % 16 < 8

    tables = tables_of(conductivity, vg_alpha, vg_n, capacity)

    def side_rows(xi):
        for source_ids, at in ((y_low, slice(0, 8)), (y_high, slice(136, 144))):
            to = slice(at.start + 8, at.stop + 8)
            kx, ky, kz, a, n, c = lookup(tables, source_ids[xi])
            alpha[xi, at, :] = a
            expo[xi, at, :] = n
            exponent[xi, at, :] = 1.0 - 1.0 / n
            cap[xi, at, :] = STORE * c
            trans_z[xi, at, :] = upward_faces(kz)
            side_x[xi, at.start // 17 : at.start // 17 + 8, :] = kx
            side_y[xi, to, :] = ky
        side_y[xi, 16:24, :] = edges[xi, 0]
        side_y[xi, 136:144, :] = edges[xi, 1]

    loop(EX, side_rows, 3)
    arrival.wait()

    def layer(z):
        def tile(k, t):
            return recv[pl.ds(pl.multiple_of(source[k, z] * PIECE + 8 * t, 8), 8), :]

        def put(t, value):
            ordered[pl.ds(pl.multiple_of(z * PIECE + 8 * t, 8), 8), :] = value

        put(0, tile(0, 0))
        put(1, tile(0, 1))
        put(2, jnp.where(sub >= 3, tile(1, 2), tile(2, 2)))
        put(3, jnp.where(sub < 5, tile(2, 3), tile(1, 3)))
        sides = jnp.where(low, tile(3, 4), tile(4, 4))
        corners = jnp.where(
            lane < 64, jnp.where(low, tile(5, 4), tile(7, 4)), jnp.where(low, tile(6, 4), tile(8, 4))
        )
        put(
            4,
            jnp.where(
                sub < 2, sides, jnp.where(sub == 3, tile(2, 4), jnp.where(sub == 4, tile(1, 4), corners))
            ),
        )

    loop(128, layer, 4)

    def plane(r):
        return ordered[pl.ds(r, 128, stride=PIECE), :].T

    for xi, r in enumerate([19, 20, 21, 22, 23] + list(range(8)) + [16, 17, 18, 27, 28]):
        head[xi, 16:144, :] = plane(r)
    for xi, r in enumerate([36, 29, 30, 31] + list(range(8, 16)) + [24, 25, 26, 35]):
        old[xi + 1, 16:144, :] = plane(r)
    for field, (y_row, corner_row) in ((head, (32, 34)), (old, (33, 37))):
        sides = plane(y_row)
        for x in range(8):
            field[5 + x, 8:16, :] = sides[16 * x : 16 * x + 8]
            field[5 + x, 144:152, :] = sides[16 * x + 8 : 16 * x + 16]
        corners = plane(corner_row)
        for x in range(8):
            xi = 13 + x if x < 4 else x - 3
            field[xi, 8:16, :] = corners[16 * x : 16 * x + 8]
            field[xi, 144:152, :] = corners[16 * x + 8 : 16 * x + 16]
    for xi in (0, 17):
        head[xi, 8:16, :] = jnp.full((8, 128), -1.0, jnp.float32)
        head[xi, 144:152, :] = jnp.full((8, 128), -1.0, jnp.float32)

    def curves(xi):
        for c in range(CHUNKS):
            at = slice(CHUNK * c, CHUNK * (c + 1))
            to = slice(8 + CHUNK * c, 8 + CHUNK * (c + 1))
            sat_v, rel_v, dsat_v, drel_v = retention(
                head[xi, to, :], alpha[xi, at, :], expo[xi, at, :], exponent[xi, at, :]
            )
            k0[xi, to, :] = sat_v
            rel[xi, to, :] = rel_v
            d_rel[xi, to, :] = drel_v
            own_c[xi, to, :] = cap[xi, at, :] * dsat_v

    for copy in copies[:4]:
        copy.wait()
    loop(EX, curves, 2)
    for copy in copies[4:]:
        copy.wait()

    def side_faces(xi):
        pair = x_inside(xi) * half_mean(side_x[xi], side_x[jnp.minimum(xi + 1, EX - 1)])
        trans_x[xi, 0:8, :] = pair[0:8]
        trans_x[xi, 136:144, :] = pair[8:16]
        for first, last in ((8, 16), (136, 152)):
            here = slice(first, last)
            value = half_mean(side_y[xi, here, :], side_y[xi, first + 1 : last + 1, :])
            trans_y[xi, here, :] = jnp.where(y_inside(value.shape, first - 8), value, 0.0)

    loop(EX, side_faces, 3)

    def face(half, h_a, h_b, r_a, r_b, d_a, d_b, rise):
        potential = h_b - h_a
        if rise:
            potential = potential + rise
        along = half * (r_a + r_b)
        slope = half * potential
        return along + slope * d_b, along - slope * d_a, along * potential, slope * (d_a + d_b)

    def x_faces(xi, to, at, h, r, d):
        c_p, c_m, flux, both = face(
            trans_x[xi, at, :], h, head[xi + 1, to, :], r, rel[xi + 1, to, :], d, d_rel[xi + 1, to, :], 0.0
        )
        cxp[xi, to, :] = c_p
        cxm[xi + 1, to, :] = c_m
        k1[xi, to, :] = flux
        k2[xi, to, :] = both
        return flux, both

    for c in range(CHUNKS):
        at = slice(CHUNK * c, CHUNK * (c + 1))
        to = slice(8 + CHUNK * c, 8 + CHUNK * (c + 1))
        x_faces(0, to, at, head[0, to, :], rel[0, to, :], d_rel[0, to, :])

    def coefficients(i):
        xi = i + 1
        for c in range(CHUNKS):
            at = slice(CHUNK * c, CHUNK * (c + 1))
            to = slice(8 + CHUNK * c, 8 + CHUNK * (c + 1))
            up = slice(9 + CHUNK * c, 9 + CHUNK * (c + 1))
            down = slice(7 + CHUNK * c, 7 + CHUNK * (c + 1))
            _, log_old = wetness(old[xi, to, :], alpha[xi, at, :], expo[xi, at, :], exponent[xi, at, :])
            old_sat = jnp.exp(exponent[xi, at, :] * log_old)
            start = cap[xi, at, :] * (old_sat - k0[xi, to, :])
            h, r, d = head[xi, to, :], rel[xi, to, :], d_rel[xi, to, :]
            flux, both = x_faces(xi, to, at, h, r, d)
            start = start + (flux - k1[xi - 1, to, :])
            centre = own_c[xi, to, :] - (both - k2[xi - 1, to, :])
            c_p, c_m, flux, both = face(
                trans_y[xi, to, :], h, head[xi, up, :], r, rel[xi, up, :], d, d_rel[xi, up, :], 0.0
            )
            cyp[xi, to, :] = c_p
            cym[xi, up, :] = c_m
            k3[xi, to, :] = flux
            k4[xi, to, :] = both
            start = start + (flux - k3[xi, down, :])
            centre = centre - (both - k4[xi, down, :])
            c_p, c_m, flux, both = face(
                trans_z[xi, at, :], h, pltpu.roll(h, 127, 1), r, pltpu.roll(r, 127, 1), d, pltpu.roll(d, 127, 1), 1.0
            )
            czp[xi, to, :] = c_p
            czm[xi, to, :] = pltpu.roll(c_m, 1, 1)
            own_c[xi, to, :] = centre - (both - pltpu.roll(both, 1, 1))
            k0[xi, to, :] = start + (flux - pltpu.roll(flux, 1, 1))

    loop(16, coefficients, 2)

    vectors = (k0, k1, k2, k3, k4)
    for step in range(4):
        v_ref, w_ref = vectors[step], vectors[step + 1]

        def apply(i):
            xi = i + 2 + step
            for c in range(CHUNKS):
                to = slice(8 + CHUNK * c, 8 + CHUNK * (c + 1))
                up = slice(9 + CHUNK * c, 9 + CHUNK * (c + 1))
                down = slice(7 + CHUNK * c, 7 + CHUNK * (c + 1))
                v = v_ref[xi, to, :]
                w = own_c[xi, to, :] * v
                w = w + cxp[xi, to, :] * (v - v_ref[xi + 1, to, :])
                w = w + cxm[xi, to, :] * (v - v_ref[xi - 1, to, :])
                w = w + cyp[xi, to, :] * (v - v_ref[xi, up, :])
                w = w + cym[xi, to, :] * (v - v_ref[xi, down, :])
                w = w + czp[xi, to, :] * (v - pltpu.roll(v, 127, 1))
                w = w + czm[xi, to, :] * (v - pltpu.roll(v, 1, 1))
                w_ref[xi, to, :] = w

        loop(14 - 2 * step, apply, 7 - step)

    keeps = [
        pltpu.make_async_copy(vectors[k].at[5:13, 16:144, :], kept.at[k], sems.at[7 + k]) for k in range(4)
    ]
    for copy in keeps:
        copy.start()

    def largest(i, tops):
        xi = 5 + i
        for c in range(16):
            at = slice(16 + 8 * c, 24 + 8 * c)
            tops = [jnp.maximum(top, jnp.abs(v[xi, at, :])) for top, v in zip(tops, vectors)]
        return tops

    tops = lax.fori_loop(0, 8, largest, [jnp.zeros((8, 128), jnp.float32) for _ in range(5)])
    scales, inverses = [], []
    for top in tops:
        top = jnp.broadcast_to(jnp.max(top, keepdims=True), (8, 128))
        scale = jnp.full((8, 128), 2.0**96, jnp.float32)
        inverse = jnp.full((8, 128), 2.0**-96, jnp.float32)
        for j in range(-5, 7):
            over = top >= 2.0 ** (16 * j - 8)
            scale = jnp.where(over, 2.0 ** (-16 * j), scale)
            inverse = jnp.where(over, 2.0 ** (16 * j), inverse)
        scales.append(scale)
        inverses.append(inverse)

    def products(i, totals):
        leading, rest = totals
        xi = 5 + i // 8
        first = 16 + 16 * (i % 8)
        for k in range(2):
            at = pl.ds(pl.multiple_of(first + 8 * k, 8), 8)
            values = [v[xi, at, :] * scale for v, scale in zip(vectors, scales)]
            halves = [split(value, 65537.0) for value in values]
            leading, rest = list(leading), list(rest)
            for e, (p, q) in enumerate(PAIRS):
                leading[e] = leading[e] + halves[p][0] * halves[q][0]
                rest[e] = rest[e] + (halves[p][0] * halves[q][1] + halves[p][1] * values[q])
        return leading, rest

    zeros = [jnp.zeros((8, 128), jnp.float32) for _ in PAIRS]
    leading, rest = lax.fori_loop(0, 64, products, (zeros, list(zeros)))
    groups = []
    for g in range(2):
        high = jnp.zeros((8, 128), jnp.float32)
        low = jnp.zeros((8, 128), jnp.float32)
        for e in range(8 * g, min(8 * g + 8, len(PAIRS))):
            pair = two_sum(leading[e], rest[e])
            for shift in (4, 2, 1):
                pair = df_add(pair, (pltpu.roll(pair[0], shift, 0), pltpu.roll(pair[1], shift, 0)))
            high = jnp.where(sub == e - 8 * g, pair[0], high)
            low = jnp.where(sub == e - 8 * g, pair[1], low)
        pair = (high, low)
        for shift in (64, 32, 16, 8, 4, 2, 1):
            pair = df_add(pair, (pltpu.roll(pair[0], shift, 1), pltpu.roll(pair[1], shift, 1)))
        groups.append(pair)
    line = jnp.zeros((8, 128), jnp.float32)
    for e in range(len(PAIRS)):
        pair = groups[e // 8]
        for half in range(2):
            line = jnp.where(lane == 16 * half + e, pair[half][e % 8 : e % 8 + 1, :], line)
    for k in range(5):
        line = jnp.where(lane == 32 + k, inverses[k], line)
        line = jnp.where(lane == 40 + k, scales[k], line)
    for t in range(16):
        sums[8 * t : 8 * t + 8, :] = line

    for copy in keeps:
        copy.wait()


def turn_back_kernel(kept, out):
    for k in range(4):
        for x in range(8):
            out[k, pl.ds(x, 128, stride=8), :] = kept[k, x].T


def finish_kernel(recv, vectors, out):
    data = recv[...]
    lane = iota((128, 128), 1)
    smallest = jnp.min(data, axis=0, keepdims=True)
    factor = data * jnp.broadcast_to(pltpu.roll(jnp.broadcast_to(smallest, (8, 128)), 120, 1)[0:1], (128, 128))
    left = jnp.zeros((128, 128), jnp.float32)
    right = jnp.zeros((128, 128), jnp.float32)
    for k in range(5):
        column = jnp.broadcast_to(factor[:, 32 + k : 33 + k], (128, 128))
        for e, (p, q) in enumerate(PAIRS):
            if p == k:
                left = jnp.where(lane % 16 == e, column, left)
            if q == k:
                right = jnp.where(lane % 16 == e, column, right)
    scaled = data * left * right
    low = pltpu.roll(scaled, 112, 1)
    pair = (scaled[0:8], low[0:8])
    for t in range(1, 16):
        pair = df_add(pair, (scaled[8 * t : 8 * t + 8], low[8 * t : 8 * t + 8]))
    for shift in (4, 2, 1):
        pair = df_add(pair, (pltpu.roll(pair[0], shift, 0), pltpu.roll(pair[1], shift, 0)))
    entry = {}
    for e, (p, q) in enumerate(PAIRS):
        entry[p, q] = tuple(jnp.broadcast_to(half[:, e : e + 1], (8, 128)) for half in pair)

    def scale_of(k):
        return jnp.broadcast_to(smallest[:, k : k + 1], (8, 128))

    rows = {(i, j): entry[i + 1, j + 1] for i in range(4) for j in range(i, 4)}
    right_side = [entry[0, j + 1] for j in range(4)]
    for k in range(4):
        for i in range(k + 1, 4):
            ratio = df_neg(df_div(rows[k, i], rows[k, k]))
            for j in range(i, 4):
                rows[i, j] = df_add(rows[i, j], df_mul(ratio, rows[k, j]))
            right_side[i] = df_add(right_side[i], df_mul(ratio, right_side[k]))
    coeffs = [None] * 4
    for k in reversed(range(4)):
        running = right_side[k]
        for j in range(k + 1, 4):
            running = df_add(running, df_neg(df_mul(rows[k, j], coeffs[j])))
        coeffs[k] = df_div(running, rows[k, k])
    inverse_first = jnp.max(jnp.where(lane == 32, data, 0.0), axis=0, keepdims=True)
    inverse_first = jnp.broadcast_to(jnp.max(inverse_first, axis=1, keepdims=True), (8, 128))
    weights = [(coeffs[k][0] * scale_of(41 + k)) * inverse_first for k in range(4)]

    def rows_of(t):
        for k in range(4):
            at = pl.ds(pl.multiple_of(32 * t + 8 * k, 8), 8)
            total = weights[0] * vectors[0, at, :]
            for j in range(1, 4):
                total = total + weights[j] * vectors[j, at, :]
            out[at, :] = total

    loop(32, rows_of)


def call(kernel, out_shape, in_specs, out_specs, scratch, mib, cost):
    return pl.pallas_call(
        kernel,
        out_shape=out_shape,
        in_specs=in_specs,
        out_specs=out_specs,
        scratch_shapes=scratch,
        compiler_params=params(mib),
        cost_estimate=pl.CostEstimate(flops=cost[0], bytes_accessed=cost[1], transcendentals=0),
    )


def body(held_head, held_head_old, material_ids, block_map, conductivity, vg_alpha, vg_n, capacity):
    count_x, count_y = lax.axis_size("gx"), lax.axis_size("gy")
    devices = count_x * count_y
    own_index = lax.axis_index(AXES)
    numbers = jnp.arange(devices, dtype=jnp.int32)
    scratch = lambda *shape: pltpu.VMEM(shape, jnp.float32)

    beside = [(i, i ^ 1) for i in range(count_x)]
    across = [pair for i in range(1, count_x - 1, 2) for pair in ((i, i + 1), (i + 1, i))]
    up_y = [(i, i + 1) for i in range(count_y - 1)]
    down_y = [(i + 1, i) for i in range(count_y - 1)]
    slot_of, inner, outer = call(
        turn_ids_kernel,
        [jax.ShapeDtypeStruct((8, 128), jnp.int32)] + [f32(DEPTH, 128, 128)] * 2,
        [VMEM, VMEM],
        [VMEM] * 3,
        [scratch(8, 128, 128)],
        63,
        (10**6, 10**6),
    )(block_map, material_ids.reshape(1024, 128))
    outer_in = lax.ppermute(outer, "gx", across)
    inner_in = lax.ppermute(inner, "gx", beside)

    packed = call(
        pack_kernel,
        f32(devices * PIECE, 128),
        [SMEM, VMEM, VMEM],
        HBM,
        [scratch(devices * PIECE, 128), scratch(PY, 128), pltpu.SemaphoreType.DMA],
        63,
        (10**6, 4 * 10**6),
    )(slot_of, held_head, held_head_old)
    packed, inner_in, outer_in = lax.optimization_barrier((packed, inner_in, outer_in))
    arrived = lax.all_to_all(packed, AXES, split_axis=0, concat_axis=0, tiled=True)

    offsets = (0, -count_y, count_y, -1, 1, count_y - 1, -count_y - 1, count_y + 1, -count_y + 1)
    bricks = own_index + jnp.array(offsets, jnp.int32)
    source = jnp.sum(
        jnp.where(block_map[None] == bricks[:, None, None], numbers[None, :, None], 0), axis=1
    )
    first, last = call(
        edge_ids_kernel, [f32(EX, 8, 128)] * 2, [VMEM] * 4, [VMEM] * 2, [], 8, (10**5, 10**6)
    )(inner, outer, inner_in, outer_in)
    y_low = lax.ppermute(last, "gy", up_y)
    y_high = lax.ppermute(first, "gy", down_y)
    *fields, edges = call(
        properties_kernel,
        [f32(EX, 128, 128)] * 7 + [f32(EX, 2, 8, 128)],
        [SMEM] * 4 + [VMEM] * 4,
        [HBM] * 8,
        [scratch(EX, 128, 128)] * 7 + [scratch(EX, 2, 8, 128), scratch(EX, 128, 128), scratch(EX, 136, 128)]
        + [pltpu.SemaphoreType.DMA((8,))],
        63,
        (40 * 10**6, 12 * 10**6),
    )(conductivity, vg_alpha, vg_n, capacity, inner, outer, inner_in, outer_in)

    kept, sums = call(
        main_kernel,
        [f32(4, 8, 128, 128), f32(devices, 128)],
        [SMEM] * 5 + [HBM] + [VMEM] * 3 + [HBM] * 7,
        [HBM, VMEM],
        [scratch(devices * PIECE, 128)] + [scratch(EX, EY, 128)] * 5 + [scratch(EX, PY, 128), scratch(EX, EY, 128)]
        + [pltpu.SemaphoreType.DMA((12,)), scratch(devices * PIECE, 128)] + [scratch(EX, PY, 128)] * 16
        + [scratch(EX, 16, 128), scratch(EX, PY, 128)],
        63,
        (200 * 10**6, 16 * 10**6),
    )(source, conductivity, vg_alpha, vg_n, capacity, arrived, y_low, y_high, edges, *fields)
    gathered = lax.all_to_all(sums.reshape(devices, 1, 128), AXES, split_axis=0, concat_axis=0, tiled=True)
    turned = call(turn_back_kernel, f32(4, 1024, 128), [VMEM], VMEM, [], 8, (10**6, 4 * 10**6))(kept)
    update = call(finish_kernel, f32(1024, 128), [VMEM] * 2, VMEM, [], 8, (10**6, 3 * 10**6))(
        gathered.reshape(devices, 128), turned
    )
    return update.reshape(128, 8, 128)


def solution(mesh):
    return jax.shard_map(
        body,
        mesh=mesh,
        in_specs=(
            P(("gx", "gy"), None, None),
            P(("gx", "gy"), None, None),
            P(None, "gx", "gy"),
            P(),
            P(),
            P(),
            P(),
            P(),
        ),
        out_specs=P(None, "gx", "gy"),
        check_vma=False,
    )
```

```python
import jax
import jax.numpy as jnp
from jax import lax
from jax.experimental import pallas as pl
from jax.experimental.pallas import tpu as pltpu
from jax.sharding import PartitionSpec as P

MATERIALS = 16
STORE = 4.0
AXES = ("gx", "gy")

PIECE = 37
LAYER = 40
DEPTH = 5
EX = 8 + 2 * DEPTH
EY = 144
PY = 160
CHUNK = 24
CHUNKS = EY // CHUNK
PAIRS = [(i, j) for j in range(1, 5) for i in range(0, j + 1)]


def f32(*shape):
    return jax.ShapeDtypeStruct(shape, jnp.float32)


def params(mib):
    return pltpu.CompilerParams(vmem_limit_bytes=mib << 20)


VMEM = pl.BlockSpec(memory_space=pltpu.VMEM)
SMEM = pl.BlockSpec(memory_space=pltpu.SMEM)
HBM = pl.BlockSpec(memory_space=pltpu.HBM)


def iota(shape, axis):
    return lax.broadcasted_iota(jnp.int32, shape, axis)


def loop(count, body, unroll=1):
    def several(i, carry):
        for k in range(unroll):
            body(unroll * i + k)
        return carry

    lax.fori_loop(0, count // unroll, several, 0)


def pack_kernel(slot_of, head, old, packed, out, edge, sem):
    sub = iota((8, 128), 0)

    def brick(b):
        own = slot_of[0, b]
        below = slot_of[0, jnp.maximum(b - 8, 0)]
        above = slot_of[0, jnp.minimum(b + 8, 127)]
        head_below, head_above = head[below], head[above]
        old_below, old_above = old[below], old[above]

        def put(tile, value):
            out[pl.ds(b * PIECE + 8 * tile, 8), :] = value

        put(0, head[own])
        put(1, old[own])
        put(2, jnp.where(sub >= 3, head_below, head_above))
        put(3, jnp.where(sub < 3, old_above, jnp.where(sub < 5, head_above, old_below)))
        put(4, jnp.where(sub == 3, old_above, old_below))

    loop(128, brick, 8)
    lane = iota((128, 128), 1)
    low = lane % 16 < 8
    edge[0:16, :] = jnp.full((16, 128), -1.0, jnp.float32)
    edge[144:160, :] = jnp.full((16, 128), -1.0, jnp.float32)
    corners = []
    for field in range(2):
        columns = jnp.zeros((128, 128), jnp.float32)
        for x in range(8):
            rows = out[pl.ds(8 * field + x, 128, stride=PIECE), :]
            columns = jnp.where(lane // 16 == x, pltpu.roll(rows, 16 * x + 8, 1), columns)
        edge[16:144, :] = columns
        out[pl.ds(32 + field, 128, stride=PIECE), :] = jnp.where(low, edge[15:143, :], edge[17:145, :])
        corners.append(
            jnp.where(
                lane < 64,
                jnp.where(low, edge[23:151, :], edge[25:153, :]),
                jnp.where(low, edge[7:135, :], edge[9:137, :]),
            )
        )
    from_old = jnp.where(low, pltpu.roll(corners[1], 124, 1), pltpu.roll(corners[1], 4, 1))
    out[pl.ds(34, 128, stride=PIECE), :] = jnp.where((lane % 16 >= 4) & (lane % 16 < 12), corners[0], from_old)
    copy = pltpu.make_async_copy(out.at[0 : packed.shape[0]], packed, sem)
    copy.start()
    copy.wait()


def is_even():
    return lax.axis_index("gx") % 2 == 0


def turn_ids_kernel(block_map, ids, slot_of, inner, outer, turned):
    row = jnp.broadcast_to(block_map[pl.ds(lax.axis_index(AXES), 1), :], (128, 128))
    match = row == iota((128, 128), 0)
    slot = jnp.sum(jnp.where(match, iota((128, 128), 1), 0).astype(jnp.float32), axis=1, keepdims=True)
    slot_of[...] = jnp.broadcast_to(slot, (128, 128)).T[0:8].astype(jnp.int32)
    for x in range(8):
        turned[x] = ids[pl.ds(x, 128, stride=8), :].astype(jnp.float32).T
    first = jnp.where(is_even(), 8 - DEPTH, 0)
    for k in range(DEPTH):
        inner[k] = turned[first + k]
        outer[k] = turned[8 - DEPTH - first + k]


def id_rows(inner, outer, inner_in, outer_in):
    even = is_even()

    def read(k, low, high, at):
        return jnp.where(even, low[k, at, :], high[k, at, :])

    return (
        (0, DEPTH, lambda k, at: read(k, outer_in, inner_in, at)),
        (DEPTH, DEPTH, lambda k, at: read(k, outer, inner, at)),
        (2 * DEPTH, 8 - DEPTH, lambda k, at: read(k + 2 * DEPTH - 8, inner, outer, at)),
        (8 + DEPTH, DEPTH, lambda k, at: read(k, inner_in, outer_in, at)),
    )


def edge_ids_kernel(inner, outer, inner_in, outer_in, first, last):
    for start, count, read in id_rows(inner, outer, inner_in, outer_in):
        for k in range(count):
            first[start + k] = read(k, slice(0, 8))
            last[start + k] = read(k, slice(120, 128))


def tables_of(conductivity, vg_alpha, vg_n, capacity):
    lane = iota((8, 128), 1)
    reads = [
        lambda m: conductivity[0, m], lambda m: conductivity[1, m], lambda m: conductivity[2, m],
        lambda m: vg_alpha[m], lambda m: vg_n[m], lambda m: capacity[m],
    ]
    tables = []
    for read in reads:
        table = jnp.zeros((8, 128), jnp.float32)
        for m in range(MATERIALS):
            table = jnp.where(lane == m, read(m), table)
        tables.append(table)
    return tables


def lookup(tables, ids):
    index = ids.astype(jnp.int32)
    return [jnp.take_along_axis(table, index, axis=1) for table in tables]


def half_mean(a, b):
    return a * b / (a + b)


def upward_faces(kz):
    return jnp.where(iota(kz.shape, 1) < 127, half_mean(kz, pltpu.roll(kz, 127, 1)), 0.0)


def x_inside(xi):
    x = lax.axis_index("gx") * 8 - DEPTH + xi
    return jnp.where((x >= 0) & (x + 1 < lax.axis_size("gx") * 8), 1.0, 0.0)


def y_inside(shape, first):
    y = lax.axis_index("gy") * 128 - 8 + first + iota(shape, 0)
    return (y >= 0) & (y + 1 < lax.axis_size("gy") * 128)


def properties_kernel(
    conductivity, vg_alpha, vg_n, capacity, inner, outer, inner_in, outer_in,
    out_a, out_n, out_m, out_c, out_x, out_y, out_z, out_e,
    alpha, expo, exponent, cap, trans_x, trans_y, trans_z, edges, cond_x, cond_y, sems,
):
    def copies(first, last):
        made = (alpha, expo, exponent, cap, trans_x, trans_y, trans_z, edges)
        outs = (out_a, out_n, out_m, out_c, out_x, out_y, out_z, out_e)
        return [pltpu.make_async_copy(made[k], outs[k], sems.at[k]) for k in range(first, last)]

    tables = tables_of(conductivity, vg_alpha, vg_n, capacity)

    def fill_row(xi, read, k):
        for t in range(16):
            at = slice(8 * t, 8 * t + 8)
            kx, ky, kz, a, n, c = lookup(tables, read(k, at))
            alpha[xi, at, :] = a
            expo[xi, at, :] = n
            exponent[xi, at, :] = 1.0 - 1.0 / n
            cap[xi, at, :] = STORE * c
            cond_x[xi, at, :] = kx
            cond_y[xi, at, :] = ky
            trans_z[xi, at, :] = upward_faces(kz)
            if t in (0, 15):
                edges[xi, t // 15] = ky

    for start, count, read in id_rows(inner, outer, inner_in, outer_in):
        loop(count, lambda k: fill_row(start + k, read, k))
    for copy in copies(0, 4):
        copy.start()

    def faces(xi):
        inside = x_inside(xi)
        above_xi = jnp.minimum(xi + 1, EX - 1)
        for c in range(4):
            at = slice(32 * c, 32 * c + 32)
            trans_x[xi, at, :] = inside * half_mean(cond_x[xi, at, :], cond_x[above_xi, at, :])
            up = slice(32 * c + 1, 32 * c + 33)
            trans_y[xi, at, :] = half_mean(cond_y[xi, at, :], cond_y[xi, up, :])

    loop(EX, faces)
    for copy in copies(4, 8):
        copy.start()
    for copy in copies(0, 8):
        copy.wait()


def wetness(level, alpha, expo, exponent):
    power = jnp.exp(expo * jnp.log(alpha * -level))
    return power, -jnp.log(1.0 + power)


def retention(level, alpha, expo, exponent):
    log_scaled = expo * jnp.log(alpha * -level)
    power = jnp.exp(log_scaled)
    total = 1.0 + power
    inverse = 1.0 / total
    log_inverse = -jnp.log(total)
    root = jnp.exp(0.5 * exponent * log_inverse)
    saturation = root * root
    rest = power * inverse
    z = 1.0 / (1.0 + 2.0 * power)
    zz = z * z
    series = 1.0 / 15.0
    for k in (13.0, 11.0, 9.0, 7.0, 5.0, 3.0, 1.0):
        series = series * zz + 1.0 / k
    log_rest = jnp.where(power >= 1.0, -2.0 * z * series, log_scaled + log_inverse)
    e = exponent * log_rest
    rest_power = jnp.exp(e)
    taylor = 1.0 + e * (1.0 / 8.0)
    for k in (7.0, 6.0, 5.0, 4.0, 3.0, 2.0):
        taylor = 1.0 + (e * (1.0 / k)) * taylor
    inner = jnp.where(e > -0.35, -e * taylor, 1.0 - rest_power)
    relperm = root * inner * inner
    rate = (expo - 1.0) / -level
    d_sat = saturation * rest * rate
    d_rel = root * inner * rate * (0.5 * inner * rest + 2.0 * inverse * rest_power)
    return saturation, relperm, d_sat, d_rel


def split(a, factor):
    c = a * factor
    high = c - (c - a)
    return high, a - high


def two_sum(a, b):
    s = a + b
    t = s - a
    return s, (a - (s - t)) + (b - t)


def df_add(a, b):
    s, e = two_sum(a[0], b[0])
    e = e + (a[1] + b[1])
    t = s + e
    return t, e - (t - s)


def df_mul(a, b):
    ah, al = split(a[0], 4097.0)
    bh, bl = split(b[0], 4097.0)
    p = a[0] * b[0]
    e = ((ah * bh - p) + ah * bl + al * bh) + al * bl
    e = e + (a[0] * b[1] + a[1] * b[0])
    t = p + e
    return t, e - (t - p)


def df_neg(a):
    return -a[0], -a[1]


def df_div(a, b):
    q = a[0] / b[0]
    zero = jnp.zeros_like(q)
    r = df_add(a, df_neg(df_mul((q, zero), b)))
    return two_sum(q, r[0] / b[0])


def main_kernel(
    source, conductivity, vg_alpha, vg_n, capacity,
    arrived, y_low, y_high, edges, in_a, in_n, in_m, in_c, in_x, in_y, in_z, kept, sums,
    recv, alpha, expo, exponent, cap, trans_x, trans_y, trans_z, sems, ordered, head, old, rel, d_rel, own_c, cxp, cxm, cyp, cym, czp, czm, k0, k1, k2, k3, k4,
    side_x, side_y,
):
    sub = iota((8, 128), 0)
    lane = iota((8, 128), 1)
    refs = (
        (in_a, alpha), (in_n, expo), (in_m, exponent), (in_c, cap),
        (in_x, trans_x), (in_y, trans_y), (in_z, trans_z),
    )
    copies = [
        pltpu.make_async_copy(a, b.at[:, 16:144] if b is trans_y else b.at[:, 8:136], sems.at[k])
        for k, (a, b) in enumerate(refs)
    ]
    arrival = pltpu.make_async_copy(arrived, recv.at[0 : arrived.shape[0]], sems.at[11])
    arrival.start()
    for copy in copies:
        copy.start()

    low = lane % 16 < 8

    tables = tables_of(conductivity, vg_alpha, vg_n, capacity)

    def side_rows(xi):
        for source_ids, at in ((y_low, slice(0, 8)), (y_high, slice(136, 144))):
            to = slice(at.start + 8, at.stop + 8)
            kx, ky, kz, a, n, c = lookup(tables, source_ids[xi])
            alpha[xi, at, :] = a
            expo[xi, at, :] = n
            exponent[xi, at, :] = 1.0 - 1.0 / n
            cap[xi, at, :] = STORE * c
            trans_z[xi, at, :] = upward_faces(kz)
            side_x[xi, at.start // 17 : at.start // 17 + 8, :] = kx
            side_y[xi, to, :] = ky
        side_y[xi, 16:24, :] = edges[xi, 0]
        side_y[xi, 136:144, :] = edges[xi, 1]

    loop(EX, side_rows, 3)
    arrival.wait()

    def layer(z):
        def tile(k, t):
            return recv[pl.ds(source[k, z] * PIECE + 8 * t, 8), :]

        def put(t, value):
            ordered[pl.ds(pl.multiple_of(z * LAYER + 8 * t, 8), 8), :] = value

        put(0, tile(0, 0))
        put(1, tile(0, 1))
        put(2, jnp.where(sub >= 3, tile(1, 2), tile(2, 2)))
        put(3, jnp.where(sub < 5, tile(2, 3), tile(1, 3)))
        sides = jnp.where(low, tile(3, 4), tile(4, 4))
        corners = jnp.where(
            lane < 64, jnp.where(low, tile(5, 4), tile(7, 4)), jnp.where(low, tile(6, 4), tile(8, 4))
        )
        put(
            4,
            jnp.where(
                sub < 2, sides, jnp.where(sub == 3, tile(2, 4), jnp.where(sub == 4, tile(1, 4), corners))
            ),
        )

    loop(128, layer, 4)

    def plane(r):
        return ordered[pl.ds(r, 128, stride=LAYER), :].T

    for xi, r in enumerate([19, 20, 21, 22, 23] + list(range(8)) + [16, 17, 18, 27, 28]):
        head[xi, 16:144, :] = plane(r)
    for xi, r in enumerate([36, 29, 30, 31] + list(range(8, 16)) + [24, 25, 26, 35]):
        old[xi + 1, 16:144, :] = plane(r)
    corners = plane(34)
    for field, y_row in ((head, 32), (old, 33)):
        sides = plane(y_row)
        for x in range(8):
            field[5 + x, 8:16, :] = sides[16 * x : 16 * x + 8]
            field[5 + x, 144:152, :] = sides[16 * x + 8 : 16 * x + 16]
        for x in range(8):
            xi = 13 + x if x < 4 else x - 3
            beside = (corners[16 * x : 16 * x + 8], corners[16 * x + 8 : 16 * x + 16])
            if field is old:
                beside = [pltpu.roll(tile, 4, 0) for tile in beside]
            field[xi, 8:16, :], field[xi, 144:152, :] = beside
    for xi in (0, 17):
        head[xi, 8:16, :] = jnp.full((8, 128), -1.0, jnp.float32)
        head[xi, 144:152, :] = jnp.full((8, 128), -1.0, jnp.float32)

    def curves(xi):
        for c in range(CHUNKS):
            at = slice(CHUNK * c, CHUNK * (c + 1))
            to = slice(8 + CHUNK * c, 8 + CHUNK * (c + 1))
            sat_v, rel_v, dsat_v, drel_v = retention(
                head[xi, to, :], alpha[xi, at, :], expo[xi, at, :], exponent[xi, at, :]
            )
            k0[xi, to, :] = sat_v
            rel[xi, to, :] = rel_v
            d_rel[xi, to, :] = drel_v
            own_c[xi, to, :] = cap[xi, at, :] * dsat_v

    for copy in copies[:4]:
        copy.wait()
    loop(EX, curves, 2)
    for copy in copies[4:]:
        copy.wait()

    def side_faces(xi):
        pair = x_inside(xi) * half_mean(side_x[xi], side_x[jnp.minimum(xi + 1, EX - 1)])
        trans_x[xi, 0:8, :] = pair[0:8]
        trans_x[xi, 136:144, :] = pair[8:16]
        for first, last in ((8, 16), (136, 152)):
            here = slice(first, last)
            value = half_mean(side_y[xi, here, :], side_y[xi, first + 1 : last + 1, :])
            trans_y[xi, here, :] = jnp.where(y_inside(value.shape, first - 8), value, 0.0)

    loop(EX, side_faces, 3)

    def face(half, low, high, rise):
        (h_a, r_a, d_a), (h_b, r_b, d_b) = low, high
        potential = h_b - h_a
        if rise:
            potential = potential + rise
        along = half * (r_a + r_b)
        slope = half * potential
        return along + slope * d_b, along - slope * d_a, along * potential, slope * (d_a + d_b)

    def coefficients(i):
        xi = i + 1
        for c in range(CHUNKS):
            at = slice(CHUNK * c, CHUNK * (c + 1))
            to = slice(8 + CHUNK * c, 8 + CHUNK * (c + 1))
            up = slice(9 + CHUNK * c, 9 + CHUNK * (c + 1))
            down = slice(7 + CHUNK * c, 7 + CHUNK * (c + 1))
            _, log_old = wetness(old[xi, to, :], alpha[xi, at, :], expo[xi, at, :], exponent[xi, at, :])
            old_sat = jnp.exp(exponent[xi, at, :] * log_old)
            start = cap[xi, at, :] * (old_sat - k0[xi, to, :])
            centre = own_c[xi, to, :]
            here = [f[xi, to, :] for f in (head, rel, d_rel)]
            above_x = [f[xi + 1, to, :] for f in (head, rel, d_rel)]
            below_x = [f[xi - 1, to, :] for f in (head, rel, d_rel)]
            above_y = [f[xi, up, :] for f in (head, rel, d_rel)]
            below_y = [f[xi, down, :] for f in (head, rel, d_rel)]
            half_z = trans_z[xi, at, :]
            above_z = [pltpu.roll(f, 127, 1) for f in here]
            below_z = [pltpu.roll(f, 1, 1) for f in here]
            for c_up, c_down, half_up, half_down, above, below, rise in (
                (cxp, cxm, trans_x[xi, at, :], trans_x[xi - 1, at, :], above_x, below_x, 0.0),
                (cyp, cym, trans_y[xi, to, :], trans_y[xi, down, :], above_y, below_y, 0.0),
                (czp, czm, half_z, pltpu.roll(half_z, 1, 1), above_z, below_z, 1.0),
            ):
                c_p, _, flux, both = face(half_up, here, above, rise)
                _, c_m, flux_m, both_m = face(half_down, below, here, rise)
                c_up[xi, to, :] = c_p
                c_down[xi, to, :] = c_m
                start = start + (flux - flux_m)
                centre = centre - (both - both_m)
            own_c[xi, to, :] = centre
            k0[xi, to, :] = start

    loop(16, coefficients, 4)

    vectors = (k0, k1, k2, k3, k4)
    for step in range(4):
        v_ref, w_ref = vectors[step], vectors[step + 1]

        def apply(i):
            xi = i + 2 + step
            for c in range(CHUNKS):
                to = slice(8 + CHUNK * c, 8 + CHUNK * (c + 1))
                up = slice(9 + CHUNK * c, 9 + CHUNK * (c + 1))
                down = slice(7 + CHUNK * c, 7 + CHUNK * (c + 1))
                v = v_ref[xi, to, :]
                w = own_c[xi, to, :] * v
                w = w + cxp[xi, to, :] * (v - v_ref[xi + 1, to, :])
                w = w + cxm[xi, to, :] * (v - v_ref[xi - 1, to, :])
                w = w + cyp[xi, to, :] * (v - v_ref[xi, up, :])
                w = w + cym[xi, to, :] * (v - v_ref[xi, down, :])
                w = w + czp[xi, to, :] * (v - pltpu.roll(v, 127, 1))
                w = w + czm[xi, to, :] * (v - pltpu.roll(v, 1, 1))
                w_ref[xi, to, :] = w

        loop(14 - 2 * step, apply, 7 - step)

    keeps = [
        pltpu.make_async_copy(vectors[k].at[5:13, 16:144, :], kept.at[k], sems.at[7 + k]) for k in range(4)
    ]
    for copy in keeps:
        copy.start()

    def largest(i, tops):
        xi = 5 + i
        for c in range(16):
            at = slice(16 + 8 * c, 24 + 8 * c)
            tops = [jnp.maximum(top, jnp.abs(v[xi, at, :])) for top, v in zip(tops, vectors)]
        return tops

    tops = lax.fori_loop(0, 8, largest, [jnp.zeros((8, 128), jnp.float32) for _ in range(5)])
    scales, inverses = [], []
    for top in tops:
        top = jnp.broadcast_to(jnp.max(top, keepdims=True), (8, 128))
        scale = jnp.full((8, 128), 2.0**96, jnp.float32)
        inverse = jnp.full((8, 128), 2.0**-96, jnp.float32)
        for j in range(-5, 7):
            over = top >= 2.0 ** (16 * j - 8)
            scale = jnp.where(over, 2.0 ** (-16 * j), scale)
            inverse = jnp.where(over, 2.0 ** (16 * j), inverse)
        scales.append(scale)
        inverses.append(inverse)

    def products(i, totals):
        leading, rest = totals
        xi = 5 + i // 8
        first = 16 + 16 * (i % 8)
        for k in range(2):
            at = pl.ds(pl.multiple_of(first + 8 * k, 8), 8)
            values = [v[xi, at, :] * scale for v, scale in zip(vectors, scales)]
            halves = [split(value, 65537.0) for value in values]
            leading, rest = list(leading), list(rest)
            for e, (p, q) in enumerate(PAIRS):
                leading[e] = leading[e] + halves[p][0] * halves[q][0]
                rest[e] = rest[e] + (halves[p][0] * halves[q][1] + halves[p][1] * values[q])
        return leading, rest

    zeros = [jnp.zeros((8, 128), jnp.float32) for _ in PAIRS]
    leading, rest = lax.fori_loop(0, 64, products, (zeros, list(zeros)))
    groups = []
    for g in range(2):
        high = jnp.zeros((8, 128), jnp.float32)
        low = jnp.zeros((8, 128), jnp.float32)
        for e in range(8 * g, min(8 * g + 8, len(PAIRS))):
            pair = two_sum(leading[e], rest[e])
            for shift in (4, 2, 1):
                pair = df_add(pair, (pltpu.roll(pair[0], shift, 0), pltpu.roll(pair[1], shift, 0)))
            high = jnp.where(sub == e - 8 * g, pair[0], high)
            low = jnp.where(sub == e - 8 * g, pair[1], low)
        pair = (high, low)
        for shift in (64, 32, 16, 8, 4, 2, 1):
            pair = df_add(pair, (pltpu.roll(pair[0], shift, 1), pltpu.roll(pair[1], shift, 1)))
        groups.append(pair)
    line = jnp.zeros((8, 128), jnp.float32)
    for e in range(len(PAIRS)):
        pair = groups[e // 8]
        for half in range(2):
            line = jnp.where(lane == 16 * half + e, pair[half][e % 8 : e % 8 + 1, :], line)
    for k in range(5):
        line = jnp.where(lane == 32 + k, inverses[k], line)
        line = jnp.where(lane == 40 + k, scales[k], line)
    for t in range(16):
        sums[8 * t : 8 * t + 8, :] = line

    for copy in keeps:
        copy.wait()


def turn_back_kernel(kept, out):
    for k in range(4):
        for x in range(8):
            out[k, pl.ds(x, 128, stride=8), :] = kept[k, x].T


def finish_kernel(recv, vectors, out):
    data = recv[...]
    lane = iota((128, 128), 1)
    smallest = jnp.min(data, axis=0, keepdims=True)
    factor = data * jnp.broadcast_to(pltpu.roll(jnp.broadcast_to(smallest, (8, 128)), 120, 1)[0:1], (128, 128))
    left = jnp.zeros((128, 128), jnp.float32)
    right = jnp.zeros((128, 128), jnp.float32)
    for k in range(5):
        column = jnp.broadcast_to(factor[:, 32 + k : 33 + k], (128, 128))
        for e, (p, q) in enumerate(PAIRS):
            if p == k:
                left = jnp.where(lane % 16 == e, column, left)
            if q == k:
                right = jnp.where(lane % 16 == e, column, right)
    scaled = data * left * right
    low = pltpu.roll(scaled, 112, 1)
    pair = (scaled[0:8], low[0:8])
    for t in range(1, 16):
        pair = df_add(pair, (scaled[8 * t : 8 * t + 8], low[8 * t : 8 * t + 8]))
    for shift in (4, 2, 1):
        pair = df_add(pair, (pltpu.roll(pair[0], shift, 0), pltpu.roll(pair[1], shift, 0)))
    entry = {}
    for e, (p, q) in enumerate(PAIRS):
        entry[p, q] = tuple(jnp.broadcast_to(half[:, e : e + 1], (8, 128)) for half in pair)

    def scale_of(k):
        return jnp.broadcast_to(smallest[:, k : k + 1], (8, 128))

    rows = {(i, j): entry[i + 1, j + 1] for i in range(4) for j in range(i, 4)}
    right_side = [entry[0, j + 1] for j in range(4)]
    for k in range(4):
        for i in range(k + 1, 4):
            ratio = df_neg(df_div(rows[k, i], rows[k, k]))
            for j in range(i, 4):
                rows[i, j] = df_add(rows[i, j], df_mul(ratio, rows[k, j]))
            right_side[i] = df_add(right_side[i], df_mul(ratio, right_side[k]))
    coeffs = [None] * 4
    for k in reversed(range(4)):
        running = right_side[k]
        for j in range(k + 1, 4):
            running = df_add(running, df_neg(df_mul(rows[k, j], coeffs[j])))
        coeffs[k] = df_div(running, rows[k, k])
    inverse_first = jnp.max(jnp.where(lane == 32, data, 0.0), axis=0, keepdims=True)
    inverse_first = jnp.broadcast_to(jnp.max(inverse_first, axis=1, keepdims=True), (8, 128))
    weights = [(coeffs[k][0] * scale_of(41 + k)) * inverse_first for k in range(4)]

    def rows_of(t):
        for k in range(4):
            at = pl.ds(pl.multiple_of(32 * t + 8 * k, 8), 8)
            total = weights[0] * vectors[0, at, :]
            for j in range(1, 4):
                total = total + weights[j] * vectors[j, at, :]
            out[at, :] = total

    loop(32, rows_of)


def call(kernel, out_shape, in_specs, out_specs, scratch, mib, cost):
    return pl.pallas_call(
        kernel,
        out_shape=out_shape,
        in_specs=in_specs,
        out_specs=out_specs,
        scratch_shapes=scratch,
        compiler_params=params(mib),
        cost_estimate=pl.CostEstimate(flops=cost[0], bytes_accessed=cost[1], transcendentals=0),
    )


def body(held_head, held_head_old, material_ids, block_map, conductivity, vg_alpha, vg_n, capacity):
    count_x, count_y = lax.axis_size("gx"), lax.axis_size("gy")
    devices = count_x * count_y
    own_index = lax.axis_index(AXES)
    numbers = jnp.arange(devices, dtype=jnp.int32)
    scratch = lambda *shape: pltpu.VMEM(shape, jnp.float32)

    beside = [(i, i ^ 1) for i in range(count_x)]
    across = [pair for i in range(1, count_x - 1, 2) for pair in ((i, i + 1), (i + 1, i))]
    up_y = [(i, i + 1) for i in range(count_y - 1)]
    down_y = [(i + 1, i) for i in range(count_y - 1)]
    slot_of, inner, outer = call(
        turn_ids_kernel,
        [jax.ShapeDtypeStruct((8, 128), jnp.int32)] + [f32(DEPTH, 128, 128)] * 2,
        [VMEM, VMEM],
        [VMEM] * 3,
        [scratch(8, 128, 128)],
        63,
        (10**6, 10**6),
    )(block_map, material_ids.reshape(1024, 128))
    outer_in = lax.ppermute(outer, "gx", across)
    inner_in = lax.ppermute(inner, "gx", beside)

    packed = call(
        pack_kernel,
        f32(devices * PIECE, 128),
        [SMEM, VMEM, VMEM],
        HBM,
        [scratch(devices * PIECE + 8, 128), scratch(PY, 128), pltpu.SemaphoreType.DMA],
        63,
        (10**6, 4 * 10**6),
    )(slot_of, held_head, held_head_old)
    packed, inner_in, outer_in = lax.optimization_barrier((packed, inner_in, outer_in))
    arrived = lax.all_to_all(
        packed.reshape(devices, PIECE, 1, 128), AXES, split_axis=0, concat_axis=0, tiled=True
    ).reshape(devices * PIECE, 128)

    offsets = (0, -count_y, count_y, -1, 1, count_y - 1, -count_y - 1, count_y + 1, -count_y + 1)
    bricks = own_index + jnp.array(offsets, jnp.int32)
    source = jnp.sum(
        jnp.where(block_map[None] == bricks[:, None, None], numbers[None, :, None], 0), axis=1
    )
    first, last = call(
        edge_ids_kernel, [f32(EX, 8, 128)] * 2, [VMEM] * 4, [VMEM] * 2, [], 8, (10**5, 10**6)
    )(inner, outer, inner_in, outer_in)
    y_low = lax.ppermute(last, "gy", up_y)
    y_high = lax.ppermute(first, "gy", down_y)
    *fields, edges = call(
        properties_kernel,
        [f32(EX, 128, 128)] * 7 + [f32(EX, 2, 8, 128)],
        [SMEM] * 4 + [VMEM] * 4,
        [HBM] * 8,
        [scratch(EX, 128, 128)] * 7 + [scratch(EX, 2, 8, 128), scratch(EX, 128, 128), scratch(EX, 136, 128)]
        + [pltpu.SemaphoreType.DMA((8,))],
        63,
        (40 * 10**6, 12 * 10**6),
    )(conductivity, vg_alpha, vg_n, capacity, inner, outer, inner_in, outer_in)

    kept, sums = call(
        main_kernel,
        [f32(4, 8, 128, 128), f32(devices, 128)],
        [SMEM] * 5 + [HBM] + [VMEM] * 3 + [HBM] * 7,
        [HBM, VMEM],
        [scratch(devices * PIECE + 8, 128)] + [scratch(EX, EY, 128)] * 5 + [scratch(EX, PY, 128), scratch(EX, EY, 128)]
        + [pltpu.SemaphoreType.DMA((12,)), scratch(128 * LAYER, 128)] + [scratch(EX, PY, 128)] * 16
        + [scratch(EX, 16, 128), scratch(EX, PY, 128)],
        63,
        (200 * 10**6, 16 * 10**6),
    )(source, conductivity, vg_alpha, vg_n, capacity, arrived, y_low, y_high, edges, *fields)
    gathered = lax.all_to_all(sums.reshape(devices, 1, 128), AXES, split_axis=0, concat_axis=0, tiled=True)
    turned = call(turn_back_kernel, f32(4, 1024, 128), [VMEM], VMEM, [], 8, (10**6, 4 * 10**6))(kept)
    update = call(finish_kernel, f32(1024, 128), [VMEM] * 2, VMEM, [], 8, (10**6, 3 * 10**6))(
        gathered.reshape(devices, 128), turned
    )
    return update.reshape(128, 8, 128)


def solution(mesh):
    return jax.shard_map(
        body,
        mesh=mesh,
        in_specs=(
            P(("gx", "gy"), None, None),
            P(("gx", "gy"), None, None),
            P(None, "gx", "gy"),
            P(),
            P(),
            P(),
            P(),
            P(),
        ),
        out_specs=P(None, "gx", "gy"),
        check_vma=False,
    )
```

```python
import jax
import jax.numpy as jnp
from jax import lax
from jax.experimental import pallas as pl
from jax.experimental.pallas import tpu as pltpu
from jax.sharding import PartitionSpec as P

MATERIALS = 16
STORE = 4.0
AXES = ("gx", "gy")

PIECE = 37
LAYER = 40
DEPTH = 5
EX = 8 + 2 * DEPTH
EY = 144
PY = 160
CHUNK = 24
CHUNKS = EY // CHUNK
PAIRS = [(i, j) for j in range(1, 5) for i in range(0, j + 1)]


def f32(*shape):
    return jax.ShapeDtypeStruct(shape, jnp.float32)


def params(mib):
    return pltpu.CompilerParams(vmem_limit_bytes=int(mib * 2**20))


VMEM = pl.BlockSpec(memory_space=pltpu.VMEM)
SMEM = pl.BlockSpec(memory_space=pltpu.SMEM)
HBM = pl.BlockSpec(memory_space=pltpu.HBM)


def iota(shape, axis):
    return lax.broadcasted_iota(jnp.int32, shape, axis)


def loop(count, body, unroll=1):
    def several(i, carry):
        for k in range(unroll):
            body(unroll * i + k)
        return carry

    lax.fori_loop(0, count // unroll, several, 0)


def pack_kernel(slot_of, head, old, packed, out, edge, sem):
    sub = iota((8, 128), 0)

    def brick(b):
        own = slot_of[0, b]
        below = slot_of[0, jnp.maximum(b - 8, 0)]
        above = slot_of[0, jnp.minimum(b + 8, 127)]
        head_below, head_above = head[below], head[above]
        old_below, old_above = old[below], old[above]

        def put(tile, value):
            out[pl.ds(b * PIECE + 8 * tile, 8), :] = value

        put(0, head[own])
        put(1, old[own])
        put(2, jnp.where(sub >= 3, head_below, head_above))
        put(3, jnp.where(sub < 3, old_above, jnp.where(sub < 5, head_above, old_below)))
        put(4, jnp.where(sub == 3, old_above, old_below))

    loop(128, brick, 8)
    lane = iota((128, 128), 1)
    low = lane % 16 < 8
    edge[0:16, :] = jnp.full((16, 128), -1.0, jnp.float32)
    edge[144:160, :] = jnp.full((16, 128), -1.0, jnp.float32)
    corners = []
    for field in range(2):
        columns = jnp.zeros((128, 128), jnp.float32)
        for x in range(8):
            rows = out[pl.ds(8 * field + x, 128, stride=PIECE), :]
            columns = jnp.where(lane // 16 == x, pltpu.roll(rows, 16 * x + 8, 1), columns)
        edge[16:144, :] = columns
        out[pl.ds(32 + field, 128, stride=PIECE), :] = jnp.where(low, edge[15:143, :], edge[17:145, :])
        corners.append(
            jnp.where(
                lane < 64,
                jnp.where(low, edge[23:151, :], edge[25:153, :]),
                jnp.where(low, edge[7:135, :], edge[9:137, :]),
            )
        )
    from_old = jnp.where(low, pltpu.roll(corners[1], 124, 1), pltpu.roll(corners[1], 4, 1))
    out[pl.ds(34, 128, stride=PIECE), :] = jnp.where((lane % 16 >= 4) & (lane % 16 < 12), corners[0], from_old)
    copy = pltpu.make_async_copy(out.at[0 : packed.shape[0]], packed, sem)
    copy.start()
    copy.wait()


def is_even():
    return lax.axis_index("gx") % 2 == 0


def turn_ids_kernel(block_map, ids, slot_of, inner, outer, turned):
    row = jnp.broadcast_to(block_map[pl.ds(lax.axis_index(AXES), 1), :], (128, 128))
    match = row == iota((128, 128), 0)
    slot = jnp.sum(jnp.where(match, iota((128, 128), 1), 0).astype(jnp.float32), axis=1, keepdims=True)
    slot_of[...] = jnp.broadcast_to(slot, (128, 128)).T[0:8].astype(jnp.int32)
    for x in range(8):
        turned[x] = ids[pl.ds(x, 128, stride=8), :].astype(jnp.float32).T
    first = jnp.where(is_even(), 8 - DEPTH, 0)
    for k in range(DEPTH):
        inner[k] = turned[first + k]
        outer[k] = turned[8 - DEPTH - first + k]


def id_rows(inner, outer, inner_in, outer_in):
    even = is_even()

    def read(k, low, high, at):
        return jnp.where(even, low[k, at, :], high[k, at, :])

    return (
        (0, DEPTH, lambda k, at: read(k, outer_in, inner_in, at)),
        (DEPTH, DEPTH, lambda k, at: read(k, outer, inner, at)),
        (2 * DEPTH, 8 - DEPTH, lambda k, at: read(k + 2 * DEPTH - 8, inner, outer, at)),
        (8 + DEPTH, DEPTH, lambda k, at: read(k, inner_in, outer_in, at)),
    )


def edge_ids_kernel(inner, outer, inner_in, outer_in, first, last):
    for start, count, read in id_rows(inner, outer, inner_in, outer_in):
        for k in range(count):
            first[start + k] = read(k, slice(0, 8))
            last[start + k] = read(k, slice(120, 128))


def tables_of(conductivity, vg_alpha, vg_n, capacity):
    lane = iota((8, 128), 1)
    reads = [
        lambda m: conductivity[0, m], lambda m: conductivity[1, m], lambda m: conductivity[2, m],
        lambda m: vg_alpha[m], lambda m: vg_n[m], lambda m: capacity[m],
    ]
    tables = []
    for read in reads:
        table = jnp.zeros((8, 128), jnp.float32)
        for m in range(MATERIALS):
            table = jnp.where(lane == m, read(m), table)
        tables.append(table)
    return tables


def lookup(tables, ids):
    index = ids.astype(jnp.int32)
    return [jnp.take_along_axis(table, index, axis=1) for table in tables]


def half_mean(a, b):
    return a * b / (a + b)


def upward_faces(kz):
    return jnp.where(iota(kz.shape, 1) < 127, half_mean(kz, pltpu.roll(kz, 127, 1)), 0.0)


def x_inside(xi):
    x = lax.axis_index("gx") * 8 - DEPTH + xi
    return jnp.where((x >= 0) & (x + 1 < lax.axis_size("gx") * 8), 1.0, 0.0)


def y_inside(shape, first):
    y = lax.axis_index("gy") * 128 - 8 + first + iota(shape, 0)
    return (y >= 0) & (y + 1 < lax.axis_size("gy") * 128)


def properties_kernel(
    conductivity, vg_alpha, vg_n, capacity, inner, outer, inner_in, outer_in,
    out_a, out_n, out_m, out_c, out_x, out_y, out_z, out_e,
    alpha, expo, exponent, cap, trans_x, trans_y, trans_z, edges, cond_x, cond_y, sems,
):
    def copies(first, last):
        made = (alpha, expo, exponent, cap, trans_x, trans_y, trans_z, edges)
        outs = (out_a, out_n, out_m, out_c, out_x, out_y, out_z, out_e)
        return [pltpu.make_async_copy(made[k], outs[k], sems.at[k]) for k in range(first, last)]

    tables = tables_of(conductivity, vg_alpha, vg_n, capacity)

    def fill_row(xi, read, k):
        for t in range(16):
            at = slice(8 * t, 8 * t + 8)
            kx, ky, kz, a, n, c = lookup(tables, read(k, at))
            alpha[xi, at, :] = a
            expo[xi, at, :] = n
            exponent[xi, at, :] = 1.0 - 1.0 / n
            cap[xi, at, :] = STORE * c
            cond_x[xi, at, :] = kx
            cond_y[xi, at, :] = ky
            trans_z[xi, at, :] = upward_faces(kz)
            if t in (0, 15):
                edges[xi, t // 15] = ky

    for start, count, read in id_rows(inner, outer, inner_in, outer_in):
        loop(count, lambda k: fill_row(start + k, read, k))
    for copy in copies(0, 4):
        copy.start()

    def faces(xi):
        inside = x_inside(xi)
        above_xi = jnp.minimum(xi + 1, EX - 1)
        for c in range(4):
            at = slice(32 * c, 32 * c + 32)
            trans_x[xi, at, :] = inside * half_mean(cond_x[xi, at, :], cond_x[above_xi, at, :])
            up = slice(32 * c + 1, 32 * c + 33)
            trans_y[xi, at, :] = half_mean(cond_y[xi, at, :], cond_y[xi, up, :])

    loop(EX, faces)
    for copy in copies(4, 8):
        copy.start()
    for copy in copies(0, 8):
        copy.wait()


def wetness(level, alpha, expo, exponent):
    power = jnp.exp(expo * jnp.log(alpha * -level))
    return power, -jnp.log(1.0 + power)


def retention(level, alpha, expo, exponent):
    log_scaled = expo * jnp.log(alpha * -level)
    power = jnp.exp(log_scaled)
    total = 1.0 + power
    inverse = 1.0 / total
    log_inverse = -jnp.log(total)
    root = jnp.exp(0.5 * exponent * log_inverse)
    saturation = root * root
    rest = power * inverse
    z = 1.0 / (1.0 + 2.0 * power)
    zz = z * z
    series = 1.0 / 15.0
    for k in (13.0, 11.0, 9.0, 7.0, 5.0, 3.0, 1.0):
        series = series * zz + 1.0 / k
    log_rest = jnp.where(power >= 1.0, -2.0 * z * series, log_scaled + log_inverse)
    e = exponent * log_rest
    rest_power = jnp.exp(e)
    taylor = 1.0 + e * (1.0 / 8.0)
    for k in (7.0, 6.0, 5.0, 4.0, 3.0, 2.0):
        taylor = 1.0 + (e * (1.0 / k)) * taylor
    inner = jnp.where(e > -0.35, -e * taylor, 1.0 - rest_power)
    relperm = root * inner * inner
    rate = (expo - 1.0) / -level
    d_sat = saturation * rest * rate
    d_rel = root * inner * rate * (0.5 * inner * rest + 2.0 * inverse * rest_power)
    return saturation, relperm, d_sat, d_rel


def split(a, factor):
    c = a * factor
    high = c - (c - a)
    return high, a - high


def two_sum(a, b):
    s = a + b
    t = s - a
    return s, (a - (s - t)) + (b - t)


def df_add(a, b):
    s, e = two_sum(a[0], b[0])
    e = e + (a[1] + b[1])
    t = s + e
    return t, e - (t - s)


def df_mul(a, b):
    ah, al = split(a[0], 4097.0)
    bh, bl = split(b[0], 4097.0)
    p = a[0] * b[0]
    e = ((ah * bh - p) + ah * bl + al * bh) + al * bl
    e = e + (a[0] * b[1] + a[1] * b[0])
    t = p + e
    return t, e - (t - p)


def df_neg(a):
    return -a[0], -a[1]


def df_div(a, b):
    q = a[0] / b[0]
    zero = jnp.zeros_like(q)
    r = df_add(a, df_neg(df_mul((q, zero), b)))
    return two_sum(q, r[0] / b[0])


def main_kernel(
    source, conductivity, vg_alpha, vg_n, capacity,
    arrived, y_low, y_high, edges, in_a, in_n, in_m, in_c, in_x, in_y, in_z, kept, sums,
    recv, alpha, expo, exponent, cap, trans_x, trans_y, trans_z, sems, ordered, head, old, rel, d_rel, own_c, cxp, cxm, cyp, cym, czp, czm, k0, k1, k2, k3, k4,
    side_x, side_y,
):
    sub = iota((8, 128), 0)
    lane = iota((8, 128), 1)
    refs = (
        (in_a, alpha), (in_n, expo), (in_m, exponent), (in_c, cap),
        (in_x, trans_x), (in_y, trans_y), (in_z, trans_z),
    )
    copies = [
        pltpu.make_async_copy(a, b.at[:, 16:144] if b is trans_y else b.at[:, 8:136], sems.at[k])
        for k, (a, b) in enumerate(refs)
    ]
    arrival = pltpu.make_async_copy(arrived, recv.at[0 : arrived.shape[0]], sems.at[11])
    arrival.start()
    for copy in copies:
        copy.start()

    low = lane % 16 < 8

    tables = tables_of(conductivity, vg_alpha, vg_n, capacity)

    def side_rows(xi):
        for source_ids, at in ((y_low, slice(0, 8)), (y_high, slice(136, 144))):
            to = slice(at.start + 8, at.stop + 8)
            kx, ky, kz, a, n, c = lookup(tables, source_ids[xi])
            alpha[xi, at, :] = a
            expo[xi, at, :] = n
            exponent[xi, at, :] = 1.0 - 1.0 / n
            cap[xi, at, :] = STORE * c
            trans_z[xi, at, :] = upward_faces(kz)
            side_x[xi, at.start // 17 : at.start // 17 + 8, :] = kx
            side_y[xi, to, :] = ky
        side_y[xi, 16:24, :] = edges[xi, 0]
        side_y[xi, 136:144, :] = edges[xi, 1]

    loop(EX, side_rows, 3)
    arrival.wait()

    def layer(z):
        def tile(k, t):
            return recv[pl.ds(source[k, z] * PIECE + 8 * t, 8), :]

        def put(t, value):
            ordered[pl.ds(pl.multiple_of(z * LAYER + 8 * t, 8), 8), :] = value

        put(0, tile(0, 0))
        put(1, tile(0, 1))
        put(2, jnp.where(sub >= 3, tile(1, 2), tile(2, 2)))
        put(3, jnp.where(sub < 5, tile(2, 3), tile(1, 3)))
        sides = jnp.where(low, tile(3, 4), tile(4, 4))
        corners = jnp.where(
            lane < 64, jnp.where(low, tile(5, 4), tile(7, 4)), jnp.where(low, tile(6, 4), tile(8, 4))
        )
        put(
            4,
            jnp.where(
                sub < 2, sides, jnp.where(sub == 3, tile(2, 4), jnp.where(sub == 4, tile(1, 4), corners))
            ),
        )

    loop(128, layer, 4)

    def plane(r):
        return ordered[pl.ds(r, 128, stride=LAYER), :].T

    for xi, r in enumerate([19, 20, 21, 22, 23] + list(range(8)) + [16, 17, 18, 27, 28]):
        head[xi, 16:144, :] = plane(r)
    for xi, r in enumerate([36, 29, 30, 31] + list(range(8, 16)) + [24, 25, 26, 35]):
        old[xi + 1, 16:144, :] = plane(r)
    corners = plane(34)
    for field, y_row in ((head, 32), (old, 33)):
        sides = plane(y_row)
        for x in range(8):
            field[5 + x, 8:16, :] = sides[16 * x : 16 * x + 8]
            field[5 + x, 144:152, :] = sides[16 * x + 8 : 16 * x + 16]
        for x in range(8):
            xi = 13 + x if x < 4 else x - 3
            beside = (corners[16 * x : 16 * x + 8], corners[16 * x + 8 : 16 * x + 16])
            if field is old:
                beside = [pltpu.roll(tile, 4, 0) for tile in beside]
            field[xi, 8:16, :], field[xi, 144:152, :] = beside
    for xi in (0, 17):
        head[xi, 8:16, :] = jnp.full((8, 128), -1.0, jnp.float32)
        head[xi, 144:152, :] = jnp.full((8, 128), -1.0, jnp.float32)

    def curves(xi):
        for c in range(CHUNKS):
            at = slice(CHUNK * c, CHUNK * (c + 1))
            to = slice(8 + CHUNK * c, 8 + CHUNK * (c + 1))
            sat_v, rel_v, dsat_v, drel_v = retention(
                head[xi, to, :], alpha[xi, at, :], expo[xi, at, :], exponent[xi, at, :]
            )
            k0[xi, to, :] = sat_v
            rel[xi, to, :] = rel_v
            d_rel[xi, to, :] = drel_v
            own_c[xi, to, :] = cap[xi, at, :] * dsat_v

    for copy in copies[:4]:
        copy.wait()
    loop(EX, curves, 2)
    for copy in copies[4:]:
        copy.wait()

    def side_faces(xi):
        pair = x_inside(xi) * half_mean(side_x[xi], side_x[jnp.minimum(xi + 1, EX - 1)])
        trans_x[xi, 0:8, :] = pair[0:8]
        trans_x[xi, 136:144, :] = pair[8:16]
        for first, last in ((8, 16), (136, 152)):
            here = slice(first, last)
            value = half_mean(side_y[xi, here, :], side_y[xi, first + 1 : last + 1, :])
            trans_y[xi, here, :] = jnp.where(y_inside(value.shape, first - 8), value, 0.0)

    loop(EX, side_faces, 3)

    def face(half, low, high, rise):
        (h_a, r_a, d_a), (h_b, r_b, d_b) = low, high
        potential = h_b - h_a
        if rise:
            potential = potential + rise
        along = half * (r_a + r_b)
        slope = half * potential
        return along + slope * d_b, along - slope * d_a, along * potential, slope * (d_a + d_b)

    def coefficients(i):
        xi = i + 1
        for c in range(CHUNKS):
            at = slice(CHUNK * c, CHUNK * (c + 1))
            to = slice(8 + CHUNK * c, 8 + CHUNK * (c + 1))
            up = slice(9 + CHUNK * c, 9 + CHUNK * (c + 1))
            down = slice(7 + CHUNK * c, 7 + CHUNK * (c + 1))
            _, log_old = wetness(old[xi, to, :], alpha[xi, at, :], expo[xi, at, :], exponent[xi, at, :])
            old_sat = jnp.exp(exponent[xi, at, :] * log_old)
            start = cap[xi, at, :] * (old_sat - k0[xi, to, :])
            centre = own_c[xi, to, :]
            here = [f[xi, to, :] for f in (head, rel, d_rel)]
            above_x = [f[xi + 1, to, :] for f in (head, rel, d_rel)]
            below_x = [f[xi - 1, to, :] for f in (head, rel, d_rel)]
            above_y = [f[xi, up, :] for f in (head, rel, d_rel)]
            below_y = [f[xi, down, :] for f in (head, rel, d_rel)]
            half_z = trans_z[xi, at, :]
            above_z = [pltpu.roll(f, 127, 1) for f in here]
            below_z = [pltpu.roll(f, 1, 1) for f in here]
            for c_up, c_down, half_up, half_down, above, below, rise in (
                (cxp, cxm, trans_x[xi, at, :], trans_x[xi - 1, at, :], above_x, below_x, 0.0),
                (cyp, cym, trans_y[xi, to, :], trans_y[xi, down, :], above_y, below_y, 0.0),
                (czp, czm, half_z, pltpu.roll(half_z, 1, 1), above_z, below_z, 1.0),
            ):
                c_p, _, flux, both = face(half_up, here, above, rise)
                _, c_m, flux_m, both_m = face(half_down, below, here, rise)
                c_up[xi, to, :] = c_p
                c_down[xi, to, :] = c_m
                start = start + (flux - flux_m)
                centre = centre - (both - both_m)
            own_c[xi, to, :] = centre
            k0[xi, to, :] = start

    loop(16, coefficients, 4)

    vectors = (k0, k1, k2, k3, k4)
    for step in range(4):
        v_ref, w_ref = vectors[step], vectors[step + 1]

        def apply(i):
            xi = i + 2 + step
            for c in range(CHUNKS):
                to = slice(8 + CHUNK * c, 8 + CHUNK * (c + 1))
                up = slice(9 + CHUNK * c, 9 + CHUNK * (c + 1))
                down = slice(7 + CHUNK * c, 7 + CHUNK * (c + 1))
                v = v_ref[xi, to, :]
                w = own_c[xi, to, :] * v
                w = w + cxp[xi, to, :] * (v - v_ref[xi + 1, to, :])
                w = w + cxm[xi, to, :] * (v - v_ref[xi - 1, to, :])
                w = w + cyp[xi, to, :] * (v - v_ref[xi, up, :])
                w = w + cym[xi, to, :] * (v - v_ref[xi, down, :])
                w = w + czp[xi, to, :] * (v - pltpu.roll(v, 127, 1))
                w = w + czm[xi, to, :] * (v - pltpu.roll(v, 1, 1))
                w_ref[xi, to, :] = w

        loop(14 - 2 * step, apply, 7 - step)

    keeps = [
        pltpu.make_async_copy(vectors[k].at[5:13, 16:144, :], kept.at[k], sems.at[7 + k]) for k in range(4)
    ]
    for copy in keeps:
        copy.start()

    def largest(i, tops):
        xi = 5 + i
        for c in range(16):
            at = slice(16 + 8 * c, 24 + 8 * c)
            tops = [jnp.maximum(top, jnp.abs(v[xi, at, :])) for top, v in zip(tops, vectors)]
        return tops

    tops = lax.fori_loop(0, 8, largest, [jnp.zeros((8, 128), jnp.float32) for _ in range(5)])
    scales, inverses = [], []
    for top in tops:
        top = jnp.broadcast_to(jnp.max(top, keepdims=True), (8, 128))
        scale = jnp.full((8, 128), 2.0**96, jnp.float32)
        inverse = jnp.full((8, 128), 2.0**-96, jnp.float32)
        for j in range(-5, 7):
            over = top >= 2.0 ** (16 * j - 8)
            scale = jnp.where(over, 2.0 ** (-16 * j), scale)
            inverse = jnp.where(over, 2.0 ** (16 * j), inverse)
        scales.append(scale)
        inverses.append(inverse)

    def products(i, totals):
        leading, rest = totals
        xi = 5 + i // 8
        first = 16 + 16 * (i % 8)
        for k in range(2):
            at = pl.ds(pl.multiple_of(first + 8 * k, 8), 8)
            values = [v[xi, at, :] * scale for v, scale in zip(vectors, scales)]
            halves = [split(value, 65537.0) for value in values]
            leading, rest = list(leading), list(rest)
            for e, (p, q) in enumerate(PAIRS):
                leading[e], lost = two_sum(leading[e], halves[p][0] * halves[q][0])
                rest[e] = rest[e] + ((halves[p][0] * halves[q][1] + halves[p][1] * values[q]) + lost)
        return leading, rest

    zeros = [jnp.zeros((8, 128), jnp.float32) for _ in PAIRS]
    leading, rest = lax.fori_loop(0, 64, products, (zeros, list(zeros)))
    groups = []
    for g in range(2):
        high = jnp.zeros((8, 128), jnp.float32)
        low = jnp.zeros((8, 128), jnp.float32)
        for e in range(8 * g, min(8 * g + 8, len(PAIRS))):
            pair = two_sum(leading[e], rest[e])
            for shift in (4, 2, 1):
                pair = df_add(pair, (pltpu.roll(pair[0], shift, 0), pltpu.roll(pair[1], shift, 0)))
            high = jnp.where(sub == e - 8 * g, pair[0], high)
            low = jnp.where(sub == e - 8 * g, pair[1], low)
        pair = (high, low)
        for shift in (64, 32, 16, 8, 4, 2, 1):
            pair = df_add(pair, (pltpu.roll(pair[0], shift, 1), pltpu.roll(pair[1], shift, 1)))
        groups.append(pair)
    line = jnp.zeros((8, 128), jnp.float32)
    for e in range(len(PAIRS)):
        pair = groups[e // 8]
        for half in range(2):
            line = jnp.where(lane == 16 * half + e, pair[half][e % 8 : e % 8 + 1, :], line)
    for k in range(5):
        line = jnp.where(lane == 32 + k, inverses[k], line)
        line = jnp.where(lane == 40 + k, scales[k], line)
    for t in range(16):
        sums[8 * t : 8 * t + 8, :] = line

    for copy in keeps:
        copy.wait()


def turn_back_kernel(kept, out):
    for k in range(4):
        for x in range(8):
            out[k, pl.ds(x, 128, stride=8), :] = kept[k, x].T


def finish_kernel(recv, vectors, out):
    data = recv[...]
    lane = iota((128, 128), 1)
    smallest = jnp.min(data, axis=0, keepdims=True)
    factor = data * jnp.broadcast_to(pltpu.roll(jnp.broadcast_to(smallest, (8, 128)), 120, 1)[0:1], (128, 128))
    left = jnp.zeros((128, 128), jnp.float32)
    right = jnp.zeros((128, 128), jnp.float32)
    for k in range(5):
        column = jnp.broadcast_to(factor[:, 32 + k : 33 + k], (128, 128))
        for e, (p, q) in enumerate(PAIRS):
            if p == k:
                left = jnp.where(lane % 16 == e, column, left)
            if q == k:
                right = jnp.where(lane % 16 == e, column, right)
    scaled = data * left * right
    low = pltpu.roll(scaled, 112, 1)
    pair = (scaled[0:8], low[0:8])
    for t in range(1, 16):
        pair = df_add(pair, (scaled[8 * t : 8 * t + 8], low[8 * t : 8 * t + 8]))
    for shift in (4, 2, 1):
        pair = df_add(pair, (pltpu.roll(pair[0], shift, 0), pltpu.roll(pair[1], shift, 0)))
    entry = {}
    for e, (p, q) in enumerate(PAIRS):
        entry[p, q] = tuple(jnp.broadcast_to(half[:, e : e + 1], (8, 128)) for half in pair)

    def scale_of(k):
        return jnp.broadcast_to(smallest[:, k : k + 1], (8, 128))

    rows = {(i, j): entry[i + 1, j + 1] for i in range(4) for j in range(i, 4)}
    right_side = [entry[0, j + 1] for j in range(4)]
    for k in range(4):
        for i in range(k + 1, 4):
            ratio = df_neg(df_div(rows[k, i], rows[k, k]))
            for j in range(i, 4):
                rows[i, j] = df_add(rows[i, j], df_mul(ratio, rows[k, j]))
            right_side[i] = df_add(right_side[i], df_mul(ratio, right_side[k]))
    coeffs = [None] * 4
    for k in reversed(range(4)):
        running = right_side[k]
        for j in range(k + 1, 4):
            running = df_add(running, df_neg(df_mul(rows[k, j], coeffs[j])))
        coeffs[k] = df_div(running, rows[k, k])
    inverse_first = jnp.max(jnp.where(lane == 32, data, 0.0), axis=0, keepdims=True)
    inverse_first = jnp.broadcast_to(jnp.max(inverse_first, axis=1, keepdims=True), (8, 128))
    weights = [(coeffs[k][0] * scale_of(41 + k)) * inverse_first for k in range(4)]

    def rows_of(t):
        for k in range(4):
            at = pl.ds(pl.multiple_of(32 * t + 8 * k, 8), 8)
            total = weights[0] * vectors[0, at, :]
            for j in range(1, 4):
                total = total + weights[j] * vectors[j, at, :]
            out[at, :] = total

    loop(32, rows_of)


def call(kernel, out_shape, in_specs, out_specs, scratch, mib, cost):
    return pl.pallas_call(
        kernel,
        out_shape=out_shape,
        in_specs=in_specs,
        out_specs=out_specs,
        scratch_shapes=scratch,
        compiler_params=params(mib),
        cost_estimate=pl.CostEstimate(flops=cost[0], bytes_accessed=cost[1], transcendentals=0),
    )


def body(held_head, held_head_old, material_ids, block_map, conductivity, vg_alpha, vg_n, capacity):
    count_x, count_y = lax.axis_size("gx"), lax.axis_size("gy")
    devices = count_x * count_y
    own_index = lax.axis_index(AXES)
    numbers = jnp.arange(devices, dtype=jnp.int32)
    scratch = lambda *shape: pltpu.VMEM(shape, jnp.float32)

    beside = [(i, i ^ 1) for i in range(count_x)]
    across = [pair for i in range(1, count_x - 1, 2) for pair in ((i, i + 1), (i + 1, i))]
    up_y = [(i, i + 1) for i in range(count_y - 1)]
    down_y = [(i + 1, i) for i in range(count_y - 1)]
    slot_of, inner, outer = call(
        turn_ids_kernel,
        [jax.ShapeDtypeStruct((8, 128), jnp.int32)] + [f32(DEPTH, 128, 128)] * 2,
        [VMEM, VMEM],
        [VMEM] * 3,
        [scratch(8, 128, 128)],
        63,
        (10**6, 10**6),
    )(block_map, material_ids.reshape(1024, 128))
    outer_in = lax.ppermute(outer, "gx", across)
    inner_in = lax.ppermute(inner, "gx", beside)

    packed = call(
        pack_kernel,
        f32(devices * PIECE, 128),
        [SMEM, VMEM, VMEM],
        HBM,
        [scratch(devices * PIECE + 8, 128), scratch(PY, 128), pltpu.SemaphoreType.DMA],
        63.75,
        (10**6, 4 * 10**6),
    )(slot_of, held_head, held_head_old)
    packed, inner_in, outer_in = lax.optimization_barrier((packed, inner_in, outer_in))
    arrived = lax.all_to_all(
        packed.reshape(devices, PIECE, 1, 128), AXES, split_axis=0, concat_axis=0, tiled=True
    ).reshape(devices * PIECE, 128)

    offsets = (0, -count_y, count_y, -1, 1, count_y - 1, -count_y - 1, count_y + 1, -count_y + 1)
    bricks = own_index + jnp.array(offsets, jnp.int32)
    source = jnp.sum(
        jnp.where(block_map[None] == bricks[:, None, None], numbers[None, :, None], 0), axis=1
    )
    first, last = call(
        edge_ids_kernel, [f32(EX, 8, 128)] * 2, [VMEM] * 4, [VMEM] * 2, [], 8, (10**5, 10**6)
    )(inner, outer, inner_in, outer_in)
    y_low = lax.ppermute(last, "gy", up_y)
    y_high = lax.ppermute(first, "gy", down_y)
    *fields, edges = call(
        properties_kernel,
        [f32(EX, 128, 128)] * 7 + [f32(EX, 2, 8, 128)],
        [SMEM] * 4 + [VMEM] * 4,
        [HBM] * 8,
        [scratch(EX, 128, 128)] * 7 + [scratch(EX, 2, 8, 128), scratch(EX, 128, 128), scratch(EX, 136, 128)]
        + [pltpu.SemaphoreType.DMA((8,))],
        63,
        (40 * 10**6, 12 * 10**6),
    )(conductivity, vg_alpha, vg_n, capacity, inner, outer, inner_in, outer_in)

    kept, sums = call(
        main_kernel,
        [f32(4, 8, 128, 128), f32(devices, 128)],
        [SMEM] * 5 + [HBM] + [VMEM] * 3 + [HBM] * 7,
        [HBM, VMEM],
        [scratch(devices * PIECE + 8, 128)] + [scratch(EX, EY, 128)] * 5 + [scratch(EX, PY, 128), scratch(EX, EY, 128)]
        + [pltpu.SemaphoreType.DMA((12,)), scratch(128 * LAYER, 128)] + [scratch(EX, PY, 128)] * 16
        + [scratch(EX, 16, 128), scratch(EX, PY, 128)],
        63,
        (200 * 10**6, 16 * 10**6),
    )(source, conductivity, vg_alpha, vg_n, capacity, arrived, y_low, y_high, edges, *fields)
    gathered = lax.all_to_all(sums.reshape(devices, 1, 128), AXES, split_axis=0, concat_axis=0, tiled=True)
    turned = call(turn_back_kernel, f32(4, 1024, 128), [VMEM], VMEM, [], 8, (10**6, 4 * 10**6))(kept)
    update = call(finish_kernel, f32(1024, 128), [VMEM] * 2, VMEM, [], 8, (10**6, 3 * 10**6))(
        gathered.reshape(devices, 128), turned
    )
    return update.reshape(128, 8, 128)


def solution(mesh):
    return jax.shard_map(
        body,
        mesh=mesh,
        in_specs=(
            P(("gx", "gy"), None, None),
            P(("gx", "gy"), None, None),
            P(None, "gx", "gy"),
            P(),
            P(),
            P(),
            P(),
            P(),
        ),
        out_specs=P(None, "gx", "gy"),
        check_vma=False,
    )
```

```python
import jax
import jax.numpy as jnp
from jax import lax
from jax.experimental import pallas as pl
from jax.experimental.pallas import tpu as pltpu
from jax.sharding import PartitionSpec as P

MATERIALS = 16
STORE = 4.0
AXES = ("gx", "gy")

PIECE = 37
LAYER = 40
DEPTH = 5
EX = 8 + 2 * DEPTH
EY = 144
PY = 160
CHUNK = 24
CHUNKS = EY // CHUNK
PAIRS = [(i, j) for j in range(1, 5) for i in range(0, j + 1)]


def f32(*shape):
    return jax.ShapeDtypeStruct(shape, jnp.float32)


def params(mib):
    return pltpu.CompilerParams(vmem_limit_bytes=int(mib * 2**20))


VMEM = pl.BlockSpec(memory_space=pltpu.VMEM)
SMEM = pl.BlockSpec(memory_space=pltpu.SMEM)
HBM = pl.BlockSpec(memory_space=pltpu.HBM)


def iota(shape, axis):
    return lax.broadcasted_iota(jnp.int32, shape, axis)


def loop(count, body, unroll=1):
    def several(i, carry):
        for k in range(unroll):
            body(unroll * i + k)
        return carry

    lax.fori_loop(0, count // unroll, several, 0)


def pack_kernel(slot_of, head, old, packed, out, edge, sem):
    sub = iota((8, 128), 0)

    def brick(b):
        own = slot_of[0, b]
        below = slot_of[0, jnp.maximum(b - 8, 0)]
        above = slot_of[0, jnp.minimum(b + 8, 127)]
        head_below, head_above = head[below], head[above]
        old_below, old_above = old[below], old[above]

        def put(tile, value):
            out[pl.ds(b * PIECE + 8 * tile, 8), :] = value

        put(0, head[own])
        put(1, old[own])
        put(2, jnp.where(sub >= 3, head_below, head_above))
        put(3, jnp.where(sub < 3, old_above, jnp.where(sub < 5, head_above, old_below)))
        put(4, jnp.where(sub == 3, old_above, old_below))

    loop(128, brick, 8)
    lane = iota((128, 128), 1)
    low = lane % 16 < 8
    edge[0:16, :] = jnp.full((16, 128), -1.0, jnp.float32)
    edge[144:160, :] = jnp.full((16, 128), -1.0, jnp.float32)
    corners = []
    for field in range(2):
        columns = jnp.zeros((128, 128), jnp.float32)
        for x in range(8):
            rows = out[pl.ds(8 * field + x, 128, stride=PIECE), :]
            columns = jnp.where(lane // 16 == x, pltpu.roll(rows, 16 * x + 8, 1), columns)
        edge[16:144, :] = columns
        out[pl.ds(32 + field, 128, stride=PIECE), :] = jnp.where(low, edge[15:143, :], edge[17:145, :])
        corners.append(
            jnp.where(
                lane < 64,
                jnp.where(low, edge[23:151, :], edge[25:153, :]),
                jnp.where(low, edge[7:135, :], edge[9:137, :]),
            )
        )
    from_old = jnp.where(low, pltpu.roll(corners[1], 124, 1), pltpu.roll(corners[1], 4, 1))
    out[pl.ds(34, 128, stride=PIECE), :] = jnp.where((lane % 16 >= 4) & (lane % 16 < 12), corners[0], from_old)
    copy = pltpu.make_async_copy(out.at[0 : packed.shape[0]], packed, sem)
    copy.start()
    copy.wait()


def is_even():
    return lax.axis_index("gx") % 2 == 0


def turn_ids_kernel(block_map, ids, slot_of, inner, outer, turned):
    row = jnp.broadcast_to(block_map[pl.ds(lax.axis_index(AXES), 1), :], (128, 128))
    match = row == iota((128, 128), 0)
    slot = jnp.sum(jnp.where(match, iota((128, 128), 1), 0).astype(jnp.float32), axis=1, keepdims=True)
    slot_of[...] = jnp.broadcast_to(slot, (128, 128)).T[0:8].astype(jnp.int32)
    for x in range(8):
        turned[x] = ids[pl.ds(x, 128, stride=8), :].astype(jnp.float32).T
    first = jnp.where(is_even(), 8 - DEPTH, 0)
    for k in range(DEPTH):
        inner[k] = turned[first + k]
        outer[k] = turned[8 - DEPTH - first + k]


def id_rows(inner, outer, inner_in, outer_in):
    even = is_even()

    def read(k, low, high, at):
        return jnp.where(even, low[k, at, :], high[k, at, :])

    return (
        (0, DEPTH, lambda k, at: read(k, outer_in, inner_in, at)),
        (DEPTH, DEPTH, lambda k, at: read(k, outer, inner, at)),
        (2 * DEPTH, 8 - DEPTH, lambda k, at: read(k + 2 * DEPTH - 8, inner, outer, at)),
        (8 + DEPTH, DEPTH, lambda k, at: read(k, inner_in, outer_in, at)),
    )


def edge_ids_kernel(inner, outer, inner_in, outer_in, first, last):
    for start, count, read in id_rows(inner, outer, inner_in, outer_in):
        for k in range(count):
            first[start + k] = read(k, slice(0, 8))
            last[start + k] = read(k, slice(120, 128))


def tables_of(conductivity, vg_alpha, vg_n, capacity):
    lane = iota((8, 128), 1)
    reads = [
        lambda m: conductivity[0, m], lambda m: conductivity[1, m], lambda m: conductivity[2, m],
        lambda m: vg_alpha[m], lambda m: vg_n[m], lambda m: capacity[m],
    ]
    tables = []
    for read in reads:
        table = jnp.zeros((8, 128), jnp.float32)
        for m in range(MATERIALS):
            table = jnp.where(lane == m, read(m), table)
        tables.append(table)
    return tables


def lookup(tables, ids):
    index = ids.astype(jnp.int32)
    return [jnp.take_along_axis(table, index, axis=1) for table in tables]


def half_mean(a, b):
    return a * b / (a + b)


def upward_faces(kz):
    return jnp.where(iota(kz.shape, 1) < 127, half_mean(kz, pltpu.roll(kz, 127, 1)), 0.0)


def x_inside(xi):
    x = lax.axis_index("gx") * 8 - DEPTH + xi
    return jnp.where((x >= 0) & (x + 1 < lax.axis_size("gx") * 8), 1.0, 0.0)


def y_inside(shape, first):
    y = lax.axis_index("gy") * 128 - 8 + first + iota(shape, 0)
    return (y >= 0) & (y + 1 < lax.axis_size("gy") * 128)


def properties_kernel(
    conductivity, vg_alpha, vg_n, capacity, inner, outer, inner_in, outer_in,
    out_a, out_n, out_m, out_c, out_x, out_y, out_z, out_e,
    alpha, expo, exponent, cap, trans_x, trans_y, trans_z, edges, cond_x, cond_y, sems,
):
    def copies(first, last):
        made = (alpha, expo, exponent, cap, trans_x, trans_y, trans_z, edges)
        outs = (out_a, out_n, out_m, out_c, out_x, out_y, out_z, out_e)
        return [pltpu.make_async_copy(made[k], outs[k], sems.at[k]) for k in range(first, last)]

    tables = tables_of(conductivity, vg_alpha, vg_n, capacity)

    def fill_row(xi, read, k):
        for t in range(16):
            at = slice(8 * t, 8 * t + 8)
            kx, ky, kz, a, n, c = lookup(tables, read(k, at))
            alpha[xi, at, :] = a
            expo[xi, at, :] = n
            exponent[xi, at, :] = 1.0 - 1.0 / n
            cap[xi, at, :] = STORE * c
            cond_x[xi, at, :] = kx
            cond_y[xi, at, :] = ky
            trans_z[xi, at, :] = upward_faces(kz)
            if t in (0, 15):
                edges[xi, t // 15] = ky

    for start, count, read in id_rows(inner, outer, inner_in, outer_in):
        loop(count, lambda k: fill_row(start + k, read, k))
    for copy in copies(0, 4):
        copy.start()

    def faces(xi):
        inside = x_inside(xi)
        above_xi = jnp.minimum(xi + 1, EX - 1)
        for c in range(4):
            at = slice(32 * c, 32 * c + 32)
            trans_x[xi, at, :] = inside * half_mean(cond_x[xi, at, :], cond_x[above_xi, at, :])
            up = slice(32 * c + 1, 32 * c + 33)
            trans_y[xi, at, :] = half_mean(cond_y[xi, at, :], cond_y[xi, up, :])

    loop(EX, faces)
    for copy in copies(4, 8):
        copy.start()
    for copy in copies(0, 8):
        copy.wait()


def wetness(level, alpha, expo, exponent):
    power = jnp.exp(expo * jnp.log(alpha * -level))
    return power, -jnp.log(1.0 + power)


def retention(level, alpha, expo, exponent):
    log_scaled = expo * jnp.log(alpha * -level)
    power = jnp.exp(log_scaled)
    total = 1.0 + power
    inverse = 1.0 / total
    log_inverse = -jnp.log(total)
    root = jnp.exp(0.5 * exponent * log_inverse)
    saturation = root * root
    rest = power * inverse
    z = 1.0 / (1.0 + 2.0 * power)
    zz = z * z
    series = 1.0 / 15.0
    for k in (13.0, 11.0, 9.0, 7.0, 5.0, 3.0, 1.0):
        series = series * zz + 1.0 / k
    log_rest = jnp.where(power >= 1.0, -2.0 * z * series, log_scaled + log_inverse)
    e = exponent * log_rest
    rest_power = jnp.exp(e)
    taylor = 1.0 + e * (1.0 / 8.0)
    for k in (7.0, 6.0, 5.0, 4.0, 3.0, 2.0):
        taylor = 1.0 + (e * (1.0 / k)) * taylor
    inner = jnp.where(e > -0.35, -e * taylor, 1.0 - rest_power)
    relperm = root * inner * inner
    rate = (expo - 1.0) / -level
    d_sat = saturation * rest * rate
    d_rel = root * inner * rate * (0.5 * inner * rest + 2.0 * inverse * rest_power)
    return saturation, relperm, d_sat, d_rel


def split(a, factor):
    c = a * factor
    high = c - (c - a)
    return high, a - high


def two_sum(a, b):
    s = a + b
    t = s - a
    return s, (a - (s - t)) + (b - t)


def df_add(a, b):
    s, e = two_sum(a[0], b[0])
    e = e + (a[1] + b[1])
    t = s + e
    return t, e - (t - s)


def df_mul(a, b):
    ah, al = split(a[0], 4097.0)
    bh, bl = split(b[0], 4097.0)
    p = a[0] * b[0]
    e = ((ah * bh - p) + ah * bl + al * bh) + al * bl
    e = e + (a[0] * b[1] + a[1] * b[0])
    t = p + e
    return t, e - (t - p)


def df_neg(a):
    return -a[0], -a[1]


def df_div(a, b):
    q = a[0] / b[0]
    zero = jnp.zeros_like(q)
    r = df_add(a, df_neg(df_mul((q, zero), b)))
    return two_sum(q, r[0] / b[0])


def main_kernel(
    source, conductivity, vg_alpha, vg_n, capacity,
    arrived, y_low, y_high, edges, in_a, in_n, in_m, in_c, in_x, in_y, in_z, kept, sums,
    recv, alpha, expo, exponent, cap, trans_x, trans_y, trans_z, sems, ordered, head, old, rel, d_rel, own_c, cxp, cxm, cyp, cym, czp, czm, k0, k1, k2, k3, k4,
    side_x, side_y,
):
    sub = iota((8, 128), 0)
    lane = iota((8, 128), 1)
    refs = (
        (in_a, alpha), (in_n, expo), (in_m, exponent), (in_c, cap),
        (in_x, trans_x), (in_y, trans_y), (in_z, trans_z),
    )
    copies = [
        pltpu.make_async_copy(a, b.at[:, 16:144] if b is trans_y else b.at[:, 8:136], sems.at[k])
        for k, (a, b) in enumerate(refs)
    ]
    arrival = pltpu.make_async_copy(arrived, recv.at[0 : arrived.shape[0]], sems.at[11])
    arrival.start()
    for copy in copies:
        copy.start()

    low = lane % 16 < 8

    tables = tables_of(conductivity, vg_alpha, vg_n, capacity)

    def side_rows(xi):
        for source_ids, at in ((y_low, slice(0, 8)), (y_high, slice(136, 144))):
            to = slice(at.start + 8, at.stop + 8)
            kx, ky, kz, a, n, c = lookup(tables, source_ids[xi])
            alpha[xi, at, :] = a
            expo[xi, at, :] = n
            exponent[xi, at, :] = 1.0 - 1.0 / n
            cap[xi, at, :] = STORE * c
            trans_z[xi, at, :] = upward_faces(kz)
            side_x[xi, at.start // 17 : at.start // 17 + 8, :] = kx
            side_y[xi, to, :] = ky
        side_y[xi, 16:24, :] = edges[xi, 0]
        side_y[xi, 136:144, :] = edges[xi, 1]

    loop(EX, side_rows, 3)
    arrival.wait()

    def layer(z):
        def tile(k, t):
            return recv[pl.ds(source[k, z] * PIECE + 8 * t, 8), :]

        def put(t, value):
            ordered[pl.ds(pl.multiple_of(z * LAYER + 8 * t, 8), 8), :] = value

        put(0, tile(0, 0))
        put(1, tile(0, 1))
        put(2, jnp.where(sub >= 3, tile(1, 2), tile(2, 2)))
        put(3, jnp.where(sub < 5, tile(2, 3), tile(1, 3)))
        sides = jnp.where(low, tile(3, 4), tile(4, 4))
        corners = jnp.where(
            lane < 64, jnp.where(low, tile(5, 4), tile(7, 4)), jnp.where(low, tile(6, 4), tile(8, 4))
        )
        put(
            4,
            jnp.where(
                sub < 2, sides, jnp.where(sub == 3, tile(2, 4), jnp.where(sub == 4, tile(1, 4), corners))
            ),
        )

    loop(128, layer, 8)

    def plane(r):
        return ordered[pl.ds(r, 128, stride=LAYER), :].T

    for xi, r in enumerate([19, 20, 21, 22, 23] + list(range(8)) + [16, 17, 18, 27, 28]):
        head[xi, 16:144, :] = plane(r)
    for xi, r in enumerate([36, 29, 30, 31] + list(range(8, 16)) + [24, 25, 26, 35]):
        old[xi + 1, 16:144, :] = plane(r)
    corners = plane(34)
    for field, y_row in ((head, 32), (old, 33)):
        sides = plane(y_row)
        for x in range(8):
            field[5 + x, 8:16, :] = sides[16 * x : 16 * x + 8]
            field[5 + x, 144:152, :] = sides[16 * x + 8 : 16 * x + 16]
        for x in range(8):
            xi = 13 + x if x < 4 else x - 3
            beside = (corners[16 * x : 16 * x + 8], corners[16 * x + 8 : 16 * x + 16])
            if field is old:
                beside = [pltpu.roll(tile, 4, 0) for tile in beside]
            field[xi, 8:16, :], field[xi, 144:152, :] = beside
    for xi in (0, 17):
        head[xi, 8:16, :] = jnp.full((8, 128), -1.0, jnp.float32)
        head[xi, 144:152, :] = jnp.full((8, 128), -1.0, jnp.float32)

    def curves(xi):
        for c in range(CHUNKS):
            at = slice(CHUNK * c, CHUNK * (c + 1))
            to = slice(8 + CHUNK * c, 8 + CHUNK * (c + 1))
            sat_v, rel_v, dsat_v, drel_v = retention(
                head[xi, to, :], alpha[xi, at, :], expo[xi, at, :], exponent[xi, at, :]
            )
            k0[xi, to, :] = sat_v
            rel[xi, to, :] = rel_v
            d_rel[xi, to, :] = drel_v
            own_c[xi, to, :] = cap[xi, at, :] * dsat_v

    for copy in copies[:4]:
        copy.wait()
    loop(EX, curves, 3)
    for copy in copies[4:]:
        copy.wait()

    def side_faces(xi):
        pair = x_inside(xi) * half_mean(side_x[xi], side_x[jnp.minimum(xi + 1, EX - 1)])
        trans_x[xi, 0:8, :] = pair[0:8]
        trans_x[xi, 136:144, :] = pair[8:16]
        for first, last in ((8, 16), (136, 152)):
            here = slice(first, last)
            value = half_mean(side_y[xi, here, :], side_y[xi, first + 1 : last + 1, :])
            trans_y[xi, here, :] = jnp.where(y_inside(value.shape, first - 8), value, 0.0)

    loop(EX, side_faces, 3)

    def face(half, low, high, rise):
        (h_a, r_a, d_a), (h_b, r_b, d_b) = low, high
        potential = h_b - h_a
        if rise:
            potential = potential + rise
        along = half * (r_a + r_b)
        slope = half * potential
        return along + slope * d_b, along - slope * d_a, along * potential, slope * (d_a + d_b)

    def coefficients(i):
        xi = i + 1
        for c in range(CHUNKS):
            at = slice(CHUNK * c, CHUNK * (c + 1))
            to = slice(8 + CHUNK * c, 8 + CHUNK * (c + 1))
            up = slice(9 + CHUNK * c, 9 + CHUNK * (c + 1))
            down = slice(7 + CHUNK * c, 7 + CHUNK * (c + 1))
            _, log_old = wetness(old[xi, to, :], alpha[xi, at, :], expo[xi, at, :], exponent[xi, at, :])
            old_sat = jnp.exp(exponent[xi, at, :] * log_old)
            start = cap[xi, at, :] * (old_sat - k0[xi, to, :])
            centre = own_c[xi, to, :]
            here = [f[xi, to, :] for f in (head, rel, d_rel)]
            above_x = [f[xi + 1, to, :] for f in (head, rel, d_rel)]
            below_x = [f[xi - 1, to, :] for f in (head, rel, d_rel)]
            above_y = [f[xi, up, :] for f in (head, rel, d_rel)]
            below_y = [f[xi, down, :] for f in (head, rel, d_rel)]
            half_z = trans_z[xi, at, :]
            above_z = [pltpu.roll(f, 127, 1) for f in here]
            below_z = [pltpu.roll(f, 1, 1) for f in here]
            for c_up, c_down, half_up, half_down, above, below, rise in (
                (cxp, cxm, trans_x[xi, at, :], trans_x[xi - 1, at, :], above_x, below_x, 0.0),
                (cyp, cym, trans_y[xi, to, :], trans_y[xi, down, :], above_y, below_y, 0.0),
                (czp, czm, half_z, pltpu.roll(half_z, 1, 1), above_z, below_z, 1.0),
            ):
                c_p, _, flux, both = face(half_up, here, above, rise)
                _, c_m, flux_m, both_m = face(half_down, below, here, rise)
                c_up[xi, to, :] = c_p
                c_down[xi, to, :] = c_m
                start = start + (flux - flux_m)
                centre = centre - (both - both_m)
            own_c[xi, to, :] = centre
            k0[xi, to, :] = start

    loop(16, coefficients, 4)

    vectors = (k0, k1, k2, k3, k4)
    for step in range(4):
        v_ref, w_ref = vectors[step], vectors[step + 1]

        def apply(i):
            xi = i + 2 + step
            for c in range(CHUNKS):
                to = slice(8 + CHUNK * c, 8 + CHUNK * (c + 1))
                up = slice(9 + CHUNK * c, 9 + CHUNK * (c + 1))
                down = slice(7 + CHUNK * c, 7 + CHUNK * (c + 1))
                v = v_ref[xi, to, :]
                w = own_c[xi, to, :] * v
                w = w + cxp[xi, to, :] * (v - v_ref[xi + 1, to, :])
                w = w + cxm[xi, to, :] * (v - v_ref[xi - 1, to, :])
                w = w + cyp[xi, to, :] * (v - v_ref[xi, up, :])
                w = w + cym[xi, to, :] * (v - v_ref[xi, down, :])
                w = w + czp[xi, to, :] * (v - pltpu.roll(v, 127, 1))
                w = w + czm[xi, to, :] * (v - pltpu.roll(v, 1, 1))
                w_ref[xi, to, :] = w

        loop(14 - 2 * step, apply, 7 - step)

    keeps = [
        pltpu.make_async_copy(vectors[k].at[5:13, 16:144, :], kept.at[k], sems.at[7 + k]) for k in range(4)
    ]
    for copy in keeps:
        copy.start()

    def largest(i, tops):
        xi = 5 + i
        for c in range(16):
            at = slice(16 + 8 * c, 24 + 8 * c)
            tops = [jnp.maximum(top, jnp.abs(v[xi, at, :])) for top, v in zip(tops, vectors)]
        return tops

    tops = lax.fori_loop(0, 8, largest, [jnp.zeros((8, 128), jnp.float32) for _ in range(5)])
    scales, inverses = [], []
    for top in tops:
        top = jnp.broadcast_to(jnp.max(top, keepdims=True), (8, 128))
        scale = jnp.full((8, 128), 2.0**96, jnp.float32)
        inverse = jnp.full((8, 128), 2.0**-96, jnp.float32)
        for j in range(-5, 7):
            over = top >= 2.0 ** (16 * j - 8)
            scale = jnp.where(over, 2.0 ** (-16 * j), scale)
            inverse = jnp.where(over, 2.0 ** (16 * j), inverse)
        scales.append(scale)
        inverses.append(inverse)

    def products(i, totals):
        leading, rest = totals
        xi = 5 + i // 4
        first = 16 + 32 * (i % 4)
        for k in range(4):
            at = pl.ds(pl.multiple_of(first + 8 * k, 8), 8)
            values = [v[xi, at, :] * scale for v, scale in zip(vectors, scales)]
            halves = [split(value, 65537.0) for value in values]
            leading, rest = list(leading), list(rest)
            for e, (p, q) in enumerate(PAIRS):
                leading[e], lost = two_sum(leading[e], halves[p][0] * halves[q][0])
                rest[e] = rest[e] + ((halves[p][0] * halves[q][1] + halves[p][1] * values[q]) + lost)
        return leading, rest

    zeros = [jnp.zeros((8, 128), jnp.float32) for _ in PAIRS]
    leading, rest = lax.fori_loop(0, 32, products, (zeros, list(zeros)))
    groups = []
    for g in range(2):
        high = jnp.zeros((8, 128), jnp.float32)
        low = jnp.zeros((8, 128), jnp.float32)
        for e in range(8 * g, min(8 * g + 8, len(PAIRS))):
            pair = two_sum(leading[e], rest[e])
            for shift in (4, 2, 1):
                pair = df_add(pair, (pltpu.roll(pair[0], shift, 0), pltpu.roll(pair[1], shift, 0)))
            high = jnp.where(sub == e - 8 * g, pair[0], high)
            low = jnp.where(sub == e - 8 * g, pair[1], low)
        pair = (high, low)
        for shift in (64, 32, 16, 8, 4, 2, 1):
            pair = df_add(pair, (pltpu.roll(pair[0], shift, 1), pltpu.roll(pair[1], shift, 1)))
        groups.append(pair)
    line = jnp.zeros((8, 128), jnp.float32)
    for e in range(len(PAIRS)):
        pair = groups[e // 8]
        for half in range(2):
            line = jnp.where(lane == 16 * half + e, pair[half][e % 8 : e % 8 + 1, :], line)
    for k in range(5):
        line = jnp.where(lane == 32 + k, inverses[k], line)
        line = jnp.where(lane == 40 + k, scales[k], line)
    for t in range(16):
        sums[8 * t : 8 * t + 8, :] = line

    for copy in keeps:
        copy.wait()


def turn_back_kernel(kept, out):
    for k in range(4):
        for x in range(8):
            out[k, pl.ds(x, 128, stride=8), :] = kept[k, x].T


def finish_kernel(recv, vectors, out):
    data = recv[...]
    lane = iota((128, 128), 1)
    smallest = jnp.min(data, axis=0, keepdims=True)
    factor = data * jnp.broadcast_to(pltpu.roll(jnp.broadcast_to(smallest, (8, 128)), 120, 1)[0:1], (128, 128))
    left = jnp.zeros((128, 128), jnp.float32)
    right = jnp.zeros((128, 128), jnp.float32)
    for k in range(5):
        column = jnp.broadcast_to(factor[:, 32 + k : 33 + k], (128, 128))
        for e, (p, q) in enumerate(PAIRS):
            if p == k:
                left = jnp.where(lane % 16 == e, column, left)
            if q == k:
                right = jnp.where(lane % 16 == e, column, right)
    scaled = data * left * right
    low = pltpu.roll(scaled, 112, 1)
    pair = (scaled[0:8], low[0:8])
    for t in range(1, 16):
        pair = df_add(pair, (scaled[8 * t : 8 * t + 8], low[8 * t : 8 * t + 8]))
    for shift in (4, 2, 1):
        pair = df_add(pair, (pltpu.roll(pair[0], shift, 0), pltpu.roll(pair[1], shift, 0)))
    entry = {}
    for e, (p, q) in enumerate(PAIRS):
        entry[p, q] = tuple(jnp.broadcast_to(half[:, e : e + 1], (8, 128)) for half in pair)

    def scale_of(k):
        return jnp.broadcast_to(smallest[:, k : k + 1], (8, 128))

    rows = {(i, j): entry[i + 1, j + 1] for i in range(4) for j in range(i, 4)}
    right_side = [entry[0, j + 1] for j in range(4)]
    for k in range(4):
        for i in range(k + 1, 4):
            ratio = df_neg(df_div(rows[k, i], rows[k, k]))
            for j in range(i, 4):
                rows[i, j] = df_add(rows[i, j], df_mul(ratio, rows[k, j]))
            right_side[i] = df_add(right_side[i], df_mul(ratio, right_side[k]))
    coeffs = [None] * 4
    for k in reversed(range(4)):
        running = right_side[k]
        for j in range(k + 1, 4):
            running = df_add(running, df_neg(df_mul(rows[k, j], coeffs[j])))
        coeffs[k] = df_div(running, rows[k, k])
    inverse_first = jnp.max(jnp.where(lane == 32, data, 0.0), axis=0, keepdims=True)
    inverse_first = jnp.broadcast_to(jnp.max(inverse_first, axis=1, keepdims=True), (8, 128))
    weights = [(coeffs[k][0] * scale_of(41 + k)) * inverse_first for k in range(4)]

    def rows_of(t):
        for k in range(16):
            at = pl.ds(pl.multiple_of(128 * t + 8 * k, 8), 8)
            total = weights[0] * vectors[0, at, :]
            for j in range(1, 4):
                total = total + weights[j] * vectors[j, at, :]
            out[at, :] = total

    loop(8, rows_of)


def call(kernel, out_shape, in_specs, out_specs, scratch, mib, cost):
    return pl.pallas_call(
        kernel,
        out_shape=out_shape,
        in_specs=in_specs,
        out_specs=out_specs,
        scratch_shapes=scratch,
        compiler_params=params(mib),
        cost_estimate=pl.CostEstimate(flops=cost[0], bytes_accessed=cost[1], transcendentals=0),
    )


def body(held_head, held_head_old, material_ids, block_map, conductivity, vg_alpha, vg_n, capacity):
    count_x, count_y = lax.axis_size("gx"), lax.axis_size("gy")
    devices = count_x * count_y
    own_index = lax.axis_index(AXES)
    numbers = jnp.arange(devices, dtype=jnp.int32)
    scratch = lambda *shape: pltpu.VMEM(shape, jnp.float32)

    beside = [(i, i ^ 1) for i in range(count_x)]
    across = [pair for i in range(1, count_x - 1, 2) for pair in ((i, i + 1), (i + 1, i))]
    up_y = [(i, i + 1) for i in range(count_y - 1)]
    down_y = [(i + 1, i) for i in range(count_y - 1)]
    slot_of, inner, outer = call(
        turn_ids_kernel,
        [jax.ShapeDtypeStruct((8, 128), jnp.int32)] + [f32(DEPTH, 128, 128)] * 2,
        [VMEM, VMEM],
        [VMEM] * 3,
        [scratch(8, 128, 128)],
        63,
        (10**6, 10**6),
    )(block_map, material_ids.reshape(1024, 128))
    outer_in = lax.ppermute(outer, "gx", across)
    inner_in = lax.ppermute(inner, "gx", beside)

    packed = call(
        pack_kernel,
        f32(devices * PIECE, 128),
        [SMEM, VMEM, VMEM],
        HBM,
        [scratch(devices * PIECE + 8, 128), scratch(PY, 128), pltpu.SemaphoreType.DMA],
        63.75,
        (10**6, 4 * 10**6),
    )(slot_of, held_head, held_head_old)
    packed, inner_in, outer_in = lax.optimization_barrier((packed, inner_in, outer_in))
    arrived = lax.all_to_all(
        packed.reshape(devices, PIECE, 1, 128), AXES, split_axis=0, concat_axis=0, tiled=True
    ).reshape(devices * PIECE, 128)

    offsets = (0, -count_y, count_y, -1, 1, count_y - 1, -count_y - 1, count_y + 1, -count_y + 1)
    bricks = own_index + jnp.array(offsets, jnp.int32)
    source = jnp.sum(
        jnp.where(block_map[None] == bricks[:, None, None], numbers[None, :, None], 0), axis=1
    )
    first, last = call(
        edge_ids_kernel, [f32(EX, 8, 128)] * 2, [VMEM] * 4, [VMEM] * 2, [], 8, (10**5, 10**6)
    )(inner, outer, inner_in, outer_in)
    y_low = lax.ppermute(last, "gy", up_y)
    y_high = lax.ppermute(first, "gy", down_y)
    *fields, edges = call(
        properties_kernel,
        [f32(EX, 128, 128)] * 7 + [f32(EX, 2, 8, 128)],
        [SMEM] * 4 + [VMEM] * 4,
        [HBM] * 8,
        [scratch(EX, 128, 128)] * 7 + [scratch(EX, 2, 8, 128), scratch(EX, 128, 128), scratch(EX, 136, 128)]
        + [pltpu.SemaphoreType.DMA((8,))],
        63,
        (40 * 10**6, 12 * 10**6),
    )(conductivity, vg_alpha, vg_n, capacity, inner, outer, inner_in, outer_in)

    kept, sums = call(
        main_kernel,
        [f32(4, 8, 128, 128), f32(devices, 128)],
        [SMEM] * 5 + [HBM] + [VMEM] * 3 + [HBM] * 7,
        [HBM, VMEM],
        [scratch(devices * PIECE + 8, 128)] + [scratch(EX, EY, 128)] * 5 + [scratch(EX, PY, 128), scratch(EX, EY, 128)]
        + [pltpu.SemaphoreType.DMA((12,)), scratch(128 * LAYER, 128)] + [scratch(EX, PY, 128)] * 16
        + [scratch(EX, 16, 128), scratch(EX, PY, 128)],
        63,
        (200 * 10**6, 16 * 10**6),
    )(source, conductivity, vg_alpha, vg_n, capacity, arrived, y_low, y_high, edges, *fields)
    gathered = lax.all_to_all(sums.reshape(devices, 1, 128), AXES, split_axis=0, concat_axis=0, tiled=True)
    turned = call(turn_back_kernel, f32(4, 1024, 128), [VMEM], VMEM, [], 8, (10**6, 4 * 10**6))(kept)
    update = call(finish_kernel, f32(1024, 128), [VMEM] * 2, VMEM, [], 8, (10**6, 3 * 10**6))(
        gathered.reshape(devices, 128), turned
    )
    return update.reshape(128, 8, 128)


def solution(mesh):
    return jax.shard_map(
        body,
        mesh=mesh,
        in_specs=(
            P(("gx", "gy"), None, None),
            P(("gx", "gy"), None, None),
            P(None, "gx", "gy"),
            P(),
            P(),
            P(),
            P(),
            P(),
        ),
        out_specs=P(None, "gx", "gy"),
        check_vma=False,
    )
```
